32 devices in a mesh: grp: 2 (over y), gen: 4 (over z), row: 2 (over x), ch: 2 (over core).
Axes of the slice: x: 2, y: 2, z: 4, core: 2. Of those that a mesh axis runs over, the one named last changes fastest.
Arguments:
- x_center: bfloat16 [24, 24, 112], P(('grp', 'row')), parts along dimension 0, may hold values from -6 to 6
- x_gens: bfloat16 [256, 12, 24, 112], P(('grp', 'gen'), 'row'), parts along dimension 0, may hold values from -0.125 to 0.125
- w_expand: bfloat16 [112, 672], P(None, 'ch'), may hold values from -0.5 to 0.5
- b_expand: float32 [672], P('ch'), may hold values from -3 to 3
- w_depth: float32 [5, 5, 672], P(None, None, 'ch'), may hold values from -1.25 to 1.25
- b_depth: float32 [672], P('ch'), may hold values from -3 to 3
- w_reduce: float32 [672, 28], replicated, may hold values from -0.25 to 0.25
- b_reduce: float32 [28], replicated, may hold values from -6 to 6
- w_excite: float32 [28, 672], P(None, 'ch'), may hold values from -1 to 1
- b_excite: float32 [672], P('ch'), may hold values from -3 to 3
Outputs:
- out_center: float32 [24, 24, 672], P(('grp', 'row'), None, 'ch'), parts along dimension 0
- out_gens: bfloat16 [256, 12, 24, 672], P(('grp', 'gen'), 'row', None, 'ch'), parts along dimension 0
- out_box: float32 [24, 24, 672], P(('grp', 'row'), None, 'ch'), parts along dimension 0
The draws below stay inside these ranges and needn't reach their ends.
There are 2 independent parts, one for each index of `grp`. The reference program is written for one: setup_inputs(seed, part) draws one part's arguments, and reference() takes and returns one part's arrays. A program takes and returns all parts, laid end to end along the dimension named above; an argument that names none is the same for every part. Nothing has to cross between parts.
All inputs are finite; a program needn't handle non-finite values.
Results may differ from the reference program's by a relative error of at most 0.007.
Values may be sent and summed in bfloat16 or wider, within the bound.
A program may use at most 64 MiB of HBM per device.

```python
import jax
import jax.numpy as jnp
from jax import lax

C_IN = 112
C_EXP = 672
C_SE = 28
KSIZE = 5
IMG_W = 24
GEN_DEV = 32
IMG_H = 12
GENS = 128
N_GEN = 4


def draw_x_gens(key, part):
    first_key, second_key = jax.random.split(jax.random.fold_in(key, 11), 2)
    common = jax.random.normal(first_key, (GENS, 1, 1, C_IN))
    rough = jax.random.normal(second_key, (GENS, IMG_H, IMG_W, C_IN))
    factor = 0.01 * jnp.ones((GENS, 1, 1, 1), jnp.float32)
    values = jnp.clip(factor * (common + rough), -0.125, 0.125)
    return values.astype(jnp.bfloat16)


def level_of(key, extent, shards, least, high):
    def one(dim, shards_of):
        draws = jax.random.uniform(jax.random.fold_in(jax.random.fold_in(key, 6), dim), (shards_of,), jnp.float32, least / len(shards), high / len(shards))
        return jnp.repeat(jnp.exp(draws), extent[dim] // shards_of).reshape((-1,) + (1,) * (len(extent) - dim - 1))

    gain = one(*shards[0])
    for cut in shards[1:]:
        gain = gain * one(*cut)
    return gain


def bell_draw(stream_key, shape, spread, most, shards=(), kind=jnp.bfloat16):
    entries = jax.random.normal(stream_key, shape, jnp.float32) * spread
    if len(shards) > 0:
        entries = level_of(stream_key, shape, shards, -0.22, 0.18) * entries
    return jnp.clip(entries, min=-most, max=most).astype(kind)


def setup_inputs(seed: int = 0, part: int = 0) -> dict:
    splits = jax.random.split(jax.random.key(seed), 11)
    own_keys = jax.random.split(jax.random.fold_in(splits[10], part), 11)
    return {
        "x_center": bell_draw(own_keys[0], (IMG_H, IMG_W, C_IN), 1.0, 6.0, ((0, 2),)),
        "x_gens": draw_x_gens(jax.random.fold_in(jax.random.fold_in(splits[10], part), 71), part),
        "w_expand": bell_draw(splits[2], (C_IN, C_EXP), C_IN ** -0.5, 0.5, ((1, 2),)),
        "b_expand": bell_draw(splits[3], (C_EXP,), 0.5, 3.0, ((0, 2),), jnp.float32),
        "w_depth": bell_draw(splits[4], (KSIZE, KSIZE, C_EXP), (KSIZE * KSIZE) ** -0.5, 1.25, ((2, 2),), jnp.float32),
        "b_depth": bell_draw(splits[5], (C_EXP,), 0.5, 3.0, ((0, 2),), jnp.float32),
        "w_reduce": bell_draw(splits[6], (C_EXP, C_SE), C_EXP ** -0.5, 0.25, (), jnp.float32),
        "b_reduce": bell_draw(splits[7], (C_SE,), 1.0, 6.0, (), jnp.float32),
        "w_excite": bell_draw(splits[8], (C_SE, C_EXP), C_SE ** -0.5, 1.0, ((1, 2),), jnp.float32),
        "b_excite": bell_draw(splits[9], (C_EXP,), 0.5, 3.0, ((0, 2),), jnp.float32),
    }


def depthwise(padded, w_depth, row_count, col_count):
    accum_sum = jnp.zeros(padded.shape[:-3] + (row_count, col_count, padded.shape[-1]), jnp.float32)
    for tap_row in range(w_depth.shape[0]):
        for tap_col in range(w_depth.shape[1]):
            window = padded[..., tap_row:tap_row + row_count, tap_col:tap_col + col_count, :]
            accum_sum = accum_sum + window.astype(jnp.float32) * w_depth[tap_row, tap_col]
    return accum_sum


def relax_gate(ex_center, gate_radius):
    low_end = ex_center - gate_radius
    high_end = ex_center + gate_radius
    sig_low = jax.nn.sigmoid(low_end)
    sig_high = jax.nn.sigmoid(high_end)
    slope_val = jnp.minimum(sig_low * (1.0 - sig_low), sig_high * (1.0 - sig_high))
    gate_center = slope_val * ex_center + 0.5 * (sig_high + sig_low - slope_val * (high_end + low_end))
    spread_term = 0.5 * (sig_high - sig_low - slope_val * (high_end - low_end))
    return gate_center, slope_val, spread_term


def reference(x_center, x_gens, w_expand, b_expand, w_depth, b_depth, w_reduce, b_reduce, w_excite, b_excite):
    precise = lax.Precision.HIGHEST
    margin = KSIZE // 2
    padding = [(margin, margin), (margin, margin), (0, 0)]
    exp_center = (jnp.dot(x_center, w_expand, preferred_element_type=jnp.float32) + b_expand).astype(jnp.bfloat16)
    dw_center = depthwise(jnp.pad(exp_center, padding), w_depth, IMG_H, IMG_W) + b_depth
    gen_blocks = x_gens.reshape(N_GEN, GEN_DEV, IMG_H, IMG_W, C_IN)

    def features(gen_block):
        exp_gens = jnp.dot(gen_block, w_expand, preferred_element_type=jnp.float32).astype(jnp.bfloat16)
        return depthwise(jnp.pad(exp_gens, [(0, 0)] + padding), w_depth, IMG_H, IMG_W).astype(jnp.bfloat16)

    def first_pass(running, gen_block):
        dw_gens = features(gen_block).astype(jnp.float32)
        return running + jnp.sum(jnp.abs(dw_gens), axis=0), jnp.sum(dw_gens, axis=(1, 2)) / (IMG_H * IMG_W)

    feat_radius, pool_gens = lax.scan(first_pass, jnp.zeros((IMG_H, IMG_W, C_EXP), jnp.float32), gen_blocks)
    pool_gens = pool_gens.reshape(GENS, C_EXP)
    pool_center = jnp.sum(dw_center, axis=(0, 1)) / (IMG_H * IMG_W)
    sq_center = jnp.dot(pool_center, w_reduce, precision=precise) + b_reduce
    sq_gens = jnp.dot(pool_gens, w_reduce, precision=precise)
    ex_center = jnp.dot(sq_center, w_excite, precision=precise) + b_excite
    ex_gens = jnp.dot(sq_gens, w_excite, precision=precise)
    gate_radius = jnp.sum(jnp.abs(ex_gens), axis=0)
    gate_center, slope_val, spread_term = relax_gate(ex_center, gate_radius)
    gate_gens = slope_val * ex_gens
    gate_total = slope_val * gate_radius + spread_term
    out_center = dw_center * gate_center

    def second_pass(inputs):
        gen_block, gate_block = inputs
        dw_gens = features(gen_block).astype(jnp.float32)
        return (dw_center[None] * gate_block[:, None, None, :] + gate_center * dw_gens).astype(jnp.bfloat16)

    out_gens = lax.map(second_pass, (gen_blocks, gate_gens.reshape(N_GEN, GEN_DEV, C_EXP)))
    out_gens = out_gens.reshape(GENS, IMG_H, IMG_W, C_EXP)
    out_box = jnp.abs(dw_center) * spread_term + feat_radius * gate_total
    return out_center, out_gens, out_box
```

```python
import functools

import jax
import jax.numpy as jnp
import ml_dtypes
import numpy as np
from jax import lax
from jax.experimental import pallas as pl
from jax.experimental.pallas import tpu as pltpu
from jax.sharding import PartitionSpec as P

MESH = pl.DeviceIdType.MESH
LANES = 128
PAIRS = 4


def dot(a, b):
    return jnp.dot(a, b, preferred_element_type=jnp.float32)


def split(values):
    high = values.astype(ml_dtypes.bfloat16)
    return high, (values - high.astype(np.float64)).astype(ml_dtypes.bfloat16)


def transforms(rows, cols, taps):
    m = taps // 2
    n_r, n_c = rows + 2 * m, cols + m
    count = n_r * n_c
    r_in, c_in = np.arange(n_r)[:, None], np.arange(cols)[None, :]
    r_out = np.arange(rows)[:, None]
    tap_r, tap_c = np.arange(taps)[:, None], np.arange(taps)[None, :] - m

    def angle(freq, r, c):
        return (2 * np.pi * (freq[0] * r / n_r + freq[1] * c / n_c)).ravel()

    seen, double, single = set(), [], []
    for freq in [(u, v) for u in range(n_r) for v in range(n_c)]:
        twin = (-freq[0] % n_r, -freq[1] % n_c)
        if freq not in seen:
            (single if twin == freq else double).append(freq)
        seen |= {freq, twin}
    blocks = [[], [], [], [], [], [], [], []]
    for freq in double:
        a, t, o = angle(freq, r_in, c_in), angle(freq, tap_r, tap_c), angle(freq, r_out, c_in)
        entry = (
            np.cos(a), -np.sin(a), np.cos(t), np.sin(t), np.sin(t), np.cos(t),
            2 * np.cos(o) / count, -2 * np.sin(o) / count,
        )
        for block, part in zip(blocks, entry):
            block.append(part)
    single += [None] * (len(single) % 2)
    for one, two in zip(single[::2], single[1::2]):
        def wave(freq, r, c):
            scale = 0.0 if freq is None else 1.0
            return scale * np.cos(angle(freq or (0, 0), r, c))

        entry = (
            wave(one, r_in, c_in), wave(two, r_in, c_in),
            wave(one, tap_r, tap_c), 0 * wave(one, tap_r, tap_c),
            0 * wave(one, tap_r, tap_c), wave(two, tap_r, tap_c),
            wave(one, r_out, c_in) / count, wave(two, r_out, c_in) / count,
        )
        for block, part in zip(blocks, entry):
            block.append(part)
    half = -(-len(blocks[0]) // 8) * 8
    blocks = [np.pad(np.array(b), ((0, half - len(b)), (0, 0))) for b in blocks]
    forward = np.concatenate(blocks[:2], axis=0)
    inverse = np.concatenate([blocks[6].T, blocks[7].T], axis=1)
    sum_high, sum_low = split(inverse.sum(axis=0))
    cells = inverse.shape[0]
    full = np.zeros((-(-(cells + 2) // 16) * 16, inverse.shape[1]), ml_dtypes.bfloat16)
    full[:cells] = inverse.astype(ml_dtypes.bfloat16)
    full[cells], full[cells + 1] = sum_high, sum_low
    waves = np.concatenate(blocks[2:6], axis=0)
    high, low = split(waves)
    step = -(-taps * taps // 8) * 8
    tap_waves = np.zeros((4 * half, 4 * step), ml_dtypes.bfloat16)
    for slot, part in enumerate((high, high, low)):
        tap_waves[:, slot * step : slot * step + taps * taps] = part
    return forward.astype(ml_dtypes.bfloat16), full, tap_waves, half, step


def relax_gate(ex_center, gate_radius):
    low_end = ex_center - gate_radius
    high_end = ex_center + gate_radius
    sig_low = jax.nn.sigmoid(low_end)
    sig_high = jax.nn.sigmoid(high_end)
    slope_val = jnp.minimum(sig_low * (1.0 - sig_low), sig_high * (1.0 - sig_high))
    gate_center = slope_val * ex_center + 0.5 * (
        sig_high + sig_low - slope_val * (high_end + low_end)
    )
    spread_term = 0.5 * (sig_high - sig_low - slope_val * (high_end - low_end))
    return (gate_center, slope_val, spread_term)


def main_kernel(
    mesh, half, step, chans, margin_span, chunk,
    x_ref, xc_ref, fwd_ref, inv_ref, tw_ref, w_ref, b_ref, wd_ref, bd_ref, wr_ref, br_ref, we_ref, be_ref,
    dwg_ref, dwc_ref, gates_ref, stats_ref, feat_ref,
    hs, cs, xcs, wf, wz, w2, wtap, spec, xf_s, y1_s, y2_s, rad, pool, own_wr,
    send_rad, recv_rad, full_rad, squeeze, gate,
    h_send, h_recv, f_send, f_recv, c_send, c_recv,
    rs_send, rs_recv, ag_send, ag_recv, sq_send, sq_recv, gt_send, gt_recv,
):
    count_gen, count_row, count_ch = mesh["gen"], mesh["row"], mesh["ch"]
    my_gen = lax.axis_index("gen")
    my_row = lax.axis_index("row")
    my_ch = lax.axis_index("ch")
    has_up = my_row > 0
    has_down = my_row < count_row - 1
    sides = ((0, has_up, has_down), (1, has_down, has_up))
    gens, pairs, span, lanes = x_ref.shape
    cells = dwc_ref.shape[0]
    all_cells = cells * count_row
    c_in = w_ref.shape[0]
    taps = wd_ref.shape[0]
    wide = wz.shape[1]
    main = w2.shape[0]
    per = recv_rad.shape[1]
    sub = chunk // count_ch

    def remote(src, dst, send_sem, recv_sem, place):
        return pltpu.make_async_remote_copy(
            src_ref=src, dst_ref=dst, send_sem=send_sem, recv_sem=recv_sem,
            device_id=place, device_id_type=MESH,
        )

    gen_peers = [(off, {"gen": lax.rem(my_gen + off, count_gen)}) for off in range(1, count_gen)]
    side_peers = []
    for off_row in range(count_row):
        for off_ch in range(count_ch):
            if off_row or off_ch:
                place = {
                    "row": lax.rem(my_row + off_row, count_row),
                    "ch": lax.rem(my_ch + off_ch, count_ch),
                }
                side_peers.append((off_row * count_ch + off_ch, place))
    barrier = pltpu.get_barrier_semaphore()
    for _, place in gen_peers + side_peers:
        pl.semaphore_signal(barrier, inc=1, device_id=place, device_id_type=MESH)

    row_place = (
        {"row": lax.rem(my_row + 1, count_row)},
        {"row": lax.rem(my_row + count_row - 1, count_row)},
    )
    edge = (pairs - 1, 0)

    def halo_copy(side, n):
        where = pl.ds(n * chunk + my_ch * sub, sub)
        return remote(
            x_ref.at[where, edge[side]], hs.at[side, where],
            h_send.at[side, n], h_recv.at[side, n], row_place[side],
        )

    def center_copy(side):
        return remote(
            xc_ref.at[edge[side]], cs.at[side], c_send.at[side], c_recv.at[side], row_place[side]
        )

    def forwards(side, n):
        where = pl.ds(n * chunk + my_ch * sub, sub)
        return [
            remote(
                hs.at[side, where], hs.at[side, where],
                f_send.at[side, n, off], f_recv.at[side, n, off],
                {"ch": lax.rem(my_ch + off, count_ch)},
            )
            for off in range(1, count_ch)
        ]

    chunks = gens // chunk

    wf[...] = jnp.zeros_like(wf)
    wf[:c_in, :chans] = w_ref[...].astype(jnp.float32)
    bias = b_ref[...][None, :]
    bias_high = bias.astype(jnp.bfloat16).astype(jnp.float32)
    wf[c_in : c_in + 1, :chans] = bias_high
    wf[c_in + 1 : c_in + 2, :chans] = bias - bias_high
    wz[...] = wf[...].astype(jnp.bfloat16)
    w2[...] = jnp.zeros_like(w2)
    w2[:LANES, :LANES] = wz[:, main:]
    w2[LANES:, LANES:] = wz[:, main:]
    wtap[...] = jnp.zeros_like(wtap)
    for row in range(taps):
        one = wd_ref[row]
        high = one.astype(jnp.bfloat16).astype(jnp.float32)
        for slot, part in enumerate((high, one - high, high)):
            start = slot * step + row * taps
            wtap[start : start + taps, :chans] = part
    spec[...] = dot(tw_ref[...], wtap[...].astype(jnp.bfloat16)).reshape(spec.shape)
    own = wr_ref[:, :chans]
    for other in range(1, count_ch):
        own = jnp.where(my_ch == other, wr_ref[:, other * chans : (other + 1) * chans], own)
    own_wr[...] = jnp.zeros_like(own_wr)
    own_wr[:, :chans] = own
    xcs[...] = jnp.zeros_like(xcs)
    xcs[1 : 1 + pairs, :, :c_in] = xc_ref[...]
    lane = lax.broadcasted_iota(jnp.int32, (span, lanes - c_in), 1)
    ones = jnp.where(lane < 2, 1.0, 0.0).astype(jnp.bfloat16)
    for row in range(pairs):
        xcs[1 + row, :, c_in:] = ones
    rad[...] = jnp.zeros_like(rad)
    pool[...] = jnp.zeros_like(pool)
    for side, arrives, _ in sides:
        @pl.when(jnp.logical_not(arrives))
        def _(side=side):
            hs[side] = jnp.zeros(hs.shape[1:], hs.dtype)

    pl.semaphore_wait(barrier, len(gen_peers) + len(side_peers))

    for side, _, leaves in sides:
        @pl.when(leaves)
        def _(side=side):
            center_copy(side).start()
            for n in range(chunks):
                halo_copy(side, n).start()

    def pass_on(n):
        for side, arrives, _ in sides:
            @pl.when(arrives)
            def _(side=side):
                halo_copy(side, n).wait_recv()
                for copy in forwards(side, n):
                    copy.start()

    def passed_on(n):
        for side, arrives, _ in sides:
            @pl.when(arrives)
            def _(side=side):
                for copy in forwards(side, n):
                    copy.wait_recv()

    pass_on(0)

    for side, arrives, _ in sides:
        @pl.when(arrives)
        def _(side=side):
            center_copy(side).wait_recv()
            place = (0, pairs + 1)[side]
            xcs[place, :, :c_in] = cs[side]
            xcs[place, :, c_in:] = ones
    xf = dot(fwd_ref[...], xcs[...].reshape((pairs + 2) * span, lanes)).astype(jnp.bfloat16)
    e = dot(xf, wz[...])
    re, im = e[:half], e[half:]
    y = jnp.concatenate(
        [re * spec[0] - im * spec[1], re * spec[2] + im * spec[3]], axis=0
    ).astype(jnp.bfloat16)
    t = dot(inv_ref[...], y)
    dwc_ref[...] = t[:cells, :chans] + bd_ref[...][None, :]
    pool[chunks, 0:1, :chans] = (
        t[cells : cells + 1, :chans] + t[cells + 1 : cells + 2, :chans]
    ) + cells * bd_ref[...][None, :]

    def image(g):
        return jnp.concatenate(
            [hs[0, g], x_ref[g].reshape(pairs * span, lanes), hs[1, g]], axis=0
        )

    def compute(n):
        for u in range(PAIRS):
            g = n * chunk + 2 * u
            both = jnp.concatenate([image(g), image(g + 1)], axis=1)
            xf_s[u] = dot(fwd_ref[...], both).astype(jnp.bfloat16)
        for u in range(PAIRS):
            xf = xf_s[u]
            e2 = dot(xf, w2[...])
            for k in range(2):
                part = slice(LANES * k, LANES * (k + 1))
                e1 = dot(xf[:, part], wz[:, :main])
                re, im = e1[:half], e1[half:]
                y1_s[u, k] = jnp.concatenate(
                    [
                        re * spec[0, :, :main] - im * spec[1, :, :main],
                        re * spec[2, :, :main] + im * spec[3, :, :main],
                    ],
                    axis=0,
                ).astype(jnp.bfloat16)
                re, im = e2[:half, part], e2[half:, part]
                y2_s[u, :, part] = jnp.concatenate(
                    [
                        re * spec[0, :, main:] - im * spec[1, :, main:],
                        re * spec[2, :, main:] + im * spec[3, :, main:],
                    ],
                    axis=0,
                ).astype(jnp.bfloat16)
        for u in range(PAIRS):
            t1 = [dot(inv_ref[...], y1_s[u, k]) for k in range(2)]
            t2 = dot(inv_ref[...], y2_s[u])
            for k in range(2):
                g = n * chunk + 2 * u + k
                mine = t2[:, LANES * k : LANES * (k + 1)]
                dwg_ref[g, :, :main] = t1[k][:cells].astype(jnp.bfloat16)
                dwg_ref[g, :, main:] = mine[:cells, : chans - main].astype(jnp.bfloat16)
                here = slice(2 * u + k, 2 * u + k + 1)
                pool[n, here, :main] = t1[k][cells : cells + 1] + t1[k][cells + 1 : cells + 2]
                pool[n, here, main:] = mine[cells : cells + 1] + mine[cells + 1 : cells + 2]
            rad[:, :main] += jnp.abs(t1[0][:cells]) + jnp.abs(t1[1][:cells])
            rad[:, main:] += jnp.abs(t2[:cells, :LANES]) + jnp.abs(t2[:cells, LANES:])

    def turn(n, _):
        @pl.when(n > 0)
        def _():
            @pl.when(n < chunks - 1)
            def _():
                pass_on(n + 1)

        passed_on(n)
        compute(n)

        @pl.when(n == 0)
        def _():
            if chunks > 1:
                pass_on(1)

        return 0

    lax.fori_loop(0, chunks, turn, 0)

    pooled = pool[...].reshape(gens + chunk, pool.shape[-1]) * (1.0 / all_cells)
    part = lax.dot_general(
        pooled, own_wr[...], (((1,), (1,)), ((), ())),
        precision=lax.Precision.HIGHEST, preferred_element_type=jnp.float32,
    )
    mine = my_row * count_ch + my_ch
    squeeze[mine] = part
    sq_copies = [
        remote(squeeze.at[mine], squeeze.at[mine], sq_send.at[off], sq_recv.at[off], place)
        for off, place in side_peers
    ]
    for copy in sq_copies:
        copy.start()

    tiles = cells // 8
    send_rad[:tiles] = rad[:, :chans].reshape(tiles, 8, chans).astype(jnp.bfloat16)
    if count_gen * per > tiles:
        send_rad[tiles:] = jnp.zeros((count_gen * per - tiles, 8, chans), jnp.bfloat16)
    recv_rad[my_gen] = send_rad[pl.ds(my_gen * per, per)]
    rs_copies = [
        remote(
            send_rad.at[pl.ds(place["gen"] * per, per)], recv_rad.at[my_gen],
            rs_send.at[off], rs_recv.at[off], place,
        )
        for off, place in gen_peers
    ]
    for copy in rs_copies:
        copy.start()
    for copy in sq_copies:
        copy.wait()
    total = squeeze[0]
    for slot in range(1, count_row * count_ch):
        total = total + squeeze[slot]
    row_of = lax.broadcasted_iota(jnp.int32, total.shape, 0)
    total = total + jnp.where(row_of == gens, br_ref[...][None, :], 0.0)
    ex_all = jnp.dot(
        total, we_ref[...], precision=lax.Precision.HIGHEST, preferred_element_type=jnp.float32
    )
    ex_gens = ex_all[:gens]
    ex_center = ex_all[gens : gens + 1] + be_ref[...][None, :]
    gate[my_gen] = jnp.sum(jnp.abs(ex_gens), axis=0, keepdims=True)
    gt_copies = [
        remote(gate.at[my_gen], gate.at[my_gen], gt_send.at[off], gt_recv.at[off], place)
        for off, place in gen_peers
    ]
    for copy in gt_copies:
        copy.start()

    for copy in rs_copies:
        copy.wait()
    total_rad = recv_rad[0].astype(jnp.float32)
    for slot in range(1, count_gen):
        total_rad = total_rad + recv_rad[slot].astype(jnp.float32)
    own_part = pl.ds(my_gen * per, per)
    full_rad[own_part] = total_rad.astype(jnp.bfloat16)
    ag_copies = [
        remote(full_rad.at[own_part], full_rad.at[own_part], ag_send.at[off], ag_recv.at[off], place)
        for off, place in gen_peers
    ]
    for copy in ag_copies:
        copy.start()

    for copy in gt_copies:
        copy.wait()
    gate_radius = gate[0]
    for slot in range(1, count_gen):
        gate_radius = gate_radius + gate[slot]
    gate_center, slope_val, spread_term = relax_gate(ex_center, gate_radius)
    gates_ref[...] = (slope_val * ex_gens)[:, None, :]
    stats_ref[0:1] = gate_center
    stats_ref[1:2] = spread_term
    stats_ref[2:3] = slope_val * gate_radius + spread_term
    for copy in ag_copies:
        copy.wait()
    feat_ref[...] = full_rad[:tiles].astype(jnp.float32).reshape(cells, chans)

    for side, arrives, leaves in sides:
        @pl.when(leaves)
        def _(side=side):
            center_copy(side).wait_send()
            for n in range(chunks):
                halo_copy(side, n).wait_send()

        @pl.when(arrives)
        def _(side=side):
            for n in range(chunks):
                for copy in forwards(side, n):
                    copy.wait_send()


def main_call(mesh, taps, cols, x, xc, w_expand, b_expand, w_depth, b_depth, wr, br, we, be):
    gens, pairs, span, lanes = x.shape
    chans = w_expand.shape[1]
    rows = pairs * span // cols
    cells = rows * cols
    chunk = 2 * PAIRS
    forward, inverse, tap_waves, half, step = transforms(rows, cols, taps)
    count_gen, count_row, count_ch = mesh["gen"], mesh["row"], mesh["ch"]
    wide = -(-chans // LANES) * LANES
    main = wide - LANES
    assert main == 2 * LANES and gens % chunk == 0
    tiles = cells // 8
    per = -(-tiles // count_gen)
    units = we.shape[0]
    side = count_row * count_ch
    chunks = gens // chunk
    vmem = pl.BlockSpec(memory_space=pltpu.VMEM)
    dma = pltpu.SemaphoreType.DMA
    bf16, f32 = jnp.bfloat16, jnp.float32
    args = (
        x, xc, jnp.asarray(forward), jnp.asarray(inverse), jnp.asarray(tap_waves),
        w_expand, b_expand, w_depth, b_depth, wr, br, we, be,
    )
    return pl.pallas_call(
        functools.partial(main_kernel, mesh, half, step, chans, span, chunk),
        in_specs=[vmem] * len(args),
        out_specs=[vmem] * 5,
        out_shape=[
            jax.ShapeDtypeStruct((gens, cells, chans), bf16),
            jax.ShapeDtypeStruct((cells, chans), f32),
            jax.ShapeDtypeStruct((gens, 1, chans), f32),
            jax.ShapeDtypeStruct((3, chans), f32),
            jax.ShapeDtypeStruct((cells, chans), f32),
        ],
        scratch_shapes=[
            pltpu.VMEM((2, gens, span, lanes), bf16),
            pltpu.VMEM((2, span, w_expand.shape[0]), bf16),
            pltpu.VMEM((pairs + 2, span, lanes), bf16),
            pltpu.VMEM((lanes, wide), f32),
            pltpu.VMEM((lanes, wide), bf16),
            pltpu.VMEM((2 * LANES, 2 * LANES), bf16),
            pltpu.VMEM((4 * step, wide), f32),
            pltpu.VMEM((4, half, wide), f32),
            pltpu.VMEM((PAIRS, 2 * half, 2 * LANES), bf16),
            pltpu.VMEM((PAIRS, 2, 2 * half, 2 * LANES), bf16),
            pltpu.VMEM((PAIRS, 2 * half, 2 * LANES), bf16),
            pltpu.VMEM((cells, wide), f32),
            pltpu.VMEM((chunks + 1, chunk, wide), f32),
            pltpu.VMEM((units, wide), f32),
            pltpu.VMEM((count_gen * per, 8, chans), bf16),
            pltpu.VMEM((count_gen, per, 8, chans), bf16),
            pltpu.VMEM((count_gen * per, 8, chans), bf16),
            pltpu.VMEM((side, gens + chunk, units), f32),
            pltpu.VMEM((count_gen, 1, chans), f32),
            dma((2, chunks)), dma((2, chunks)),
            dma((2, chunks, count_ch)), dma((2, chunks, count_ch)),
            dma((2,)), dma((2,)),
            dma((count_gen,)), dma((count_gen,)), dma((count_gen,)), dma((count_gen,)),
            dma((side,)), dma((side,)), dma((count_gen,)), dma((count_gen,)),
        ],
        compiler_params=pltpu.CompilerParams(
            collective_id=1, has_side_effects=True, vmem_limit_bytes=32 << 20
        ),
    )(*args)


def final_kernel(block, dwg_ref, gates_ref, dwc_ref, feat_ref, stats_ref, oc_ref, og_ref, ob_ref):
    center = dwc_ref[...]
    gate_center = stats_ref[0:1]

    @pl.when(pl.program_id(0) == 0)
    def _():
        oc_ref[...] = center * gate_center
        ob_ref[...] = jnp.abs(center) * stats_ref[1:2] + feat_ref[...] * stats_ref[2:3]

    for k in range(block):
        og_ref[k] = (
            center * gates_ref[k] + gate_center * dwg_ref[k].astype(jnp.float32)
        ).astype(jnp.bfloat16)


def final_call(dw_gens, gates, dw_center, feat, stats):
    gens, cells, chans = dw_gens.shape
    block = 8
    whole = pl.BlockSpec((cells, chans), lambda i: (0, 0))
    big = pl.BlockSpec((block, cells, chans), lambda i: (i, 0, 0))
    return pl.pallas_call(
        functools.partial(final_kernel, block),
        grid=(gens // block,),
        in_specs=[
            big,
            pl.BlockSpec((block, 1, chans), lambda i: (i, 0, 0)),
            whole,
            whole,
            pl.BlockSpec((3, chans), lambda i: (0, 0)),
        ],
        out_specs=[whole, big, whole],
        out_shape=[
            jax.ShapeDtypeStruct((cells, chans), jnp.float32),
            jax.ShapeDtypeStruct(dw_gens.shape, jnp.bfloat16),
            jax.ShapeDtypeStruct((cells, chans), jnp.float32),
        ],
        compiler_params=pltpu.CompilerParams(
            dimension_semantics=("arbitrary",), vmem_limit_bytes=12 << 20
        ),
    )(dw_gens, gates, dw_center, feat, stats)


def on_device(
    shape, x_center, x_gens, w_expand, b_expand, w_depth, b_depth, w_reduce, b_reduce, w_excite, b_excite
):
    gens, rows, cols, c_in = x_gens.shape
    chans = w_expand.shape[1]
    taps = w_depth.shape[0]
    margin = taps // 2
    pairs, span = rows // margin, margin * cols
    x = jnp.pad(x_gens, ((0, 0), (0, 0), (0, 0), (0, LANES - c_in))).reshape(gens, pairs, span, LANES)
    xc = x_center.reshape(pairs, span, c_in)
    dw_gens, dw_center, gates, stats, feat = main_call(
        shape, taps, cols, x, xc, w_expand, b_expand, w_depth, b_depth,
        w_reduce.T, b_reduce, w_excite, b_excite,
    )
    out_center, out_gens, out_box = final_call(dw_gens, gates, dw_center, feat, stats)
    image = (rows, cols, chans)
    return out_center.reshape(image), out_gens.reshape((gens,) + image), out_box.reshape(image)


def solution(mesh):
    in_specs = (
        P(("grp", "row"), None, None),
        P(("grp", "gen"), "row", None, None),
        P(None, "ch"),
        P("ch"),
        P(None, None, "ch"),
        P("ch"),
        P(),
        P(),
        P(None, "ch"),
        P("ch"),
    )
    out_specs = (
        P(("grp", "row"), None, "ch"),
        P(("grp", "gen"), "row", None, "ch"),
        P(("grp", "row"), None, "ch"),
    )
    return jax.shard_map(
        functools.partial(on_device, dict(mesh.shape)), mesh=mesh, in_specs=in_specs, out_specs=out_specs, check_vma=False
    )
```

```python
import functools

import jax
import jax.numpy as jnp
import ml_dtypes
import numpy as np
from jax import lax
from jax.experimental import pallas as pl
from jax.experimental.pallas import tpu as pltpu
from jax.sharding import PartitionSpec as P

MESH = pl.DeviceIdType.MESH
LANES = 128
PAIRS = 4
GROUP = 32
ROOM = 32 << 20
OUTS = 5
HELD = 15
HALO = 2


def dot(a, b):
    return jnp.dot(a, b, preferred_element_type=jnp.float32)


def split(values):
    high = values.astype(ml_dtypes.bfloat16)
    return high, (values - high.astype(np.float64)).astype(ml_dtypes.bfloat16)


def transforms(rows, cols, taps):
    m = taps // 2
    n_r, n_c = rows + 2 * m, cols + m
    count = n_r * n_c
    r_in, c_in = np.arange(n_r)[:, None], np.arange(cols)[None, :]
    r_out = np.arange(rows)[:, None]
    tap_r, tap_c = np.arange(taps)[:, None], np.arange(taps)[None, :] - m

    def angle(freq, r, c):
        return (2 * np.pi * (freq[0] * r / n_r + freq[1] * c / n_c)).ravel()

    seen, double, single = set(), [], []
    for freq in [(u, v) for u in range(n_r) for v in range(n_c)]:
        twin = (-freq[0] % n_r, -freq[1] % n_c)
        if freq not in seen:
            (single if twin == freq else double).append(freq)
        seen |= {freq, twin}
    blocks = [[], [], [], [], [], [], [], []]
    for freq in double:
        a, t, o = angle(freq, r_in, c_in), angle(freq, tap_r, tap_c), angle(freq, r_out, c_in)
        entry = (
            np.cos(a), -np.sin(a), np.cos(t), np.sin(t), np.sin(t), np.cos(t),
            2 * np.cos(o) / count, -2 * np.sin(o) / count,
        )
        for block, part in zip(blocks, entry):
            block.append(part)
    single += [None] * (len(single) % 2)
    for one, two in zip(single[::2], single[1::2]):
        def wave(freq, r, c):
            scale = 0.0 if freq is None else 1.0
            return scale * np.cos(angle(freq or (0, 0), r, c))

        entry = (
            wave(one, r_in, c_in), wave(two, r_in, c_in),
            wave(one, tap_r, tap_c), 0 * wave(one, tap_r, tap_c),
            0 * wave(one, tap_r, tap_c), wave(two, tap_r, tap_c),
            wave(one, r_out, c_in) / count, wave(two, r_out, c_in) / count,
        )
        for block, part in zip(blocks, entry):
            block.append(part)
    half = -(-len(blocks[0]) // 8) * 8
    blocks = [np.pad(np.array(b), ((0, half - len(b)), (0, 0))) for b in blocks]
    forward = np.concatenate(blocks[:2], axis=0)
    inverse = np.concatenate([blocks[6].T, blocks[7].T], axis=1)
    sum_high, sum_low = split(inverse.sum(axis=0))
    cells = inverse.shape[0]
    full = np.zeros((-(-(cells + 2) // 16) * 16, inverse.shape[1]), ml_dtypes.bfloat16)
    full[:cells] = inverse.astype(ml_dtypes.bfloat16)
    full[cells], full[cells + 1] = sum_high, sum_low
    waves = np.concatenate(blocks[2:6], axis=0)
    high, low = split(waves)
    step = -(-taps * taps // 8) * 8
    tap_waves = np.zeros((4 * half, 4 * step), ml_dtypes.bfloat16)
    for slot, part in enumerate((high, high, low)):
        tap_waves[:, slot * step : slot * step + taps * taps] = part
    return forward.astype(ml_dtypes.bfloat16), full, tap_waves, half, step


def relax_gate(ex_center, gate_radius):
    low_end = ex_center - gate_radius
    high_end = ex_center + gate_radius
    sig_low = jax.nn.sigmoid(low_end)
    sig_high = jax.nn.sigmoid(high_end)
    slope_val = jnp.minimum(sig_low * (1.0 - sig_low), sig_high * (1.0 - sig_high))
    gate_center = slope_val * ex_center + 0.5 * (
        sig_high + sig_low - slope_val * (high_end + low_end)
    )
    spread_term = 0.5 * (sig_high - sig_low - slope_val * (high_end - low_end))
    return (gate_center, slope_val, spread_term)


def main_kernel(mesh, plans, chunk, x_hbm, *refs):
    main_body(
        mesh, plans, chunk, x_hbm, refs[:HELD], refs[HELD : HELD + OUTS],
        refs[HELD + OUTS : 2 * HELD + OUTS], *refs[2 * HELD + OUTS :],
    )


def main_body(
    mesh, plans, chunk, x_hbm, sources, outs, locals_,
    dwg_ref, dwc_ref, gates_ref, stats_ref, feat_ref, g_sem, o_sem, xs, l_sem, x_sem,
    xcat, xcs, xcp, wf, wz, w2, spec_a, spec_b, xf_s, y1_s, y2_s,
    rad, pool, own_wr, wr_high, wr_low, we_three, br_wide,
    send_a, recv_a, full_a, send_b, recv_b, full_b, squeeze, gate,
    h_send, h_recv, f_send, f_recv, c_send, c_recv,
    rs_send, rs_recv, ag_send, ag_recv, sq_send, sq_recv, gt_send, gt_recv,
):
    (
        xc_ref, fwd_a, inv_a, tw_a, fwd_b, inv_b, tw_b,
        w_ref, b_ref, wd_ref, bd_ref, wr_ref, br_ref, we_ref, be_ref,
    ) = locals_
    count_gen, count_row, count_ch = mesh["gen"], mesh["row"], mesh["ch"]
    my_gen = lax.axis_index("gen")
    my_row = lax.axis_index("row")
    my_ch = lax.axis_index("ch")
    has_up = my_row > 0
    has_down = my_row < count_row - 1
    last = jnp.logical_and(has_up, jnp.logical_not(has_down))
    inner = jnp.logical_and(has_up, has_down)
    flip = jnp.where(last, 1, 0)
    gens, pairs, span, chans = dwg_ref.shape
    c_in = w_ref.shape[0]
    taps = wd_ref.shape[0]
    wide = wz.shape[1]
    main = wide - LANES
    chunks = gens // chunk
    all_cells = pairs * span * count_row
    sub = gens // (HALO * count_ch)

    def remote(src, dst, send_sem, recv_sem, place):
        return pltpu.make_async_remote_copy(
            src_ref=src, dst_ref=dst, send_sem=send_sem, recv_sem=recv_sem,
            device_id=place, device_id_type=MESH,
        )

    gen_peers = [(off, {"gen": lax.rem(my_gen + off, count_gen)}) for off in range(1, count_gen)]
    side_peers = []
    for off_row in range(count_row):
        for off_ch in range(count_ch):
            if off_row or off_ch:
                place = {
                    "row": lax.rem(my_row + off_row, count_row),
                    "ch": lax.rem(my_ch + off_ch, count_ch),
                }
                side_peers.append((off_row * count_ch + off_ch, place))
    barrier = pltpu.get_barrier_semaphore()
    for _, place in gen_peers + side_peers:
        pl.semaphore_signal(barrier, inc=1, device_id=place, device_id_type=MESH)

    loads = [
        pltpu.make_async_copy(source, target, l_sem.at[k])
        for k, (source, target) in enumerate(zip(sources, locals_))
    ]
    for load in loads:
        load.start()
    x_loads = [
        pltpu.make_async_copy(x_hbm.at[:, row], xs.at[1 + row], x_sem.at[row]) for row in range(pairs)
    ]
    for load in x_loads:
        load.start()
    pl.semaphore_wait(barrier, len(gen_peers) + len(side_peers))

    row_place = (
        {"row": lax.rem(my_row + 1, count_row)},
        {"row": lax.rem(my_row + count_row - 1, count_row)},
    )
    edge = (pairs - 1, 0)
    place_of = (0, pairs + 1)

    def halo_copy(side, n):
        where = pl.ds((n * count_ch + my_ch) * sub, sub)
        return remote(
            x_hbm.at[where, edge[side]], xs.at[place_of[side], where],
            h_send.at[side, n], h_recv.at[side, n], row_place[side],
        )

    def center_copy(side):
        return remote(
            sources[0].at[edge[side]], xcs.at[side], c_send.at[side], c_recv.at[side], row_place[side]
        )

    def forwards(side, n):
        where = xs.at[place_of[side], pl.ds((n * count_ch + my_ch) * sub, sub)]
        return [
            remote(
                where, where, f_send.at[side, n, off], f_recv.at[side, n, off],
                {"ch": lax.rem(my_ch + off, count_ch)},
            )
            for off in range(1, count_ch)
        ]

    for side, leaves in ((0, has_down), (1, has_up)):
        @pl.when(leaves)
        def _(side=side):
            center_copy(side).start()
            for n in range(HALO):
                halo_copy(side, n).start()

    def pass_on(side, n):
        halo_copy(side, n).wait_recv()
        for copy in forwards(side, n):
            copy.start()

    def passed_on(side):
        center_copy(side).wait_recv()
        for n in range(HALO):
            for copy in forwards(side, n):
                copy.wait_recv()

    def late(action):
        @pl.when(last)
        def _():
            action(0)

        @pl.when(has_down)
        def _():
            action(1)

    for load in loads:
        load.wait()
    wf[...] = jnp.zeros_like(wf)
    wf[:c_in, :chans] = w_ref[...].astype(jnp.float32)
    bias = b_ref[...][None, :]
    bias_high = bias.astype(jnp.bfloat16).astype(jnp.float32)
    wf[c_in : c_in + 1, :chans] = bias_high
    wf[c_in + 1 : c_in + 2, :chans] = bias - bias_high
    wz[...] = wf[...].astype(jnp.bfloat16)
    w2[...] = jnp.zeros_like(w2)
    w2[:LANES, :LANES] = wz[:, main:]
    w2[LANES:, LANES:] = wz[:, main:]
    wf[...] = jnp.zeros_like(wf)
    step = plans[0][1]
    for row in range(taps):
        one = wd_ref[row]
        high = one.astype(jnp.bfloat16).astype(jnp.float32)
        for slot, part in enumerate((high, one - high, high)):
            start = slot * step + row * taps
            wf[start : start + taps, :chans] = part
    wtap = wf[...].astype(jnp.bfloat16)
    spec_a[...] = dot(tw_a[...], wtap).reshape(spec_a.shape)
    spec_b[...] = dot(tw_b[...], wtap).reshape(spec_b.shape)
    ones = jnp.where(
        lax.broadcasted_iota(jnp.int32, (span, LANES - c_in), 1) < 2, 1.0, 0.0
    ).astype(jnp.bfloat16)
    xcp[...] = jnp.zeros_like(xcp)
    xcp[1 : 1 + pairs, :, :c_in] = xc_ref[...]
    for row in range(pairs):
        xcp[1 + row, :, c_in:] = ones
    xcat[...] = jnp.zeros_like(xcat)
    rad[...] = jnp.zeros_like(rad)
    pool[...] = jnp.zeros_like(pool)
    for side, arrives in ((0, has_up), (1, has_down)):
        @pl.when(jnp.logical_not(arrives))
        def _(side=side):
            xs[place_of[side]] = jnp.zeros(xs.shape[1:], xs.dtype)

    @pl.when(inner)
    def _():
        for n in range(HALO):
            pass_on(0, n)
        passed_on(0)

    for load in x_loads:
        load.wait()

    parts = (
        (fwd_a, inv_a, spec_a, flip, flip, 0) + plans[0],
        (fwd_b, inv_b, spec_b, (pairs - 1) * (1 - flip), (pairs - 1) * (1 - flip), pairs - 1) + plans[1],
    )

    def compute(part, n):
        fwd, inv, spec, first, out, slot, half, _, made = part
        depth = fwd.shape[1]
        cells = made * span
        for u in range(PAIRS):
            for k in range(2):
                lane = slice(LANES * k, LANES * k + c_in)
                for row in range(depth // span):
                    xcat[u, row * span : (row + 1) * span, lane] = xs[first + row, n * chunk + 2 * u + k]
        for u in range(PAIRS):
            xf_s[u, : 2 * half] = dot(fwd[...], xcat[u, :depth]).astype(jnp.bfloat16)
        for u in range(PAIRS):
            xf = xf_s[u, : 2 * half]
            e2 = dot(xf, w2[...])
            for k in range(2):
                lane = slice(LANES * k, LANES * (k + 1))
                e1 = dot(xf[:, lane], wz[:, :main])
                re, im = e1[:half], e1[half:]
                y1_s[u, k, : 2 * half] = jnp.concatenate(
                    [
                        re * spec[0, :, :main] - im * spec[1, :, :main],
                        re * spec[2, :, :main] + im * spec[3, :, :main],
                    ],
                    axis=0,
                ).astype(jnp.bfloat16)
                re, im = e2[:half, lane], e2[half:, lane]
                y2_s[u, : 2 * half, lane] = jnp.concatenate(
                    [
                        re * spec[0, :, main:] - im * spec[1, :, main:],
                        re * spec[2, :, main:] + im * spec[3, :, main:],
                    ],
                    axis=0,
                ).astype(jnp.bfloat16)
        for u in range(PAIRS):
            t1 = [dot(inv[...], y1_s[u, k, : 2 * half]) for k in range(2)]
            t2 = dot(inv[...], y2_s[u, : 2 * half])
            for k in range(2):
                g = n * chunk + 2 * u + k
                mine = t2[:, LANES * k : LANES * (k + 1)]
                for row in range(made):
                    cut = slice(row * span, (row + 1) * span)
                    dwg_ref[g, out + row, :, :main] = t1[k][cut].astype(jnp.bfloat16)
                    dwg_ref[g, out + row, :, main:] = mine[cut, : chans - main].astype(jnp.bfloat16)
                here = slice(2 * u + k, 2 * u + k + 1)
                pool[n, here, :main] += t1[k][cells : cells + 1] + t1[k][cells + 1 : cells + 2]
                pool[n, here, main:] += mine[cells : cells + 1] + mine[cells + 1 : cells + 2]
            where = slice(slot, slot + made)
            rad[where, :, :main] += (
                jnp.abs(t1[0][:cells]) + jnp.abs(t1[1][:cells])
            ).reshape(made, span, main)
            rad[where, :, main:] += (
                jnp.abs(t2[:cells, :LANES]) + jnp.abs(t2[:cells, LANES:])
            ).reshape(made, span, LANES)

    def center(part):
        fwd, inv, spec, first, out, _, half, _, made = part
        depth = fwd.shape[1]
        cells = made * span
        both = xcp[pl.ds(first, depth // span)].reshape(depth, LANES)
        xf = dot(fwd[...], both).astype(jnp.bfloat16)
        e = dot(xf, wz[...])
        re, im = e[:half], e[half:]
        y = jnp.concatenate(
            [re * spec[0] - im * spec[1], re * spec[2] + im * spec[3]], axis=0
        ).astype(jnp.bfloat16)
        t = dot(inv[...], y)
        bias = bd_ref[...][None, :]
        for row in range(made):
            dwc_ref[out + row] = t[row * span : (row + 1) * span, :chans] + bias
        pool[chunks, 0:1, :chans] += (
            t[cells : cells + 1, :chans] + t[cells + 1 : cells + 2, :chans] + cells * bias
        )

    def done_copy(n):
        where = pl.ds(n * chunk, chunk)
        return pltpu.make_async_copy(dwg_ref.at[where], outs[0].at[where], g_sem.at[n])

    results = [
        pltpu.make_async_copy(source, target, o_sem.at[k])
        for k, (source, target) in enumerate(
            zip((dwc_ref, gates_ref, stats_ref, feat_ref), outs[1:])
        )
    ]

    def first_turn(n, _):
        compute(parts[0], n)
        for k in range(HALO):
            @pl.when(n == chunks - HALO + k)
            def _(k=k):
                late(lambda side: pass_on(side, k))

        return 0

    lax.fori_loop(0, chunks, first_turn, 0)

    radii = ((send_a, recv_a, full_a), (send_b, recv_b, full_b))

    def reduce_copies(which):
        send, recv, _ = radii[which]
        per = recv.shape[1]
        return [
            remote(
                send.at[pl.ds(place["gen"] * per, per)], recv.at[my_gen],
                rs_send.at[which, off], rs_recv.at[which, off], place,
            )
            for off, place in gen_peers
        ]

    def gather_copies(which):
        full, per = radii[which][2], radii[which][1].shape[1]
        mine = full.at[pl.ds(my_gen * per, per)]
        return [
            remote(mine, mine, ag_send.at[which, off], ag_recv.at[which, off], place)
            for off, place in gen_peers
        ]

    def reduce_start(which):
        send, recv, _ = radii[which]
        per = recv.shape[1]
        _, _, _, _, _, slot, _, _, made = parts[which]
        tiles = made * span // 8
        send[:tiles] = rad[slot : slot + made].reshape(tiles, 8, wide).astype(jnp.bfloat16)
        if count_gen * per > tiles:
            send[tiles:] = jnp.zeros((count_gen * per - tiles, 8, wide), jnp.bfloat16)
        recv[my_gen] = send[pl.ds(my_gen * per, per)]
        for copy in reduce_copies(which):
            copy.start()

    def gather_start(which):
        _, recv, full = radii[which]
        per = recv.shape[1]
        for copy in reduce_copies(which):
            copy.wait()
        total = recv[0].astype(jnp.float32)
        for slot in range(1, count_gen):
            total = total + recv[slot].astype(jnp.float32)
        full[pl.ds(my_gen * per, per)] = total.astype(jnp.bfloat16)
        for copy in gather_copies(which):
            copy.start()

    reduce_start(0)

    own = wr_ref[:, :chans]
    for other in range(1, count_ch):
        own = jnp.where(my_ch == other, wr_ref[:, other * chans : (other + 1) * chans], own)
    units = own.shape[0]
    own_wr[...] = jnp.zeros_like(own_wr)
    own_wr[:units, :chans] = own
    turned = own_wr[...].T
    turned_high = turned.astype(jnp.bfloat16)
    wr_high[...] = turned_high
    wr_low[...] = (turned - turned_high.astype(jnp.float32)).astype(jnp.bfloat16)
    own_wr[...] = jnp.zeros_like(own_wr)
    we_high = we_ref[...].astype(jnp.bfloat16).astype(jnp.float32)
    own_wr[:units, :chans] = we_high
    own_wr[GROUP : GROUP + units, :chans] = we_high
    own_wr[2 * GROUP : 2 * GROUP + units, :chans] = we_ref[...] - we_high
    we_three[...] = own_wr[...].astype(jnp.bfloat16)
    br_wide[...] = jnp.zeros_like(br_wide)
    br_wide[0:1, :units] = br_ref[...][None, :]
    late(passed_on)
    for side, arrives in ((0, has_up), (1, has_down)):
        @pl.when(arrives)
        def _(side=side):
            xcp[place_of[side], :, :c_in] = xcs[side]
            xcp[place_of[side], :, c_in:] = ones

    center(parts[0])
    center(parts[1])
    results[0].start()

    def second_turn(n, _):
        compute(parts[1], n)
        done_copy(n).start()
        return 0

    lax.fori_loop(0, chunks // 2, second_turn, 0)
    gather_start(0)
    lax.fori_loop(chunks // 2, chunks, second_turn, 0)

    pooled = pool[...].reshape(gens + chunk, wide) * (1.0 / all_cells)
    high = pooled.astype(jnp.bfloat16)
    low = (pooled - high.astype(jnp.float32)).astype(jnp.bfloat16)
    part = dot(high, wr_high[...]) + (dot(low, wr_high[...]) + dot(high, wr_low[...]))
    packed = part[:chunk]
    for n in range(1, chunks):
        packed = packed + pltpu.roll(part[n * chunk : (n + 1) * chunk], n * GROUP, 1)
    mine = my_row * count_ch + my_ch
    squeeze[mine, :chunk] = packed
    squeeze[mine, chunk:] = part[gens:]
    sq_copies = [
        remote(squeeze.at[mine], squeeze.at[mine], sq_send.at[off], sq_recv.at[off], place)
        for off, place in side_peers
    ]
    for copy in sq_copies:
        copy.start()
    reduce_start(1)
    for copy in sq_copies:
        copy.wait()
    total = squeeze[0]
    for slot in range(1, count_row * count_ch):
        total = total + squeeze[slot]
    spread = [total[:chunk]]
    spread += [pltpu.roll(total[:chunk], LANES - n * GROUP, 1) for n in range(1, chunks)]
    spread.append(total[chunk:] + br_wide[...])
    total = jnp.concatenate(spread, axis=0)
    total = jnp.where(lax.broadcasted_iota(jnp.int32, total.shape, 1) < GROUP, total, 0.0)
    high = total.astype(jnp.bfloat16).astype(jnp.float32)
    three = high + pltpu.roll(total - high, GROUP, 1) + pltpu.roll(high, 2 * GROUP, 1)
    ex_all = dot(three.astype(jnp.bfloat16), we_three[...])
    ex_gens = ex_all[:gens, :chans]
    ex_center = ex_all[gens : gens + 1, :chans] + be_ref[...][None, :]
    gate[my_gen] = jnp.sum(jnp.abs(ex_gens), axis=0, keepdims=True)
    gt_copies = [
        remote(gate.at[my_gen], gate.at[my_gen], gt_send.at[off], gt_recv.at[off], place)
        for off, place in gen_peers
    ]
    for copy in gt_copies:
        copy.start()

    gather_start(1)
    for copy in gt_copies:
        copy.wait()
    gate_radius = gate[0]
    for slot in range(1, count_gen):
        gate_radius = gate_radius + gate[slot]
    gate_center, slope_val, spread_term = relax_gate(ex_center, gate_radius)
    gates_ref[...] = (slope_val * ex_gens)[:, None, :]
    stats_ref[0:1] = gate_center
    stats_ref[1:2] = spread_term
    stats_ref[2:3] = slope_val * gate_radius + spread_term
    results[1].start()
    results[2].start()
    for which in range(2):
        for copy in gather_copies(which):
            copy.wait()
        _, _, _, _, out, _, _, _, made = parts[which]
        whole = radii[which][2][: made * span // 8].astype(jnp.float32).reshape(made, span, wide)
        for row in range(made):
            feat_ref[out + row] = whole[row, :, :chans]
    results[3].start()

    for side, arrives, leaves in ((0, has_up, has_down), (1, has_down, has_up)):
        @pl.when(leaves)
        def _(side=side):
            center_copy(side).wait_send()
            for n in range(HALO):
                halo_copy(side, n).wait_send()

        @pl.when(arrives)
        def _(side=side):
            for n in range(HALO):
                for copy in forwards(side, n):
                    copy.wait_send()

    for n in range(chunks):
        done_copy(n).wait()
    for copy in results:
        copy.wait()


def main_call(mesh, taps, cols, x, xc, w_expand, b_expand, w_depth, b_depth, wr, br, we, be):
    gens, pairs, span, c_in = x.shape
    chans = w_expand.shape[1]
    chunk = 2 * PAIRS
    count_gen, count_row, count_ch = mesh["gen"], mesh["row"], mesh["ch"]
    wide = -(-chans // LANES) * LANES
    chunks = gens // chunk
    assert wide == 3 * LANES and gens % (HALO * count_ch) == 0 and gens == chunks * chunk
    assert we.shape[0] <= GROUP and chunks * GROUP <= LANES and chunks >= HALO
    plans, tables = [], []
    for made in (pairs - 1, 1):
        forward, inverse, tap_waves, half, step = transforms(made * span // cols, cols, taps)
        plans.append((half, step, made))
        tables += [jnp.asarray(forward), jnp.asarray(inverse), jnp.asarray(tap_waves)]
    half_a, half_b = plans[0][0], plans[1][0]
    hbm = pl.BlockSpec(memory_space=pltpu.HBM)
    dma = pltpu.SemaphoreType.DMA
    bf16, f32 = jnp.bfloat16, jnp.float32
    args = [x, xc] + tables + [w_expand, b_expand, w_depth, b_depth, wr, br, we, be]
    outs = [
        jax.ShapeDtypeStruct((gens, pairs, span, chans), bf16),
        jax.ShapeDtypeStruct((pairs, span, chans), f32),
        jax.ShapeDtypeStruct((gens, 1, chans), f32),
        jax.ShapeDtypeStruct((3, chans), f32),
        jax.ShapeDtypeStruct((pairs, span, chans), f32),
    ]
    held = [pltpu.VMEM(one.shape, one.dtype) for one in args[1:] + outs]
    sums = []
    for half, step, made in plans:
        per = -(-(made * span // 8) // count_gen)
        whole = pltpu.VMEM((count_gen * per, 8, wide), bf16)
        sums += [whole, pltpu.VMEM((count_gen, per, 8, wide), bf16), whole]
    side = count_row * count_ch
    deep = (pairs + 1) * span
    return pl.pallas_call(
        functools.partial(main_kernel, mesh, tuple(plans), chunk),
        in_specs=[hbm] * len(args),
        out_specs=[hbm] * OUTS,
        out_shape=outs,
        scratch_shapes=held
        + [
            dma((chunks,)), dma((OUTS - 1,)),
            pltpu.VMEM((pairs + 2, gens, span, c_in), bf16), dma((HELD,)), dma((pairs,)),
            pltpu.VMEM((PAIRS, deep, 2 * LANES), bf16),
            pltpu.VMEM((2, span, c_in), bf16),
            pltpu.VMEM((pairs + 2, span, LANES), bf16),
            pltpu.VMEM((LANES, wide), f32),
            pltpu.VMEM((LANES, wide), bf16),
            pltpu.VMEM((2 * LANES, 2 * LANES), bf16),
            pltpu.VMEM((4, half_a, wide), f32),
            pltpu.VMEM((4, half_b, wide), f32),
            pltpu.VMEM((PAIRS, 2 * half_a, 2 * LANES), bf16),
            pltpu.VMEM((PAIRS, 2, 2 * half_a, 2 * LANES), bf16),
            pltpu.VMEM((PAIRS, 2 * half_a, 2 * LANES), bf16),
            pltpu.VMEM((pairs, span, wide), f32),
            pltpu.VMEM((chunks + 1, chunk, wide), f32),
            pltpu.VMEM((LANES, wide), f32), pltpu.VMEM((wide, LANES), bf16), pltpu.VMEM((wide, LANES), bf16),
            pltpu.VMEM((LANES, wide), bf16), pltpu.VMEM((chunk, LANES), f32),
        ]
        + sums
        + [
            pltpu.VMEM((side, 2 * chunk, LANES), f32),
            pltpu.VMEM((count_gen, 1, chans), f32),
            dma((2, HALO)), dma((2, HALO)),
            dma((2, HALO, count_ch)), dma((2, HALO, count_ch)),
            dma((2,)), dma((2,)),
            dma((2, count_gen)), dma((2, count_gen)), dma((2, count_gen)), dma((2, count_gen)),
            dma((side,)), dma((side,)), dma((count_gen,)), dma((count_gen,)),
        ],
        compiler_params=pltpu.CompilerParams(
            collective_id=1, has_side_effects=True, vmem_limit_bytes=ROOM
        ),
    )(*[pltpu.with_memory_space_constraint(one, pltpu.HBM) for one in args])


def final_kernel(
    block, dw_ref, gates_ref, dwc_ref, feat_ref, stats_ref, og_hbm, oc_hbm, ob_hbm,
    og_ref, oc_ref, ob_ref, og_sem, oc_sem, ob_sem,
):
    turns = dw_ref.shape[0] // block
    gate_center = stats_ref[0:1]

    def save(n):
        where = pl.ds(n * block, block)
        return pltpu.make_async_copy(og_ref.at[where], og_hbm.at[where], og_sem.at[n])

    def turn(n, _):
        for k in range(block):
            g = n * block + k
            og_ref[g] = (
                dwc_ref[...] * gates_ref[g] + gate_center * dw_ref[g].astype(jnp.float32)
            ).astype(jnp.bfloat16)
        save(n).start()
        return 0

    lax.fori_loop(0, turns, turn, 0)
    oc_ref[...] = dwc_ref[...] * gate_center
    oc_save = pltpu.make_async_copy(oc_ref, oc_hbm, oc_sem)
    oc_save.start()
    ob_ref[...] = jnp.abs(dwc_ref[...]) * stats_ref[1:2] + feat_ref[...] * stats_ref[2:3]
    ob_save = pltpu.make_async_copy(ob_ref, ob_hbm, ob_sem)
    ob_save.start()
    for n in range(turns):
        save(n).wait()
    oc_save.wait()
    ob_save.wait()


def final_call(dw_gens, gates, dw_center, feat, stats):
    gens = dw_gens.shape[0]
    block = 4
    hbm = pl.BlockSpec(memory_space=pltpu.HBM)
    vmem = pl.BlockSpec(memory_space=pltpu.VMEM)
    dma = pltpu.SemaphoreType.DMA
    outs = [jax.ShapeDtypeStruct(one.shape, one.dtype) for one in (dw_gens, dw_center, feat)]
    out_gens, out_center, out_box = pl.pallas_call(
        functools.partial(final_kernel, block),
        in_specs=[vmem] * 5,
        out_specs=[hbm] * 3,
        out_shape=outs,
        scratch_shapes=[pltpu.VMEM(one.shape, one.dtype) for one in outs]
        + [dma((gens // block,)), dma(()), dma(())],
        compiler_params=pltpu.CompilerParams(vmem_limit_bytes=12 << 20),
    )(dw_gens, gates, dw_center, feat, stats)
    return out_center, out_gens, out_box


def on_device(
    shape, x_center, x_gens, w_expand, b_expand, w_depth, b_depth, w_reduce, b_reduce, w_excite, b_excite
):
    gens, rows, cols, c_in = x_gens.shape
    chans = w_expand.shape[1]
    taps = w_depth.shape[0]
    margin = taps // 2
    pairs, span = rows // margin, margin * cols
    x = x_gens.reshape(gens, pairs, span, c_in)
    xc = x_center.reshape(pairs, span, c_in)
    dw_gens, dw_center, gates, stats, feat = main_call(
        shape, taps, cols, x, xc, w_expand, b_expand, w_depth, b_depth,
        w_reduce.T, b_reduce, w_excite, b_excite,
    )
    out_center, out_gens, out_box = final_call(dw_gens, gates, dw_center, feat, stats)
    image = (rows, cols, chans)
    return out_center.reshape(image), out_gens.reshape((gens,) + image), out_box.reshape(image)


def solution(mesh):
    in_specs = (
        P(("grp", "row"), None, None),
        P(("grp", "gen"), "row", None, None),
        P(None, "ch"),
        P("ch"),
        P(None, None, "ch"),
        P("ch"),
        P(),
        P(),
        P(None, "ch"),
        P("ch"),
    )
    out_specs = (
        P(("grp", "row"), None, "ch"),
        P(("grp", "gen"), "row", None, "ch"),
        P(("grp", "row"), None, "ch"),
    )
    return jax.shard_map(
        functools.partial(on_device, dict(mesh.shape)), mesh=mesh, in_specs=in_specs, out_specs=out_specs, check_vma=False
    )
```

```python
import functools

import jax
import jax.numpy as jnp
import ml_dtypes
import numpy as np
from jax import lax
from jax.experimental import pallas as pl
from jax.experimental.pallas import tpu as pltpu
from jax.sharding import PartitionSpec as P

MESH = pl.DeviceIdType.MESH
LANES = 128
PAIRS = 4
GROUP = 32
ROOM = 40 << 20
OUTS = 3
HELD = 16
HALO = 2


def dot(a, b):
    return jnp.dot(a, b, preferred_element_type=jnp.float32)


def split(values):
    high = values.astype(ml_dtypes.bfloat16)
    return high, (values - high.astype(np.float64)).astype(ml_dtypes.bfloat16)


def transforms(rows, cols, taps):
    m = taps // 2
    n_r, n_c = rows + 2 * m, cols + m
    count = n_r * n_c
    r_in, c_in = np.arange(n_r)[:, None], np.arange(cols)[None, :]
    r_out = np.arange(rows)[:, None]
    tap_r, tap_c = np.arange(taps)[:, None], np.arange(taps)[None, :] - m

    def angle(freq, r, c):
        return (2 * np.pi * (freq[0] * r / n_r + freq[1] * c / n_c)).ravel()

    seen, double, single = set(), [], []
    for freq in [(u, v) for u in range(n_r) for v in range(n_c)]:
        twin = (-freq[0] % n_r, -freq[1] % n_c)
        if freq not in seen:
            (single if twin == freq else double).append(freq)
        seen |= {freq, twin}
    blocks = [[], [], [], [], [], [], [], []]
    for freq in double:
        a, t, o = angle(freq, r_in, c_in), angle(freq, tap_r, tap_c), angle(freq, r_out, c_in)
        entry = (
            np.cos(a), -np.sin(a), np.cos(t), np.sin(t), np.sin(t), np.cos(t),
            2 * np.cos(o) / count, -2 * np.sin(o) / count,
        )
        for block, part in zip(blocks, entry):
            block.append(part)
    single += [None] * (len(single) % 2)
    for one, two in zip(single[::2], single[1::2]):
        def wave(freq, r, c):
            scale = 0.0 if freq is None else 1.0
            return scale * np.cos(angle(freq or (0, 0), r, c))

        entry = (
            wave(one, r_in, c_in), wave(two, r_in, c_in),
            wave(one, tap_r, tap_c), 0 * wave(one, tap_r, tap_c),
            0 * wave(one, tap_r, tap_c), wave(two, tap_r, tap_c),
            wave(one, r_out, c_in) / count, wave(two, r_out, c_in) / count,
        )
        for block, part in zip(blocks, entry):
            block.append(part)
    half = -(-len(blocks[0]) // 8) * 8
    blocks = [np.pad(np.array(b), ((0, half - len(b)), (0, 0))) for b in blocks]
    forward = np.concatenate(blocks[:2], axis=0)
    inverse = np.concatenate([blocks[6].T, blocks[7].T], axis=1)
    waves = np.concatenate(blocks[2:6], axis=0)
    high, low = split(waves)
    step = -(-taps * taps // 8) * 8
    tap_waves = np.zeros((4 * half, 4 * step), ml_dtypes.bfloat16)
    for slot, part in enumerate((high, high, low)):
        tap_waves[:, slot * step : slot * step + taps * taps] = part
    return forward.astype(ml_dtypes.bfloat16), inverse.astype(ml_dtypes.bfloat16), tap_waves, half, step


def windows(rows, cols, taps, depth):
    m = taps // 2
    tap_r, tap_c = np.divmod(np.arange(taps * taps)[:, None], taps)
    row, col = np.divmod(np.arange(rows * cols)[None, :], cols)
    inside = (col - tap_c + m >= 0) & (col - tap_c + m < cols)
    masks = np.zeros((3, depth, rows * cols), ml_dtypes.bfloat16)
    masks[0, : taps * taps] = inside
    masks[1, : taps * taps] = inside & (row - tap_r + m < 0)
    masks[2, : taps * taps] = inside & (row - tap_r + m >= rows)
    return masks


def relax_gate(ex_center, gate_radius):
    low_end = ex_center - gate_radius
    high_end = ex_center + gate_radius
    sig_low = jax.nn.sigmoid(low_end)
    sig_high = jax.nn.sigmoid(high_end)
    slope_val = jnp.minimum(sig_low * (1.0 - sig_low), sig_high * (1.0 - sig_high))
    gate_center = slope_val * ex_center + 0.5 * (
        sig_high + sig_low - slope_val * (high_end + low_end)
    )
    spread_term = 0.5 * (sig_high - sig_low - slope_val * (high_end - low_end))
    return (gate_center, slope_val, spread_term)


def main_kernel(mesh, plans, chunk, x_hbm, *refs):
    main_body(
        mesh, plans, chunk, x_hbm, refs[:HELD], refs[HELD : HELD + OUTS],
        refs[HELD + OUTS : 2 * HELD + OUTS], *refs[2 * HELD + OUTS :],
    )


def main_body(
    mesh, plans, chunk, x_hbm, sources, outs, locals_,
    oc_ref, ob_ref, dwg_ref, dwc_ref, gates_ref, stats_ref, g_sem, o_sem, xs, l_sem, x_sem,
    xall, xcs, xcp, sums, taps_f, og_ref, wf, wz, w2, spec_a, spec_b, xf_s, y1_s, y2_s,
    rad, pool, own_wr, wr_high, wr_low, we_three, br_wide, ex,
    send_a, recv_a, full_a, recv_b, squeeze, gate,
    h_send, h_recv, f_send, f_recv, c_send, c_recv,
    rs_send, rs_recv, ag_send, ag_recv, bc_send, bc_recv, sq_send, sq_recv, gt_send, gt_recv,
):
    (
        xc_ref, fwd_a, inv_a, tw_a, fwd_b, inv_b, tw_b, mask_ref,
        w_ref, b_ref, wd_ref, bd_ref, wr_ref, br_ref, we_ref, be_ref,
    ) = locals_
    count_gen, count_row, count_ch = mesh["gen"], mesh["row"], mesh["ch"]
    my_gen = lax.axis_index("gen")
    my_row = lax.axis_index("row")
    my_ch = lax.axis_index("ch")
    has_up = my_row > 0
    has_down = my_row < count_row - 1
    last = jnp.logical_and(has_up, jnp.logical_not(has_down))
    inner = jnp.logical_and(has_up, has_down)
    flip = jnp.where(last, 1, 0)
    gens, pairs, span, chans = dwg_ref.shape
    c_in = w_ref.shape[0]
    taps = wd_ref.shape[0]
    wide = wz.shape[1]
    main = wide - LANES
    chunks = gens // chunk
    all_cells = pairs * span * count_row
    sub = gens // (HALO * count_ch)

    def remote(src, dst, send_sem, recv_sem, place):
        return pltpu.make_async_remote_copy(
            src_ref=src, dst_ref=dst, send_sem=send_sem, recv_sem=recv_sem,
            device_id=place, device_id_type=MESH,
        )

    gen_peers = [(off, {"gen": lax.rem(my_gen + off, count_gen)}) for off in range(1, count_gen)]
    side_peers = []
    for off_row in range(count_row):
        for off_ch in range(count_ch):
            if off_row or off_ch:
                place = {
                    "row": lax.rem(my_row + off_row, count_row),
                    "ch": lax.rem(my_ch + off_ch, count_ch),
                }
                side_peers.append((off_row * count_ch + off_ch, place))
    barrier = pltpu.get_barrier_semaphore()
    for _, place in gen_peers + side_peers:
        pl.semaphore_signal(barrier, inc=1, device_id=place, device_id_type=MESH)

    loads = [
        pltpu.make_async_copy(source, target, l_sem.at[k])
        for k, (source, target) in enumerate(zip(sources, locals_))
    ]
    for load in loads:
        load.start()
    x_loads = [
        pltpu.make_async_copy(x_hbm.at[:, row], xs.at[1 + row], x_sem.at[row]) for row in range(pairs)
    ]
    for load in x_loads:
        load.start()
    pl.semaphore_wait(barrier, len(gen_peers) + len(side_peers))

    row_place = (
        {"row": lax.rem(my_row + 1, count_row)},
        {"row": lax.rem(my_row + count_row - 1, count_row)},
    )
    edge = (pairs - 1, 0)
    place_of = (0, pairs + 1)

    def halo_copy(side, n):
        where = pl.ds((n * count_ch + my_ch) * sub, sub)
        return remote(
            x_hbm.at[where, edge[side]], xs.at[place_of[side], where],
            h_send.at[side, n], h_recv.at[side, n], row_place[side],
        )

    def center_copy(side):
        return remote(
            sources[0].at[edge[side]], xcs.at[side], c_send.at[side], c_recv.at[side], row_place[side]
        )

    def forwards(side, n):
        where = xs.at[place_of[side], pl.ds((n * count_ch + my_ch) * sub, sub)]
        return [
            remote(
                where, where, f_send.at[side, n, off], f_recv.at[side, n, off],
                {"ch": lax.rem(my_ch + off, count_ch)},
            )
            for off in range(1, count_ch)
        ]

    for side, leaves in ((0, has_down), (1, has_up)):
        @pl.when(leaves)
        def _(side=side):
            center_copy(side).start()
            for n in range(HALO):
                halo_copy(side, n).start()

    def pass_on(side, n):
        halo_copy(side, n).wait_recv()
        for copy in forwards(side, n):
            copy.start()

    def passed_on(side):
        center_copy(side).wait_recv()
        for n in range(HALO):
            for copy in forwards(side, n):
                copy.wait_recv()

    def late(action):
        @pl.when(last)
        def _():
            action(0)

        @pl.when(has_down)
        def _():
            action(1)

    mine = my_row * count_ch + my_ch
    sq_copies = [
        remote(squeeze.at[mine], squeeze.at[mine], sq_send.at[off], sq_recv.at[off], place)
        for off, place in side_peers
    ]
    gt_copies = [
        remote(gate.at[my_gen], gate.at[my_gen], gt_send.at[off], gt_recv.at[off], place)
        for off, place in gen_peers
    ]

    def send_squeeze():
        pooled = pool[...].reshape(gens + chunk, wide) * (1.0 / all_cells)
        high = pooled.astype(jnp.bfloat16)
        low = (pooled - high.astype(jnp.float32)).astype(jnp.bfloat16)
        part = dot(high, wr_high[...]) + (dot(low, wr_high[...]) + dot(high, wr_low[...]))
        packed = part[:chunk]
        for n in range(1, chunks):
            packed = packed + pltpu.roll(part[n * chunk : (n + 1) * chunk], n * GROUP, 1)
        squeeze[mine, :chunk] = packed
        squeeze[mine, chunk:] = part[gens:]
        for copy in sq_copies:
            copy.start()

    def send_gate():
        for copy in sq_copies:
            copy.wait()
        total = squeeze[0]
        for slot in range(1, count_row * count_ch):
            total = total + squeeze[slot]
        spread = [total[:chunk]]
        spread += [pltpu.roll(total[:chunk], LANES - n * GROUP, 1) for n in range(1, chunks)]
        spread.append(total[chunk:] + br_wide[...])
        total = jnp.concatenate(spread, axis=0)
        total = jnp.where(lax.broadcasted_iota(jnp.int32, total.shape, 1) < GROUP, total, 0.0)
        high = total.astype(jnp.bfloat16).astype(jnp.float32)
        three = high + pltpu.roll(total - high, GROUP, 1) + pltpu.roll(high, 2 * GROUP, 1)
        ex_all = dot(three.astype(jnp.bfloat16), we_three[...])
        ex[...] = ex_all[:, :chans]
        ex_gens = ex[:gens]
        gate[my_gen] = jnp.sum(jnp.abs(ex_gens), axis=0, keepdims=True)
        for copy in gt_copies:
            copy.start()

    def finish_gate():
        for copy in gt_copies:
            copy.wait()
        gate_radius = gate[0]
        for slot in range(1, count_gen):
            gate_radius = gate_radius + gate[slot]
        ex_center = ex[gens : gens + 1] + be_ref[...][None, :]
        gate_center, slope_val, spread_term = relax_gate(ex_center, gate_radius)
        gates_ref[...] = (slope_val * ex[:gens])[:, None, :]
        stats_ref[0:1] = gate_center
        stats_ref[1:2] = spread_term
        stats_ref[2:3] = slope_val * gate_radius + spread_term

    for load in loads:
        load.wait()
    wf[...] = jnp.zeros_like(wf)
    wf[:c_in, :chans] = w_ref[...].astype(jnp.float32)
    bias = b_ref[...][None, :]
    bias_high = bias.astype(jnp.bfloat16).astype(jnp.float32)
    wf[c_in : c_in + 1, :chans] = bias_high
    wf[c_in + 1 : c_in + 2, :chans] = bias - bias_high
    wz[...] = wf[...].astype(jnp.bfloat16)
    w2[...] = jnp.zeros_like(w2)
    w2[:LANES, :LANES] = wz[:, main:]
    w2[LANES:, LANES:] = wz[:, main:]
    wf[...] = jnp.zeros_like(wf)
    taps_f[...] = jnp.zeros_like(taps_f)
    step = plans[0][1]
    for row in range(taps):
        one = wd_ref[row]
        taps_f[row * taps : (row + 1) * taps, :chans] = one
        high = one.astype(jnp.bfloat16).astype(jnp.float32)
        for slot, part in enumerate((high, one - high, high)):
            start = slot * step + row * taps
            wf[start : start + taps, :chans] = part
    wtap = wf[...].astype(jnp.bfloat16)
    spec_a[...] = dot(tw_a[...], wtap).reshape(spec_a.shape)
    spec_b[...] = dot(tw_b[...], wtap).reshape(spec_b.shape)
    ones = jnp.where(
        lax.broadcasted_iota(jnp.int32, (span, LANES - c_in), 1) < 2, 1.0, 0.0
    ).astype(jnp.bfloat16)
    xcp[...] = jnp.zeros_like(xcp)
    xcp[1 : 1 + pairs, :, :c_in] = xc_ref[...]
    for row in range(pairs):
        xcp[1 + row, :, c_in:] = ones
    xall[...] = jnp.zeros_like(xall)
    rad[...] = jnp.zeros_like(rad)
    own = wr_ref[:, :chans]
    for other in range(1, count_ch):
        own = jnp.where(my_ch == other, wr_ref[:, other * chans : (other + 1) * chans], own)
    units = own.shape[0]
    own_wr[...] = jnp.zeros_like(own_wr)
    own_wr[:units, :chans] = own
    turned = own_wr[...].T
    turned_high = turned.astype(jnp.bfloat16)
    wr_high[...] = turned_high
    wr_low[...] = (turned - turned_high.astype(jnp.float32)).astype(jnp.bfloat16)
    own_wr[...] = jnp.zeros_like(own_wr)
    we_high = we_ref[...].astype(jnp.bfloat16).astype(jnp.float32)
    own_wr[:units, :chans] = we_high
    own_wr[GROUP : GROUP + units, :chans] = we_high
    own_wr[2 * GROUP : 2 * GROUP + units, :chans] = we_ref[...] - we_high
    we_three[...] = own_wr[...].astype(jnp.bfloat16)
    br_wide[...] = jnp.zeros_like(br_wide)
    br_wide[0:1, :units] = br_ref[...][None, :]

    def fill(row):
        for g in range(gens):
            lane = slice(LANES * (g % 2), LANES * (g % 2) + c_in)
            xall[g // 2, row * span : (row + 1) * span, lane] = xs[row, g]

    def take(side):
        xcp[place_of[side], :, :c_in] = xcs[side]
        xcp[place_of[side], :, c_in:] = ones
        fill(place_of[side])

    @pl.when(inner)
    def _():
        for n in range(HALO):
            pass_on(0, n)
        passed_on(0)
        take(0)

    for row, load in enumerate(x_loads):
        load.wait()
        fill(1 + row)

    above = jnp.where(has_up, 0.0, 1.0)
    below = jnp.where(has_down, 0.0, 1.0)
    window = (
        mask_ref[0].astype(jnp.float32)
        - above * mask_ref[1].astype(jnp.float32)
        - below * mask_ref[2].astype(jnp.float32)
    ).astype(jnp.bfloat16)
    body = slice(span, (1 + pairs) * span)
    deep = window.shape[0]
    for q in range(gens // 2):
        both = dot(window, xall[q, body]).astype(jnp.bfloat16)
        sums[2 * q] = both[:, :LANES]
        sums[2 * q + 1] = both[:, LANES:]
    sums[gens] = dot(window, xcp[1 : 1 + pairs].reshape(pairs * span, LANES)).astype(jnp.bfloat16)
    for n in range(chunks):
        block = dot(sums[n * chunk : (n + 1) * chunk].reshape(chunk * deep, LANES), wz[...])
        pool[n] = jnp.sum(block.reshape(chunk, deep, wide) * taps_f[...], axis=1)
    pool[chunks] = jnp.zeros((chunk, wide), jnp.float32)
    pool[chunks, 0:1] = jnp.sum(dot(sums[gens], wz[...]) * taps_f[...], axis=0, keepdims=True)
    pool[chunks, 0:1, :chans] += (pairs * span) * bd_ref[...][None, :]
    send_squeeze()

    parts = (
        (fwd_a, inv_a, spec_a, flip, flip, 0) + plans[0],
        (fwd_b, inv_b, spec_b, (pairs - 1) * (1 - flip), (pairs - 1) * (1 - flip), pairs - 1) + plans[1],
    )

    def compute(part, n):
        fwd, inv, spec, first, out, slot, half, _, made = part
        depth = fwd.shape[1]
        cells = made * span
        rows = pl.ds(pl.multiple_of(first * span, span), depth)
        for u in range(PAIRS):
            both = xall[n * PAIRS + u, rows]
            xf_s[u, : 2 * half] = dot(fwd[...], both).astype(jnp.bfloat16)
        for u in range(PAIRS):
            xf = xf_s[u, : 2 * half]
            e2 = dot(xf, w2[...])
            for k in range(2):
                lane = slice(LANES * k, LANES * (k + 1))
                e1 = dot(xf[:, lane], wz[:, :main])
                re, im = e1[:half], e1[half:]
                y1_s[u, k, : 2 * half] = jnp.concatenate(
                    [
                        re * spec[0, :, :main] - im * spec[1, :, :main],
                        re * spec[2, :, :main] + im * spec[3, :, :main],
                    ],
                    axis=0,
                ).astype(jnp.bfloat16)
                re, im = e2[:half, lane], e2[half:, lane]
                y2_s[u, : 2 * half, lane] = jnp.concatenate(
                    [
                        re * spec[0, :, main:] - im * spec[1, :, main:],
                        re * spec[2, :, main:] + im * spec[3, :, main:],
                    ],
                    axis=0,
                ).astype(jnp.bfloat16)
        for u in range(PAIRS):
            t1 = [dot(inv[...], y1_s[u, k, : 2 * half]) for k in range(2)]
            t2 = dot(inv[...], y2_s[u, : 2 * half])
            for k in range(2):
                g = n * chunk + 2 * u + k
                mine = t2[:, LANES * k : LANES * (k + 1)]
                for row in range(made):
                    cut = slice(row * span, (row + 1) * span)
                    dwg_ref[g, out + row, :, :main] = t1[k][cut].astype(jnp.bfloat16)
                    dwg_ref[g, out + row, :, main:] = mine[cut, : chans - main].astype(jnp.bfloat16)
            where = slice(slot, slot + made)
            rad[where, :, :main] += (
                jnp.abs(t1[0][:cells]) + jnp.abs(t1[1][:cells])
            ).reshape(made, span, main)
            rad[where, :, main:] += (
                jnp.abs(t2[:cells, :LANES]) + jnp.abs(t2[:cells, LANES:])
            ).reshape(made, span, LANES)

    def center(part):
        fwd, inv, spec, first, out, _, half, _, made = part
        depth = fwd.shape[1]
        cells = made * span
        both = xcp[pl.ds(first, depth // span)].reshape(depth, LANES)
        xf = dot(fwd[...], both).astype(jnp.bfloat16)
        e = dot(xf, wz[...])
        re, im = e[:half], e[half:]
        y = jnp.concatenate(
            [re * spec[0] - im * spec[1], re * spec[2] + im * spec[3]], axis=0
        ).astype(jnp.bfloat16)
        t = dot(inv[...], y)
        bias = bd_ref[...][None, :]
        for row in range(made):
            dwc_ref[out + row] = t[row * span : (row + 1) * span, :chans] + bias

    def done_copy(n):
        where = pl.ds(n * chunk, chunk)
        return pltpu.make_async_copy(og_ref.at[where], outs[0].at[where], g_sem.at[n])

    results = [
        pltpu.make_async_copy(source, target, o_sem.at[k])
        for k, (source, target) in enumerate(
            zip((oc_ref, ob_ref), outs[1:])
        )
    ]

    def first_turn(n, _):
        compute(parts[0], n)
        return 0

    near = chunks // 2
    lax.fori_loop(0, near, first_turn, 0)
    send_gate()
    lax.fori_loop(near, chunks - 1, first_turn, 0)
    for n in range(HALO):
        late(lambda side: pass_on(side, n))
    lax.fori_loop(chunks - 1, chunks, first_turn, 0)

    radii = ((send_a, recv_a, full_a),)

    def reduce_copies(which):
        send, recv, _ = radii[which]
        per = recv.shape[1]
        return [
            remote(
                send.at[pl.ds(place["gen"] * per, per)], recv.at[my_gen],
                rs_send.at[which, off], rs_recv.at[which, off], place,
            )
            for off, place in gen_peers
        ]

    def gather_copies(which):
        full, per = radii[which][2], radii[which][1].shape[1]
        mine = full.at[pl.ds(my_gen * per, per)]
        return [
            remote(mine, mine, ag_send.at[which, off], ag_recv.at[which, off], place)
            for off, place in gen_peers
        ]

    def reduce_start(which):
        send, recv, _ = radii[which]
        per = recv.shape[1]
        _, _, _, _, _, slot, _, _, made = parts[which]
        tiles = made * span // 8
        send[:tiles] = rad[slot : slot + made].reshape(tiles, 8, wide).astype(jnp.bfloat16)
        if count_gen * per > tiles:
            send[tiles:] = jnp.zeros((count_gen * per - tiles, 8, wide), jnp.bfloat16)
        recv[my_gen] = send[pl.ds(my_gen * per, per)]
        for copy in reduce_copies(which):
            copy.start()

    def gather_start(which):
        _, recv, full = radii[which]
        per = recv.shape[1]
        for copy in reduce_copies(which):
            copy.wait()
        total = recv[0].astype(jnp.float32)
        for slot in range(1, count_gen):
            total = total + recv[slot].astype(jnp.float32)
        full[pl.ds(my_gen * per, per)] = total.astype(jnp.bfloat16)
        for copy in gather_copies(which):
            copy.start()

    reduce_start(0)

    finish_gate()
    late(passed_on)
    late(take)
    center(parts[0])
    center(parts[1])

    def second_turn(n, _):
        compute(parts[1], n)
        return 0

    lax.fori_loop(0, chunks - 1, second_turn, 0)
    gather_start(0)
    lax.fori_loop(chunks - 1, chunks, second_turn, 0)

    _, _, _, _, last_out, slot, _, _, made = parts[1]
    recv_b[my_gen] = rad[slot].astype(jnp.bfloat16)
    bc_copies = [
        remote(recv_b.at[my_gen], recv_b.at[my_gen], bc_send.at[off], bc_recv.at[off], place)
        for off, place in gen_peers
    ]
    for copy in bc_copies:
        copy.start()

    gate_center = stats_ref[0:1]

    def out_turn(n, _):
        for k in range(chunk):
            g = n * chunk + k
            og_ref[g] = (
                dwc_ref[...] * gates_ref[g] + gate_center * dwg_ref[g].astype(jnp.float32)
            ).astype(jnp.bfloat16)
        done_copy(n).start()
        return 0

    lax.fori_loop(0, chunks, out_turn, 0)
    oc_ref[...] = dwc_ref[...] * gate_center
    results[0].start()
    base = jnp.abs(dwc_ref[...]) * stats_ref[1:2]
    ob_ref[...] = base
    for copy in gather_copies(0):
        copy.wait()
    _, _, _, _, out, _, _, _, made = parts[0]
    whole = full_a[: made * span // 8].astype(jnp.float32).reshape(made, span, wide)
    for row in range(made):
        ob_ref[out + row] += whole[row, :, :chans] * stats_ref[2:3]
    for copy in bc_copies:
        copy.wait()
    total = recv_b[0].astype(jnp.float32)
    for slot in range(1, count_gen):
        total = total + recv_b[slot].astype(jnp.float32)
    ob_ref[last_out] += total[:, :chans] * stats_ref[2:3]
    results[1].start()

    for side, arrives, leaves in ((0, has_up, has_down), (1, has_down, has_up)):
        @pl.when(leaves)
        def _(side=side):
            center_copy(side).wait_send()
            for n in range(HALO):
                halo_copy(side, n).wait_send()

        @pl.when(arrives)
        def _(side=side):
            for n in range(HALO):
                for copy in forwards(side, n):
                    copy.wait_send()

    for n in range(chunks):
        done_copy(n).wait()
    for copy in results:
        copy.wait()


def main_call(mesh, taps, cols, x, xc, w_expand, b_expand, w_depth, b_depth, wr, br, we, be):
    gens, pairs, span, c_in = x.shape
    chans = w_expand.shape[1]
    chunk = 2 * PAIRS
    count_gen, count_row, count_ch = mesh["gen"], mesh["row"], mesh["ch"]
    wide = -(-chans // LANES) * LANES
    chunks = gens // chunk
    assert wide == 3 * LANES and gens % (HALO * count_ch) == 0 and gens == chunks * chunk
    assert we.shape[0] <= GROUP and chunks * GROUP <= LANES and chunks >= HALO
    plans, tables = [], []
    for made in (pairs - 1, 1):
        forward, inverse, tap_waves, half, step = transforms(made * span // cols, cols, taps)
        plans.append((half, step, made))
        tables += [jnp.asarray(forward), jnp.asarray(inverse), jnp.asarray(tap_waves)]
    half_a, half_b = plans[0][0], plans[1][0]
    hbm = pl.BlockSpec(memory_space=pltpu.HBM)
    dma = pltpu.SemaphoreType.DMA
    bf16, f32 = jnp.bfloat16, jnp.float32
    masks = jnp.asarray(windows(pairs * span // cols, cols, taps, plans[0][1]))
    args = [x, xc] + tables + [masks, w_expand, b_expand, w_depth, b_depth, wr, br, we, be]
    outs = [
        jax.ShapeDtypeStruct((gens, pairs, span, chans), bf16),
        jax.ShapeDtypeStruct((pairs, span, chans), f32),
        jax.ShapeDtypeStruct((pairs, span, chans), f32),
    ]
    held = [pltpu.VMEM(one.shape, one.dtype) for one in args[1:] + outs[1:]]
    held += [pltpu.VMEM(one.shape, one.dtype) for one in outs[:2]]
    held += [pltpu.VMEM((gens, 1, chans), f32), pltpu.VMEM((3, chans), f32)]
    per = -(-(plans[0][2] * span // 8) // count_gen)
    whole = pltpu.VMEM((count_gen * per, 8, wide), bf16)
    sums = [
        whole, pltpu.VMEM((count_gen, per, 8, wide), bf16), whole, pltpu.VMEM((count_gen, span, wide), bf16),
    ]
    side = count_row * count_ch
    step = plans[0][1]
    return pl.pallas_call(
        functools.partial(main_kernel, mesh, tuple(plans), chunk),
        in_specs=[hbm] * len(args),
        out_specs=[hbm] * OUTS,
        out_shape=outs,
        scratch_shapes=held
        + [
            dma((chunks,)), dma((OUTS - 1,)),
            pltpu.VMEM((pairs + 2, gens, span, c_in), bf16), dma((HELD,)), dma((pairs,)),
            pltpu.VMEM((gens // 2, (pairs + 2) * span, 2 * LANES), bf16),
            pltpu.VMEM((2, span, c_in), bf16),
            pltpu.VMEM((pairs + 2, span, LANES), bf16),
            pltpu.VMEM((gens + 1, step, LANES), bf16),
            pltpu.VMEM((step, wide), f32),
            pltpu.VMEM((gens, pairs, span, chans), bf16),
            pltpu.VMEM((LANES, wide), f32),
            pltpu.VMEM((LANES, wide), bf16),
            pltpu.VMEM((2 * LANES, 2 * LANES), bf16),
            pltpu.VMEM((4, half_a, wide), f32),
            pltpu.VMEM((4, half_b, wide), f32),
            pltpu.VMEM((PAIRS, 2 * half_a, 2 * LANES), bf16),
            pltpu.VMEM((PAIRS, 2, 2 * half_a, 2 * LANES), bf16),
            pltpu.VMEM((PAIRS, 2 * half_a, 2 * LANES), bf16),
            pltpu.VMEM((pairs, span, wide), f32),
            pltpu.VMEM((chunks + 1, chunk, wide), f32),
            pltpu.VMEM((LANES, wide), f32), pltpu.VMEM((wide, LANES), bf16), pltpu.VMEM((wide, LANES), bf16),
            pltpu.VMEM((LANES, wide), bf16), pltpu.VMEM((chunk, LANES), f32),
            pltpu.VMEM((gens + chunk, chans), f32),
        ]
        + sums
        + [
            pltpu.VMEM((side, 2 * chunk, LANES), f32),
            pltpu.VMEM((count_gen, 1, chans), f32),
            dma((2, HALO)), dma((2, HALO)),
            dma((2, HALO, count_ch)), dma((2, HALO, count_ch)),
            dma((2,)), dma((2,)),
            dma((1, count_gen)), dma((1, count_gen)), dma((1, count_gen)), dma((1, count_gen)),
            dma((count_gen,)), dma((count_gen,)),
            dma((side,)), dma((side,)), dma((count_gen,)), dma((count_gen,)),
        ],
        compiler_params=pltpu.CompilerParams(
            collective_id=1, has_side_effects=True, vmem_limit_bytes=ROOM
        ),
    )(*[pltpu.with_memory_space_constraint(one, pltpu.HBM) for one in args])


def final_kernel(*refs):
    half = len(refs) // 2
    sources, targets, sem = refs[:half], refs[half : 2 * half], refs[-1]
    gens, parts = sources[0].shape[0], 4
    copies = []
    for k in range(parts):
        where = pl.ds(k * (gens // parts), gens // parts)
        copies.append(pltpu.make_async_copy(sources[0].at[where], targets[0].at[where], sem.at[k]))
    for k, (source, target) in enumerate(zip(sources[1:], targets[1:])):
        copies.append(pltpu.make_async_copy(source, target, sem.at[parts + k]))
    for copy in copies:
        copy.start()
    for copy in copies:
        copy.wait()


def final_call(*arrays):
    return pl.pallas_call(
        final_kernel,
        in_specs=[pl.BlockSpec(memory_space=pltpu.VMEM)] * len(arrays),
        out_specs=[pl.BlockSpec(memory_space=pltpu.HBM)] * len(arrays),
        out_shape=[jax.ShapeDtypeStruct(one.shape, one.dtype) for one in arrays],
        scratch_shapes=[pltpu.SemaphoreType.DMA((3 + len(arrays),))],
        compiler_params=pltpu.CompilerParams(vmem_limit_bytes=1 << 20),
    )(*arrays)


def on_device(
    shape, x_center, x_gens, w_expand, b_expand, w_depth, b_depth, w_reduce, b_reduce, w_excite, b_excite
):
    gens, rows, cols, c_in = x_gens.shape
    chans = w_expand.shape[1]
    taps = w_depth.shape[0]
    margin = taps // 2
    pairs, span = rows // margin, margin * cols
    x = x_gens.reshape(gens, pairs, span, c_in)
    xc = x_center.reshape(pairs, span, c_in)
    made = main_call(
        shape, taps, cols, x, xc, w_expand, b_expand, w_depth, b_depth,
        w_reduce.T, b_reduce, w_excite, b_excite,
    )
    out_gens, out_center, out_box = final_call(*made)
    image = (rows, cols, chans)
    return out_center.reshape(image), out_gens.reshape((gens,) + image), out_box.reshape(image)


def solution(mesh):
    in_specs = (
        P(("grp", "row"), None, None),
        P(("grp", "gen"), "row", None, None),
        P(None, "ch"),
        P("ch"),
        P(None, None, "ch"),
        P("ch"),
        P(),
        P(),
        P(None, "ch"),
        P("ch"),
    )
    out_specs = (
        P(("grp", "row"), None, "ch"),
        P(("grp", "gen"), "row", None, "ch"),
        P(("grp", "row"), None, "ch"),
    )
    return jax.shard_map(
        functools.partial(on_device, dict(mesh.shape)), mesh=mesh, in_specs=in_specs, out_specs=out_specs, check_vma=False
    )
```

```python
import functools

import jax
import jax.numpy as jnp
import ml_dtypes
import numpy as np
from jax import lax
from jax.experimental import pallas as pl
from jax.experimental.pallas import tpu as pltpu
from jax.sharding import PartitionSpec as P

MESH = pl.DeviceIdType.MESH
LANES = 128
PAIRS = 8
CHUNK = 8
GROUP = 32
ROOM = 40 << 20
OUTS = 3
HELD = 16
HALO = 2


def dot(a, b):
    return jnp.dot(a, b, preferred_element_type=jnp.float32)


def split(values):
    high = values.astype(ml_dtypes.bfloat16)
    return high, (values - high.astype(np.float64)).astype(ml_dtypes.bfloat16)


def transforms(rows, cols, taps):
    m = taps // 2
    n_r, n_c = rows + 2 * m, cols + m
    count = n_r * n_c
    r_in, c_in = np.arange(n_r)[:, None], np.arange(cols)[None, :]
    r_out = np.arange(rows)[:, None]
    tap_r, tap_c = np.arange(taps)[:, None], np.arange(taps)[None, :] - m

    def angle(freq, r, c):
        return (2 * np.pi * (freq[0] * r / n_r + freq[1] * c / n_c)).ravel()

    seen, double, single = set(), [], []
    for freq in [(u, v) for u in range(n_r) for v in range(n_c)]:
        twin = (-freq[0] % n_r, -freq[1] % n_c)
        if freq not in seen:
            (single if twin == freq else double).append(freq)
        seen |= {freq, twin}
    blocks = [[], [], [], [], [], [], [], []]
    for freq in double:
        a, t, o = angle(freq, r_in, c_in), angle(freq, tap_r, tap_c), angle(freq, r_out, c_in)
        entry = (
            np.cos(a), -np.sin(a), np.cos(t), np.sin(t), np.sin(t), np.cos(t),
            2 * np.cos(o) / count, -2 * np.sin(o) / count,
        )
        for block, part in zip(blocks, entry):
            block.append(part)
    single += [None] * (len(single) % 2)
    for one, two in zip(single[::2], single[1::2]):
        def wave(freq, r, c):
            scale = 0.0 if freq is None else 1.0
            return scale * np.cos(angle(freq or (0, 0), r, c))

        entry = (
            wave(one, r_in, c_in), wave(two, r_in, c_in),
            wave(one, tap_r, tap_c), 0 * wave(one, tap_r, tap_c),
            0 * wave(one, tap_r, tap_c), wave(two, tap_r, tap_c),
            wave(one, r_out, c_in) / count, wave(two, r_out, c_in) / count,
        )
        for block, part in zip(blocks, entry):
            block.append(part)
    half = -(-len(blocks[0]) // 8) * 8
    blocks = [np.pad(np.array(b), ((0, half - len(b)), (0, 0))) for b in blocks]
    def alternate(one, two):
        shape = (half // 8, 8, -1)
        return np.stack([one.reshape(shape), two.reshape(shape)], axis=1).reshape(2 * half, -1)

    forward = alternate(blocks[0], blocks[1])
    inverse = alternate(blocks[6], blocks[7]).T
    waves = np.concatenate(blocks[2:6], axis=0)
    high, low = split(waves)
    step = -(-taps * taps // 8) * 8
    tap_waves = np.zeros((4 * half, 4 * step), ml_dtypes.bfloat16)
    for slot, part in enumerate((high, high, low)):
        tap_waves[:, slot * step : slot * step + taps * taps] = part
    return forward.astype(ml_dtypes.bfloat16), inverse.astype(ml_dtypes.bfloat16), tap_waves, half, step


def windows(rows, cols, taps, depth):
    m = taps // 2
    tap_r, tap_c = np.divmod(np.arange(taps * taps)[:, None], taps)
    row, col = np.divmod(np.arange(rows * cols)[None, :], cols)
    inside = (col - tap_c + m >= 0) & (col - tap_c + m < cols)
    masks = np.zeros((3, depth, rows * cols), ml_dtypes.bfloat16)
    masks[0, : taps * taps] = inside
    masks[1, : taps * taps] = inside & (row - tap_r + m < 0)
    masks[2, : taps * taps] = inside & (row - tap_r + m >= rows)
    return masks


def relax_gate(ex_center, gate_radius):
    low_end = ex_center - gate_radius
    high_end = ex_center + gate_radius
    sig_low = jax.nn.sigmoid(low_end)
    sig_high = jax.nn.sigmoid(high_end)
    slope_val = jnp.minimum(sig_low * (1.0 - sig_low), sig_high * (1.0 - sig_high))
    gate_center = slope_val * ex_center + 0.5 * (
        sig_high + sig_low - slope_val * (high_end + low_end)
    )
    spread_term = 0.5 * (sig_high - sig_low - slope_val * (high_end - low_end))
    return (gate_center, slope_val, spread_term)


def main_kernel(mesh, plans, chunk, x_hbm, *refs):
    main_body(
        mesh, plans, chunk, x_hbm, refs[:HELD], refs[HELD : HELD + OUTS],
        refs[HELD + OUTS : 2 * HELD + OUTS], *refs[2 * HELD + OUTS :],
    )


def main_body(
    mesh, plans, chunk, x_hbm, sources, outs, locals_,
    oc_ref, ob_ref, dwg_ref, dwc_ref, gates_ref, stats_ref, g_sem, o_sem, xs, l_sem, x_sem,
    xall, xcs, xcp, sums, taps_f, og_ref, wf, wz, w2, spec_a, spec_b, xf_s, y1_s, y2_s,
    rad, pool, own_wr, wr_high, wr_low, we_three, br_wide, ex,
    send_a, recv_a, full_a, recv_b, squeeze, gate,
    h_send, h_recv, f_send, f_recv, c_send, c_recv,
    rs_send, rs_recv, ag_send, ag_recv, bc_send, bc_recv, sq_send, sq_recv, gt_send, gt_recv,
):
    (
        xc_ref, fwd_a, inv_a, tw_a, fwd_b, inv_b, tw_b, mask_ref,
        w_ref, b_ref, wd_ref, bd_ref, wr_ref, br_ref, we_ref, be_ref,
    ) = locals_
    count_gen, count_row, count_ch = mesh["gen"], mesh["row"], mesh["ch"]
    my_gen = lax.axis_index("gen")
    my_row = lax.axis_index("row")
    my_ch = lax.axis_index("ch")
    has_up = my_row > 0
    has_down = my_row < count_row - 1
    last = jnp.logical_and(has_up, jnp.logical_not(has_down))
    inner = jnp.logical_and(has_up, has_down)
    flip = jnp.where(last, 1, 0)
    gens, pairs, span, chans = dwg_ref.shape
    c_in = w_ref.shape[0]
    taps = wd_ref.shape[0]
    wide = wz.shape[1]
    main = wide - LANES
    chunks = gens // chunk
    all_cells = pairs * span * count_row
    sub = gens // (HALO * count_ch)

    def remote(src, dst, send_sem, recv_sem, place):
        return pltpu.make_async_remote_copy(
            src_ref=src, dst_ref=dst, send_sem=send_sem, recv_sem=recv_sem,
            device_id=place, device_id_type=MESH,
        )

    gen_peers = [(off, {"gen": lax.rem(my_gen + off, count_gen)}) for off in range(1, count_gen)]
    side_peers = []
    for off_row in range(count_row):
        for off_ch in range(count_ch):
            if off_row or off_ch:
                place = {
                    "row": lax.rem(my_row + off_row, count_row),
                    "ch": lax.rem(my_ch + off_ch, count_ch),
                }
                side_peers.append((off_row * count_ch + off_ch, place))
    barrier = pltpu.get_barrier_semaphore()
    for _, place in gen_peers + side_peers:
        pl.semaphore_signal(barrier, inc=1, device_id=place, device_id_type=MESH)

    loads = [
        pltpu.make_async_copy(source, target, l_sem.at[k])
        for k, (source, target) in enumerate(zip(sources, locals_))
    ]
    for load in loads:
        load.start()
    x_loads = [
        pltpu.make_async_copy(x_hbm.at[:, row], xs.at[1 + row], x_sem.at[row]) for row in range(pairs)
    ]
    for load in x_loads:
        load.start()
    pl.semaphore_wait(barrier, len(gen_peers) + len(side_peers))

    row_place = (
        {"row": lax.rem(my_row + 1, count_row)},
        {"row": lax.rem(my_row + count_row - 1, count_row)},
    )
    edge = (pairs - 1, 0)
    place_of = (0, pairs + 1)

    def halo_copy(side, n):
        where = pl.ds((n * count_ch + my_ch) * sub, sub)
        return remote(
            x_hbm.at[where, edge[side]], xs.at[place_of[side], where],
            h_send.at[side, n], h_recv.at[side, n], row_place[side],
        )

    def center_copy(side):
        return remote(
            sources[0].at[edge[side]], xcs.at[side], c_send.at[side], c_recv.at[side], row_place[side]
        )

    def forwards(side, n):
        where = xs.at[place_of[side], pl.ds((n * count_ch + my_ch) * sub, sub)]
        return [
            remote(
                where, where, f_send.at[side, n, off], f_recv.at[side, n, off],
                {"ch": lax.rem(my_ch + off, count_ch)},
            )
            for off in range(1, count_ch)
        ]

    for side, leaves in ((0, has_down), (1, has_up)):
        @pl.when(leaves)
        def _(side=side):
            center_copy(side).start()
            for n in range(HALO):
                halo_copy(side, n).start()

    def pass_on(side, n):
        halo_copy(side, n).wait_recv()
        for copy in forwards(side, n):
            copy.start()

    def passed_on(side):
        center_copy(side).wait_recv()
        for n in range(HALO):
            for copy in forwards(side, n):
                copy.wait_recv()

    def late(action):
        @pl.when(last)
        def _():
            action(0)

        @pl.when(has_down)
        def _():
            action(1)

    mine = my_row * count_ch + my_ch
    sq_copies = [
        remote(squeeze.at[mine], squeeze.at[mine], sq_send.at[off], sq_recv.at[off], place)
        for off, place in side_peers
    ]
    gt_copies = [
        remote(gate.at[my_gen], gate.at[my_gen], gt_send.at[off], gt_recv.at[off], place)
        for off, place in gen_peers
    ]

    def send_squeeze():
        pooled = pool[...].reshape(gens + chunk, wide) * (1.0 / all_cells)
        high = pooled.astype(jnp.bfloat16)
        low = (pooled - high.astype(jnp.float32)).astype(jnp.bfloat16)
        part = dot(high, wr_high[...]) + (dot(low, wr_high[...]) + dot(high, wr_low[...]))
        packed = part[:chunk]
        for n in range(1, chunks):
            packed = packed + pltpu.roll(part[n * chunk : (n + 1) * chunk], n * GROUP, 1)
        squeeze[mine, :chunk] = packed
        squeeze[mine, chunk:] = part[gens:]
        for copy in sq_copies:
            copy.start()

    def send_gate():
        for copy in sq_copies:
            copy.wait()
        total = squeeze[0]
        for slot in range(1, count_row * count_ch):
            total = total + squeeze[slot]
        spread = [total[:chunk]]
        spread += [pltpu.roll(total[:chunk], LANES - n * GROUP, 1) for n in range(1, chunks)]
        spread.append(total[chunk:] + br_wide[...])
        total = jnp.concatenate(spread, axis=0)
        total = jnp.where(lax.broadcasted_iota(jnp.int32, total.shape, 1) < GROUP, total, 0.0)
        high = total.astype(jnp.bfloat16).astype(jnp.float32)
        three = high + pltpu.roll(total - high, GROUP, 1) + pltpu.roll(high, 2 * GROUP, 1)
        ex_all = dot(three.astype(jnp.bfloat16), we_three[...])
        ex[...] = ex_all[:, :chans]
        ex_gens = ex[:gens]
        gate[my_gen] = jnp.sum(jnp.abs(ex_gens), axis=0, keepdims=True)
        for copy in gt_copies:
            copy.start()

    def finish_gate():
        for copy in gt_copies:
            copy.wait()
        gate_radius = gate[0]
        for slot in range(1, count_gen):
            gate_radius = gate_radius + gate[slot]
        ex_center = ex[gens : gens + 1] + be_ref[...][None, :]
        gate_center, slope_val, spread_term = relax_gate(ex_center, gate_radius)
        gates_ref[...] = (slope_val * ex[:gens])[:, None, :]
        stats_ref[0:1] = gate_center
        stats_ref[1:2] = spread_term
        stats_ref[2:3] = slope_val * gate_radius + spread_term

    for load in loads:
        load.wait()
    wf[...] = jnp.zeros_like(wf)
    wf[:c_in, :chans] = w_ref[...].astype(jnp.float32)
    bias = b_ref[...][None, :]
    bias_high = bias.astype(jnp.bfloat16).astype(jnp.float32)
    wf[c_in : c_in + 1, :chans] = bias_high
    wf[c_in + 1 : c_in + 2, :chans] = bias - bias_high
    wz[...] = wf[...].astype(jnp.bfloat16)
    w2[...] = jnp.zeros_like(w2)
    w2[:LANES, :LANES] = wz[:, main:]
    w2[LANES:, LANES:] = wz[:, main:]
    wf[...] = jnp.zeros_like(wf)
    taps_f[...] = jnp.zeros_like(taps_f)
    step = plans[0][1]
    for row in range(taps):
        one = wd_ref[row]
        taps_f[row * taps : (row + 1) * taps, :chans] = one
        high = one.astype(jnp.bfloat16).astype(jnp.float32)
        for slot, part in enumerate((high, one - high, high)):
            start = slot * step + row * taps
            wf[start : start + taps, :chans] = part
    wtap = wf[...].astype(jnp.bfloat16)
    spec_a[...] = dot(tw_a[...], wtap).reshape(spec_a.shape)
    spec_b[...] = dot(tw_b[...], wtap).reshape(spec_b.shape)
    ones = jnp.where(
        lax.broadcasted_iota(jnp.int32, (span, LANES - c_in), 1) < 2, 1.0, 0.0
    ).astype(jnp.bfloat16)
    xcp[...] = jnp.zeros_like(xcp)
    xcp[1 : 1 + pairs, :, :c_in] = xc_ref[...]
    for row in range(pairs):
        xcp[1 + row, :, c_in:] = ones
    xall[...] = jnp.zeros_like(xall)
    rad[...] = jnp.zeros_like(rad)
    own = wr_ref[:, :chans]
    for other in range(1, count_ch):
        own = jnp.where(my_ch == other, wr_ref[:, other * chans : (other + 1) * chans], own)
    units = own.shape[0]
    own_wr[...] = jnp.zeros_like(own_wr)
    own_wr[:units, :chans] = own
    turned = own_wr[...].T
    turned_high = turned.astype(jnp.bfloat16)
    wr_high[...] = turned_high
    wr_low[...] = (turned - turned_high.astype(jnp.float32)).astype(jnp.bfloat16)
    own_wr[...] = jnp.zeros_like(own_wr)
    we_high = we_ref[...].astype(jnp.bfloat16).astype(jnp.float32)
    own_wr[:units, :chans] = we_high
    own_wr[GROUP : GROUP + units, :chans] = we_high
    own_wr[2 * GROUP : 2 * GROUP + units, :chans] = we_ref[...] - we_high
    we_three[...] = own_wr[...].astype(jnp.bfloat16)
    br_wide[...] = jnp.zeros_like(br_wide)
    br_wide[0:1, :units] = br_ref[...][None, :]

    def fill(row):
        for g in range(gens):
            lane = slice(LANES * (g % 2), LANES * (g % 2) + c_in)
            xall[g // 2, row * span : (row + 1) * span, lane] = xs[row, g]

    def take(side):
        xcp[place_of[side], :, :c_in] = xcs[side]
        xcp[place_of[side], :, c_in:] = ones
        fill(place_of[side])

    @pl.when(inner)
    def _():
        for n in range(HALO):
            pass_on(0, n)
        passed_on(0)
        take(0)

    for row, load in enumerate(x_loads):
        load.wait()
        fill(1 + row)

    above = jnp.where(has_up, 0.0, 1.0)
    below = jnp.where(has_down, 0.0, 1.0)
    window = (
        mask_ref[0].astype(jnp.float32)
        - above * mask_ref[1].astype(jnp.float32)
        - below * mask_ref[2].astype(jnp.float32)
    ).astype(jnp.bfloat16)
    body = slice(span, (1 + pairs) * span)
    deep = window.shape[0]
    for q in range(gens // 2):
        both = dot(window, xall[q, body]).astype(jnp.bfloat16)
        sums[2 * q] = both[:, :LANES]
        sums[2 * q + 1] = both[:, LANES:]
    sums[gens] = dot(window, xcp[1 : 1 + pairs].reshape(pairs * span, LANES)).astype(jnp.bfloat16)
    for n in range(chunks):
        block = dot(sums[n * chunk : (n + 1) * chunk].reshape(chunk * deep, LANES), wz[...])
        pool[n] = jnp.sum(block.reshape(chunk, deep, wide) * taps_f[...], axis=1)
    pool[chunks] = jnp.zeros((chunk, wide), jnp.float32)
    pool[chunks, 0:1] = jnp.sum(dot(sums[gens], wz[...]) * taps_f[...], axis=0, keepdims=True)
    pool[chunks, 0:1, :chans] += (pairs * span) * bd_ref[...][None, :]
    send_squeeze()

    parts = (
        (fwd_a, inv_a, spec_a, flip, flip, 0) + plans[0],
        (fwd_b, inv_b, spec_b, (pairs - 1) * (1 - flip), (pairs - 1) * (1 - flip), pairs - 1) + plans[1],
    )

    def mix(e, spec, lane, half):
        count, width = e.shape[0] // (2 * half), e.shape[1]
        e = e.reshape(count, half // 8, 2, 8, width)
        a, b, c, d = [spec[k, :, lane].reshape(1, half // 8, 8, width) for k in range(4)]
        re, im = e[:, :, 0], e[:, :, 1]
        y = jnp.stack([re * a - im * b, re * c + im * d], axis=2)
        return y.reshape(count * 2 * half, width).astype(jnp.bfloat16)

    def compute(part, start, count):
        fwd, inv, spec, first, out, slot, half, _, made = part
        depth = fwd.shape[1]
        size = 2 * half
        cells = made * span
        rows = pl.ds(pl.multiple_of(first * span, span), depth)
        where = slice(slot, slot + made)
        for u in range(count):
            xf = dot(fwd[...], xall[start + u, rows]).astype(jnp.bfloat16)
            xf_s[2 * u * size : (2 * u + 1) * size] = xf[:, :LANES]
            xf_s[(2 * u + 1) * size : (2 * u + 2) * size] = xf[:, LANES:]
        for u in range(count):
            both = xf_s[2 * u * size : (2 * u + 2) * size]
            y1_s[u, : 2 * size] = mix(dot(both, wz[:, :main]), spec, slice(0, main), half)
            e2 = dot(jnp.concatenate([both[:size], both[size:]], axis=1), w2[...])
            for k in range(2):
                lane = slice(LANES * k, LANES * (k + 1))
                y2_s[u, :size, lane] = mix(e2[:, lane], spec, slice(main, wide), half)
        total = None
        for u in range(count):
            for k in range(2):
                g = 2 * (start + u) + k
                t = dot(inv[...], y1_s[u, k * size : (k + 1) * size])
                for row in range(made):
                    dwg_ref[g, out + row, :, :main] = t[row * span : (row + 1) * span].astype(jnp.bfloat16)
                total = jnp.abs(t) if total is None else total + jnp.abs(t)
        rad[where, :, :main] += total.reshape(made, span, main)
        total = None
        for u in range(count):
            t = dot(inv[...], y2_s[u, :size])
            for k in range(2):
                g = 2 * (start + u) + k
                mine = t[:, LANES * k : LANES * (k + 1)]
                for row in range(made):
                    dwg_ref[g, out + row, :, main:] = mine[
                        row * span : (row + 1) * span, : chans - main
                    ].astype(jnp.bfloat16)
                total = jnp.abs(mine) if total is None else total + jnp.abs(mine)
        rad[where, :, main:] += total.reshape(made, span, LANES)

    def center(part):
        fwd, inv, spec, first, out, _, half, _, made = part
        depth = fwd.shape[1]
        cells = made * span
        both = xcp[pl.ds(first, depth // span)].reshape(depth, LANES)
        xf = dot(fwd[...], both).astype(jnp.bfloat16)
        y = mix(dot(xf, wz[...]), spec, slice(0, wide), half)
        t = dot(inv[...], y)
        bias = bd_ref[...][None, :]
        for row in range(made):
            dwc_ref[out + row] = t[row * span : (row + 1) * span, :chans] + bias

    def done_copy(n):
        where = pl.ds(n * chunk, chunk)
        return pltpu.make_async_copy(og_ref.at[where], outs[0].at[where], g_sem.at[n])

    results = [
        pltpu.make_async_copy(source, target, o_sem.at[k])
        for k, (source, target) in enumerate(
            zip((oc_ref, ob_ref), outs[1:])
        )
    ]

    half_way = gens // 4
    compute(parts[0], 0, half_way)
    compute(parts[0], half_way, half_way // 2)
    send_gate()
    for n in range(HALO):
        late(lambda side: pass_on(side, n))
    compute(parts[0], half_way + half_way // 2, half_way // 2)

    radii = ((send_a, recv_a, full_a),)

    def reduce_copies(which):
        send, recv, _ = radii[which]
        per = recv.shape[1]
        return [
            remote(
                send.at[pl.ds(place["gen"] * per, per)], recv.at[my_gen],
                rs_send.at[which, off], rs_recv.at[which, off], place,
            )
            for off, place in gen_peers
        ]

    def gather_copies(which):
        full, per = radii[which][2], radii[which][1].shape[1]
        mine = full.at[pl.ds(my_gen * per, per)]
        return [
            remote(mine, mine, ag_send.at[which, off], ag_recv.at[which, off], place)
            for off, place in gen_peers
        ]

    def reduce_start(which):
        send, recv, _ = radii[which]
        per = recv.shape[1]
        _, _, _, _, _, slot, _, _, made = parts[which]
        tiles = made * span // 8
        send[:tiles] = rad[slot : slot + made].reshape(tiles, 8, wide).astype(jnp.bfloat16)
        if count_gen * per > tiles:
            send[tiles:] = jnp.zeros((count_gen * per - tiles, 8, wide), jnp.bfloat16)
        recv[my_gen] = send[pl.ds(my_gen * per, per)]
        for copy in reduce_copies(which):
            copy.start()

    def gather_start(which):
        _, recv, full = radii[which]
        per = recv.shape[1]
        for copy in reduce_copies(which):
            copy.wait()
        total = recv[0].astype(jnp.float32)
        for slot in range(1, count_gen):
            total = total + recv[slot].astype(jnp.float32)
        full[pl.ds(my_gen * per, per)] = total.astype(jnp.bfloat16)
        for copy in gather_copies(which):
            copy.start()

    reduce_start(0)

    center(parts[0])
    late(passed_on)
    late(take)
    center(parts[1])

    compute(parts[1], 0, half_way)
    compute(parts[1], half_way, half_way)

    _, _, _, _, last_out, slot, _, _, made = parts[1]
    recv_b[my_gen] = rad[slot].astype(jnp.bfloat16)
    bc_copies = [
        remote(recv_b.at[my_gen], recv_b.at[my_gen], bc_send.at[off], bc_recv.at[off], place)
        for off, place in gen_peers
    ]
    for copy in bc_copies:
        copy.start()
    gather_start(0)

    finish_gate()
    gate_center = stats_ref[0:1]

    def out_turn(n, _):
        for k in range(chunk):
            g = n * chunk + k
            og_ref[g] = (
                dwc_ref[...] * gates_ref[g] + gate_center * dwg_ref[g].astype(jnp.float32)
            ).astype(jnp.bfloat16)
        done_copy(n).start()
        return 0

    lax.fori_loop(0, chunks, out_turn, 0)
    oc_ref[...] = dwc_ref[...] * gate_center
    results[0].start()
    base = jnp.abs(dwc_ref[...]) * stats_ref[1:2]
    ob_ref[...] = base
    for copy in gather_copies(0):
        copy.wait()
    _, _, _, _, out, _, _, _, made = parts[0]
    whole = full_a[: made * span // 8].astype(jnp.float32).reshape(made, span, wide)
    for row in range(made):
        ob_ref[out + row] += whole[row, :, :chans] * stats_ref[2:3]
    for copy in bc_copies:
        copy.wait()
    total = recv_b[0].astype(jnp.float32)
    for slot in range(1, count_gen):
        total = total + recv_b[slot].astype(jnp.float32)
    ob_ref[last_out] += total[:, :chans] * stats_ref[2:3]
    results[1].start()

    for side, arrives, leaves in ((0, has_up, has_down), (1, has_down, has_up)):
        @pl.when(leaves)
        def _(side=side):
            center_copy(side).wait_send()
            for n in range(HALO):
                halo_copy(side, n).wait_send()

        @pl.when(arrives)
        def _(side=side):
            for n in range(HALO):
                for copy in forwards(side, n):
                    copy.wait_send()

    for n in range(chunks):
        done_copy(n).wait()
    for copy in results:
        copy.wait()


def main_call(mesh, taps, cols, x, xc, w_expand, b_expand, w_depth, b_depth, wr, br, we, be):
    gens, pairs, span, c_in = x.shape
    chans = w_expand.shape[1]
    chunk = CHUNK
    count_gen, count_row, count_ch = mesh["gen"], mesh["row"], mesh["ch"]
    wide = -(-chans // LANES) * LANES
    chunks = gens // chunk
    assert wide == 3 * LANES and gens % (HALO * count_ch) == 0 and gens == chunks * chunk
    assert we.shape[0] <= GROUP and chunks * GROUP <= LANES and gens == 4 * PAIRS
    plans, tables = [], []
    for made in (pairs - 1, 1):
        forward, inverse, tap_waves, half, step = transforms(made * span // cols, cols, taps)
        plans.append((half, step, made))
        tables += [jnp.asarray(forward), jnp.asarray(inverse), jnp.asarray(tap_waves)]
    half_a, half_b = plans[0][0], plans[1][0]
    hbm = pl.BlockSpec(memory_space=pltpu.HBM)
    dma = pltpu.SemaphoreType.DMA
    bf16, f32 = jnp.bfloat16, jnp.float32
    masks = jnp.asarray(windows(pairs * span // cols, cols, taps, plans[0][1]))
    args = [x, xc] + tables + [masks, w_expand, b_expand, w_depth, b_depth, wr, br, we, be]
    outs = [
        jax.ShapeDtypeStruct((gens, pairs, span, chans), bf16),
        jax.ShapeDtypeStruct((pairs, span, chans), f32),
        jax.ShapeDtypeStruct((pairs, span, chans), f32),
    ]
    held = [pltpu.VMEM(one.shape, one.dtype) for one in args[1:] + outs[1:]]
    held += [pltpu.VMEM(one.shape, one.dtype) for one in outs[:2]]
    held += [pltpu.VMEM((gens, 1, chans), f32), pltpu.VMEM((3, chans), f32)]
    per = -(-(plans[0][2] * span // 8) // count_gen)
    whole = pltpu.VMEM((count_gen * per, 8, wide), bf16)
    sums = [
        whole, pltpu.VMEM((count_gen, per, 8, wide), bf16), whole, pltpu.VMEM((count_gen, span, wide), bf16),
    ]
    side = count_row * count_ch
    step = plans[0][1]
    return pl.pallas_call(
        functools.partial(main_kernel, mesh, tuple(plans), chunk),
        in_specs=[hbm] * len(args),
        out_specs=[hbm] * OUTS,
        out_shape=outs,
        scratch_shapes=held
        + [
            dma((chunks,)), dma((OUTS - 1,)),
            pltpu.VMEM((pairs + 2, gens, span, c_in), bf16), dma((HELD,)), dma((pairs,)),
            pltpu.VMEM((gens // 2, (pairs + 2) * span, 2 * LANES), bf16),
            pltpu.VMEM((2, span, c_in), bf16),
            pltpu.VMEM((pairs + 2, span, LANES), bf16),
            pltpu.VMEM((gens + 1, step, LANES), bf16),
            pltpu.VMEM((step, wide), f32),
            pltpu.VMEM((gens, pairs, span, chans), bf16),
            pltpu.VMEM((LANES, wide), f32),
            pltpu.VMEM((LANES, wide), bf16),
            pltpu.VMEM((2 * LANES, 2 * LANES), bf16),
            pltpu.VMEM((4, half_a, wide), f32),
            pltpu.VMEM((4, half_b, wide), f32),
            pltpu.VMEM((PAIRS * 4 * half_a, LANES), bf16),
            pltpu.VMEM((PAIRS, 4 * half_a, 2 * LANES), bf16),
            pltpu.VMEM((PAIRS, 2 * half_a, 2 * LANES), bf16),
            pltpu.VMEM((pairs, span, wide), f32),
            pltpu.VMEM((chunks + 1, chunk, wide), f32),
            pltpu.VMEM((LANES, wide), f32), pltpu.VMEM((wide, LANES), bf16), pltpu.VMEM((wide, LANES), bf16),
            pltpu.VMEM((LANES, wide), bf16), pltpu.VMEM((chunk, LANES), f32),
            pltpu.VMEM((gens + chunk, chans), f32),
        ]
        + sums
        + [
            pltpu.VMEM((side, 2 * chunk, LANES), f32),
            pltpu.VMEM((count_gen, 1, chans), f32),
            dma((2, HALO)), dma((2, HALO)),
            dma((2, HALO, count_ch)), dma((2, HALO, count_ch)),
            dma((2,)), dma((2,)),
            dma((1, count_gen)), dma((1, count_gen)), dma((1, count_gen)), dma((1, count_gen)),
            dma((count_gen,)), dma((count_gen,)),
            dma((side,)), dma((side,)), dma((count_gen,)), dma((count_gen,)),
        ],
        compiler_params=pltpu.CompilerParams(
            collective_id=1, has_side_effects=True, vmem_limit_bytes=ROOM
        ),
    )(*[pltpu.with_memory_space_constraint(one, pltpu.HBM) for one in args])


def final_kernel(*refs):
    half = len(refs) // 2
    sources, targets, sem = refs[:half], refs[half : 2 * half], refs[-1]
    gens, parts = sources[0].shape[0], 4
    copies = []
    for k in range(parts):
        where = pl.ds(k * (gens // parts), gens // parts)
        copies.append(pltpu.make_async_copy(sources[0].at[where], targets[0].at[where], sem.at[k]))
    for k, (source, target) in enumerate(zip(sources[1:], targets[1:])):
        copies.append(pltpu.make_async_copy(source, target, sem.at[parts + k]))
    for copy in copies:
        copy.start()
    for copy in copies:
        copy.wait()


def final_call(*arrays):
    return pl.pallas_call(
        final_kernel,
        in_specs=[pl.BlockSpec(memory_space=pltpu.VMEM)] * len(arrays),
        out_specs=[pl.BlockSpec(memory_space=pltpu.HBM)] * len(arrays),
        out_shape=[jax.ShapeDtypeStruct(one.shape, one.dtype) for one in arrays],
        scratch_shapes=[pltpu.SemaphoreType.DMA((3 + len(arrays),))],
        compiler_params=pltpu.CompilerParams(vmem_limit_bytes=1 << 20),
    )(*arrays)


def on_device(
    shape, x_center, x_gens, w_expand, b_expand, w_depth, b_depth, w_reduce, b_reduce, w_excite, b_excite
):
    gens, rows, cols, c_in = x_gens.shape
    chans = w_expand.shape[1]
    taps = w_depth.shape[0]
    margin = taps // 2
    pairs, span = rows // margin, margin * cols
    x = x_gens.reshape(gens, pairs, span, c_in)
    xc = x_center.reshape(pairs, span, c_in)
    made = main_call(
        shape, taps, cols, x, xc, w_expand, b_expand, w_depth, b_depth,
        w_reduce.T, b_reduce, w_excite, b_excite,
    )
    out_gens, out_center, out_box = final_call(*made)
    image = (rows, cols, chans)
    return out_center.reshape(image), out_gens.reshape((gens,) + image), out_box.reshape(image)


def solution(mesh):
    in_specs = (
        P(("grp", "row"), None, None),
        P(("grp", "gen"), "row", None, None),
        P(None, "ch"),
        P("ch"),
        P(None, None, "ch"),
        P("ch"),
        P(),
        P(),
        P(None, "ch"),
        P("ch"),
    )
    out_specs = (
        P(("grp", "row"), None, "ch"),
        P(("grp", "gen"), "row", None, "ch"),
        P(("grp", "row"), None, "ch"),
    )
    return jax.shard_map(
        functools.partial(on_device, dict(mesh.shape)), mesh=mesh, in_specs=in_specs, out_specs=out_specs, check_vma=False
    )
```

```python
import functools

import jax
import jax.numpy as jnp
import ml_dtypes
import numpy as np
from jax import lax
from jax.experimental import pallas as pl
from jax.experimental.pallas import tpu as pltpu
from jax.sharding import PartitionSpec as P

MESH = pl.DeviceIdType.MESH
LANES = 128
PAIRS = 8
CHUNK = 8
GROUP = 32
ROOM = 40 << 20
OUTS = 3
HELD = 16


def dot(a, b):
    return jnp.dot(a, b, preferred_element_type=jnp.float32)


def split(values):
    high = values.astype(ml_dtypes.bfloat16)
    return high, (values - high.astype(np.float64)).astype(ml_dtypes.bfloat16)


def transforms(rows, cols, taps):
    m = taps // 2
    n_r, n_c = rows + 2 * m, cols + m
    count = n_r * n_c
    r_in, c_in = np.arange(n_r)[:, None], np.arange(cols)[None, :]
    r_out = np.arange(rows)[:, None]
    tap_r, tap_c = np.arange(taps)[:, None], np.arange(taps)[None, :] - m

    def angle(freq, r, c):
        return (2 * np.pi * (freq[0] * r / n_r + freq[1] * c / n_c)).ravel()

    seen, double, single = set(), [], []
    for freq in [(u, v) for u in range(n_r) for v in range(n_c)]:
        twin = (-freq[0] % n_r, -freq[1] % n_c)
        if freq not in seen:
            (single if twin == freq else double).append(freq)
        seen |= {freq, twin}
    blocks = [[], [], [], [], [], [], [], []]
    for freq in double:
        a, t, o = angle(freq, r_in, c_in), angle(freq, tap_r, tap_c), angle(freq, r_out, c_in)
        entry = (
            np.cos(a), -np.sin(a), np.cos(t), np.sin(t), np.sin(t), np.cos(t),
            2 * np.cos(o) / count, -2 * np.sin(o) / count,
        )
        for block, part in zip(blocks, entry):
            block.append(part)
    single += [None] * (len(single) % 2)
    for one, two in zip(single[::2], single[1::2]):
        def wave(freq, r, c):
            scale = 0.0 if freq is None else 1.0
            return scale * np.cos(angle(freq or (0, 0), r, c))

        entry = (
            wave(one, r_in, c_in), wave(two, r_in, c_in),
            wave(one, tap_r, tap_c), 0 * wave(one, tap_r, tap_c),
            0 * wave(one, tap_r, tap_c), wave(two, tap_r, tap_c),
            wave(one, r_out, c_in) / count, wave(two, r_out, c_in) / count,
        )
        for block, part in zip(blocks, entry):
            block.append(part)
    half = -(-len(blocks[0]) // 8) * 8
    blocks = [np.pad(np.array(b), ((0, half - len(b)), (0, 0))) for b in blocks]
    def alternate(one, two):
        shape = (half // 8, 8, -1)
        return np.stack([one.reshape(shape), two.reshape(shape)], axis=1).reshape(2 * half, -1)

    forward = alternate(blocks[0], blocks[1])
    inverse = alternate(blocks[6], blocks[7]).T
    waves = np.concatenate(blocks[2:6], axis=0)
    high, low = split(waves)
    step = -(-taps * taps // 8) * 8
    tap_waves = np.zeros((4 * half, 4 * step), ml_dtypes.bfloat16)
    for slot, part in enumerate((high, high, low)):
        tap_waves[:, slot * step : slot * step + taps * taps] = part
    return forward.astype(ml_dtypes.bfloat16), inverse.astype(ml_dtypes.bfloat16), tap_waves, half, step


def windows(rows, cols, taps, depth):
    m = taps // 2
    tap_r, tap_c = np.divmod(np.arange(taps * taps)[:, None], taps)
    row, col = np.divmod(np.arange(rows * cols)[None, :], cols)
    inside = (col - tap_c + m >= 0) & (col - tap_c + m < cols)
    masks = np.zeros((3, depth, rows * cols), ml_dtypes.bfloat16)
    masks[0, : taps * taps] = inside
    masks[1, : taps * taps] = inside & (row - tap_r + m < 0)
    masks[2, : taps * taps] = inside & (row - tap_r + m >= rows)
    return masks


def relax_gate(ex_center, gate_radius):
    low_end = ex_center - gate_radius
    high_end = ex_center + gate_radius
    sig_low = jax.nn.sigmoid(low_end)
    sig_high = jax.nn.sigmoid(high_end)
    slope_val = jnp.minimum(sig_low * (1.0 - sig_low), sig_high * (1.0 - sig_high))
    gate_center = slope_val * ex_center + 0.5 * (
        sig_high + sig_low - slope_val * (high_end + low_end)
    )
    spread_term = 0.5 * (sig_high - sig_low - slope_val * (high_end - low_end))
    return (gate_center, slope_val, spread_term)


def main_kernel(mesh, plans, chunk, x_hbm, *refs):
    main_body(
        mesh, plans, chunk, x_hbm, refs[:HELD], refs[HELD : HELD + OUTS],
        refs[HELD + OUTS : 2 * HELD + OUTS], *refs[2 * HELD + OUTS :],
    )


def main_body(
    mesh, plans, chunk, x_hbm, sources, outs, locals_,
    oc_ref, ob_ref, dwg_ref, dwc_ref, gates_ref, stats_ref, g_sem, o_sem, xs, l_sem, x_sem,
    xall, xcs, xcp, sums, taps_f, og_ref, wf, wz, w2, spec_a, spec_b, xf_s, y1_s, y2_s,
    rad, pool, own_wr, wr_high, wr_low, we_three, br_wide, ex,
    send_a, recv_a, full_a, recv_b, squeeze, gate,
    h_send, h_recv, f_send, f_recv, c_send, c_recv,
    rs_send, rs_recv, ag_send, ag_recv, bc_send, bc_recv, sq_send, sq_recv, gt_send, gt_recv,
):
    (
        xc_ref, fwd_a, inv_a, tw_a, fwd_b, inv_b, tw_b, mask_ref,
        w_ref, b_ref, wd_ref, bd_ref, wr_ref, br_ref, we_ref, be_ref,
    ) = locals_
    count_gen, count_row, count_ch = mesh["gen"], mesh["row"], mesh["ch"]
    my_gen = lax.axis_index("gen")
    my_row = lax.axis_index("row")
    my_ch = lax.axis_index("ch")
    has_up = my_row > 0
    has_down = my_row < count_row - 1
    last = jnp.logical_and(has_up, jnp.logical_not(has_down))
    inner = jnp.logical_and(has_up, has_down)
    flip = jnp.where(last, 1, 0)
    gens, pairs, span, chans = dwg_ref.shape
    c_in = w_ref.shape[0]
    taps = wd_ref.shape[0]
    wide = wz.shape[1]
    main = wide - LANES
    chunks = gens // chunk
    all_cells = pairs * span * count_row
    sub = gens // (2 * count_ch)

    def remote(src, dst, send_sem, recv_sem, place):
        return pltpu.make_async_remote_copy(
            src_ref=src, dst_ref=dst, send_sem=send_sem, recv_sem=recv_sem,
            device_id=place, device_id_type=MESH,
        )

    gen_peers = [(off, {"gen": lax.rem(my_gen + off, count_gen)}) for off in range(1, count_gen)]
    side_peers = []
    for off_row in range(count_row):
        for off_ch in range(count_ch):
            if off_row or off_ch:
                place = {
                    "row": lax.rem(my_row + off_row, count_row),
                    "ch": lax.rem(my_ch + off_ch, count_ch),
                }
                side_peers.append((off_row * count_ch + off_ch, place))
    barrier = pltpu.get_barrier_semaphore()
    for _, place in gen_peers + side_peers:
        pl.semaphore_signal(barrier, inc=1, device_id=place, device_id_type=MESH)

    x_loads = [
        pltpu.make_async_copy(x_hbm.at[:, row], xs.at[row], x_sem.at[row]) for row in range(pairs)
    ]
    for row in (0, pairs - 1) + tuple(range(1, pairs - 1)):
        x_loads[row].start()
    loads = [
        pltpu.make_async_copy(source, target, l_sem.at[k])
        for k, (source, target) in enumerate(zip(sources, locals_))
    ]
    for load in loads:
        load.start()
    own_rows = slice(span, (1 + pairs) * span)
    for k in range(2):
        pad = slice(LANES * k + c_in, LANES * (k + 1))
        xall[:, own_rows, pad] = jnp.zeros((gens // 2, pairs * span, LANES - c_in), jnp.bfloat16)
    for place, arrives in ((0, has_up), (pairs + 1, has_down)):
        @pl.when(jnp.logical_not(arrives))
        def _(place=place):
            xall[:, place * span : (place + 1) * span] = jnp.zeros(
                (gens // 2, span, 2 * LANES), jnp.bfloat16
            )

    def fill(row):
        x_loads[row].wait()
        for g in range(gens):
            lane = slice(LANES * (g % 2), LANES * (g % 2) + c_in)
            xall[g // 2, (1 + row) * span : (2 + row) * span, lane] = xs[row, g]

    fill(0)
    fill(pairs - 1)
    pl.semaphore_wait(barrier, len(gen_peers) + len(side_peers))

    row_place = (
        {"row": lax.rem(my_row + 1, count_row)},
        {"row": lax.rem(my_row + count_row - 1, count_row)},
    )
    edge = (pairs - 1, 0)
    place_of = (0, pairs + 1)

    def edge_of(row):
        return xall.at[pl.ds(my_ch * sub, sub), pl.ds(row * span, span)]

    def halo_copy(side):
        return remote(
            edge_of(1 + edge[side]), edge_of(place_of[side]),
            h_send.at[side], h_recv.at[side], row_place[side],
        )

    def center_copy(side):
        return remote(
            sources[0].at[edge[side]], xcs.at[side], c_send.at[side], c_recv.at[side], row_place[side]
        )

    def forwards(side):
        return [
            remote(
                edge_of(place_of[side]), edge_of(place_of[side]),
                f_send.at[side, off], f_recv.at[side, off],
                {"ch": lax.rem(my_ch + off, count_ch)},
            )
            for off in range(1, count_ch)
        ]

    for side, leaves in ((0, has_down), (1, has_up)):
        @pl.when(leaves)
        def _(side=side):
            halo_copy(side).start()
            center_copy(side).start()

    for row in range(1, pairs - 1):
        fill(row)

    def pass_on(side):
        halo_copy(side).wait_recv()
        for copy in forwards(side):
            copy.start()

    def passed_on(side):
        for copy in forwards(side):
            copy.wait_recv()

    def late(action):
        @pl.when(last)
        def _():
            action(0)

        @pl.when(has_down)
        def _():
            action(1)

    mine = my_row * count_ch + my_ch
    sq_copies = [
        remote(squeeze.at[mine], squeeze.at[mine], sq_send.at[off], sq_recv.at[off], place)
        for off, place in side_peers
    ]
    gt_copies = [
        remote(gate.at[my_gen], gate.at[my_gen], gt_send.at[off], gt_recv.at[off], place)
        for off, place in gen_peers
    ]

    def send_squeeze():
        pooled = pool[...].reshape(gens + chunk, wide) * (1.0 / all_cells)
        high = pooled.astype(jnp.bfloat16)
        low = (pooled - high.astype(jnp.float32)).astype(jnp.bfloat16)
        part = dot(high, wr_high[...]) + (dot(low, wr_high[...]) + dot(high, wr_low[...]))
        packed = part[:chunk]
        for n in range(1, chunks):
            packed = packed + pltpu.roll(part[n * chunk : (n + 1) * chunk], n * GROUP, 1)
        squeeze[mine, :chunk] = packed
        squeeze[mine, chunk:] = part[gens:]
        for copy in sq_copies:
            copy.start()

    def send_gate():
        for copy in sq_copies:
            copy.wait()
        total = squeeze[0]
        for slot in range(1, count_row * count_ch):
            total = total + squeeze[slot]
        spread = [total[:chunk]]
        spread += [pltpu.roll(total[:chunk], LANES - n * GROUP, 1) for n in range(1, chunks)]
        spread.append(total[chunk:] + br_wide[...])
        total = jnp.concatenate(spread, axis=0)
        total = jnp.where(lax.broadcasted_iota(jnp.int32, total.shape, 1) < GROUP, total, 0.0)
        high = total.astype(jnp.bfloat16).astype(jnp.float32)
        three = high + pltpu.roll(total - high, GROUP, 1) + pltpu.roll(high, 2 * GROUP, 1)
        ex_all = dot(three.astype(jnp.bfloat16), we_three[...])
        ex[...] = ex_all[:, :chans]
        ex_gens = ex[:gens]
        gate[my_gen] = jnp.sum(jnp.abs(ex_gens), axis=0, keepdims=True)
        for copy in gt_copies:
            copy.start()

    def finish_gate():
        for copy in gt_copies:
            copy.wait()
        gate_radius = gate[0]
        for slot in range(1, count_gen):
            gate_radius = gate_radius + gate[slot]
        ex_center = ex[gens : gens + 1] + be_ref[...][None, :]
        gate_center, slope_val, spread_term = relax_gate(ex_center, gate_radius)
        gates_ref[...] = (slope_val * ex[:gens])[:, None, :]
        stats_ref[0:1] = gate_center
        stats_ref[1:2] = spread_term
        stats_ref[2:3] = slope_val * gate_radius + spread_term

    for load in loads:
        load.wait()
    wf[...] = jnp.zeros_like(wf)
    wf[:c_in, :chans] = w_ref[...].astype(jnp.float32)
    bias = b_ref[...][None, :]
    bias_high = bias.astype(jnp.bfloat16).astype(jnp.float32)
    wf[c_in : c_in + 1, :chans] = bias_high
    wf[c_in + 1 : c_in + 2, :chans] = bias - bias_high
    wz[...] = wf[...].astype(jnp.bfloat16)
    w2[...] = jnp.zeros_like(w2)
    w2[:LANES, :LANES] = wz[:, main:]
    w2[LANES:, LANES:] = wz[:, main:]
    wf[...] = jnp.zeros_like(wf)
    taps_f[...] = jnp.zeros_like(taps_f)
    step = plans[0][1]
    for row in range(taps):
        one = wd_ref[row]
        taps_f[row * taps : (row + 1) * taps, :chans] = one
        high = one.astype(jnp.bfloat16).astype(jnp.float32)
        for slot, part in enumerate((high, one - high, high)):
            start = slot * step + row * taps
            wf[start : start + taps, :chans] = part
    wtap = wf[...].astype(jnp.bfloat16)
    spec_a[...] = dot(tw_a[...], wtap).reshape(spec_a.shape)
    spec_b[...] = dot(tw_b[...], wtap).reshape(spec_b.shape)
    ones = jnp.where(
        lax.broadcasted_iota(jnp.int32, (span, LANES - c_in), 1) < 2, 1.0, 0.0
    ).astype(jnp.bfloat16)
    xcp[...] = jnp.zeros_like(xcp)
    xcp[1 : 1 + pairs, :, :c_in] = xc_ref[...]
    for row in range(pairs):
        xcp[1 + row, :, c_in:] = ones
    rad[...] = jnp.zeros_like(rad)
    own = wr_ref[:, :chans]
    for other in range(1, count_ch):
        own = jnp.where(my_ch == other, wr_ref[:, other * chans : (other + 1) * chans], own)
    units = own.shape[0]
    own_wr[...] = jnp.zeros_like(own_wr)
    own_wr[:units, :chans] = own
    turned = own_wr[...].T
    turned_high = turned.astype(jnp.bfloat16)
    wr_high[...] = turned_high
    wr_low[...] = (turned - turned_high.astype(jnp.float32)).astype(jnp.bfloat16)
    own_wr[...] = jnp.zeros_like(own_wr)
    we_high = we_ref[...].astype(jnp.bfloat16).astype(jnp.float32)
    own_wr[:units, :chans] = we_high
    own_wr[GROUP : GROUP + units, :chans] = we_high
    own_wr[2 * GROUP : 2 * GROUP + units, :chans] = we_ref[...] - we_high
    we_three[...] = own_wr[...].astype(jnp.bfloat16)
    br_wide[...] = jnp.zeros_like(br_wide)
    br_wide[0:1, :units] = br_ref[...][None, :]

    def take(side):
        center_copy(side).wait_recv()
        xcp[place_of[side], :, :c_in] = xcs[side]
        xcp[place_of[side], :, c_in:] = ones

    @pl.when(inner)
    def _():
        pass_on(0)
        passed_on(0)
        take(0)

    above = jnp.where(has_up, 0.0, 1.0)
    below = jnp.where(has_down, 0.0, 1.0)
    window = (
        mask_ref[0].astype(jnp.float32)
        - above * mask_ref[1].astype(jnp.float32)
        - below * mask_ref[2].astype(jnp.float32)
    ).astype(jnp.bfloat16)
    deep = window.shape[0]
    for q in range(gens // 2):
        both = dot(window, xall[q, own_rows]).astype(jnp.bfloat16)
        sums[2 * q] = both[:, :LANES]
        sums[2 * q + 1] = both[:, LANES:]
    sums[gens] = dot(window, xcp[1 : 1 + pairs].reshape(pairs * span, LANES)).astype(jnp.bfloat16)
    for n in range(chunks):
        block = dot(sums[n * chunk : (n + 1) * chunk].reshape(chunk * deep, LANES), wz[...])
        pool[n] = jnp.sum(block.reshape(chunk, deep, wide) * taps_f[...], axis=1)
    pool[chunks] = jnp.zeros((chunk, wide), jnp.float32)
    pool[chunks, 0:1] = jnp.sum(dot(sums[gens], wz[...]) * taps_f[...], axis=0, keepdims=True)
    pool[chunks, 0:1, :chans] += (pairs * span) * bd_ref[...][None, :]
    send_squeeze()

    parts = (
        (fwd_a, inv_a, spec_a, flip, flip, 0) + plans[0],
        (fwd_b, inv_b, spec_b, (pairs - 1) * (1 - flip), (pairs - 1) * (1 - flip), pairs - 1) + plans[1],
    )

    def mix(e, spec, lane, half):
        count, width = e.shape[0] // (2 * half), e.shape[1]
        e = e.reshape(count, half // 8, 2, 8, width)
        a, b, c, d = [spec[k, :, lane].reshape(1, half // 8, 8, width) for k in range(4)]
        re, im = e[:, :, 0], e[:, :, 1]
        y = jnp.stack([re * a - im * b, re * c + im * d], axis=2)
        return y.reshape(count * 2 * half, width).astype(jnp.bfloat16)

    def compute(part, start, count):
        fwd, inv, spec, first, out, slot, half, _, made = part
        depth = fwd.shape[1]
        size = 2 * half
        cells = made * span
        rows = pl.ds(pl.multiple_of(first * span, span), depth)
        where = slice(slot, slot + made)
        for u in range(count):
            xf = dot(fwd[...], xall[start + u, rows]).astype(jnp.bfloat16)
            xf_s[2 * u * size : (2 * u + 1) * size] = xf[:, :LANES]
            xf_s[(2 * u + 1) * size : (2 * u + 2) * size] = xf[:, LANES:]
        for u in range(count):
            both = xf_s[2 * u * size : (2 * u + 2) * size]
            y1_s[u, : 2 * size] = mix(dot(both, wz[:, :main]), spec, slice(0, main), half)
            e2 = dot(jnp.concatenate([both[:size], both[size:]], axis=1), w2[...])
            for k in range(2):
                lane = slice(LANES * k, LANES * (k + 1))
                y2_s[u, :size, lane] = mix(e2[:, lane], spec, slice(main, wide), half)
        total = None
        for u in range(count):
            for k in range(2):
                g = 2 * (start + u) + k
                t = dot(inv[...], y1_s[u, k * size : (k + 1) * size])
                for row in range(made):
                    dwg_ref[g, out + row, :, :main] = t[row * span : (row + 1) * span].astype(jnp.bfloat16)
                total = jnp.abs(t) if total is None else total + jnp.abs(t)
        rad[where, :, :main] += total.reshape(made, span, main)
        total = None
        for u in range(count):
            t = dot(inv[...], y2_s[u, :size])
            for k in range(2):
                g = 2 * (start + u) + k
                mine = t[:, LANES * k : LANES * (k + 1)]
                for row in range(made):
                    dwg_ref[g, out + row, :, main:] = mine[
                        row * span : (row + 1) * span, : chans - main
                    ].astype(jnp.bfloat16)
                total = jnp.abs(mine) if total is None else total + jnp.abs(mine)
        rad[where, :, main:] += total.reshape(made, span, LANES)

    def center(part):
        fwd, inv, spec, first, out, _, half, _, made = part
        depth = fwd.shape[1]
        cells = made * span
        both = xcp[pl.ds(first, depth // span)].reshape(depth, LANES)
        xf = dot(fwd[...], both).astype(jnp.bfloat16)
        y = mix(dot(xf, wz[...]), spec, slice(0, wide), half)
        t = dot(inv[...], y)
        bias = bd_ref[...][None, :]
        for row in range(made):
            dwc_ref[out + row] = t[row * span : (row + 1) * span, :chans] + bias

    def done_copy(n):
        where = pl.ds(n * chunk, chunk)
        return pltpu.make_async_copy(og_ref.at[where], outs[0].at[where], g_sem.at[n])

    results = [
        pltpu.make_async_copy(source, target, o_sem.at[k])
        for k, (source, target) in enumerate(
            zip((oc_ref, ob_ref), outs[1:])
        )
    ]

    for start in range(0, gens // 2, PAIRS):
        compute(parts[0], start, PAIRS)
    send_gate()

    radii = ((send_a, recv_a, full_a),)

    def reduce_copies(which):
        send, recv, _ = radii[which]
        per = recv.shape[1]
        return [
            remote(
                send.at[pl.ds(place["gen"] * per, per)], recv.at[my_gen],
                rs_send.at[which, off], rs_recv.at[which, off], place,
            )
            for off, place in gen_peers
        ]

    def gather_copies(which):
        full, per = radii[which][2], radii[which][1].shape[1]
        mine = full.at[pl.ds(my_gen * per, per)]
        return [
            remote(mine, mine, ag_send.at[which, off], ag_recv.at[which, off], place)
            for off, place in gen_peers
        ]

    def reduce_start(which):
        send, recv, _ = radii[which]
        per = recv.shape[1]
        _, _, _, _, _, slot, _, _, made = parts[which]
        tiles = made * span // 8
        send[:tiles] = rad[slot : slot + made].reshape(tiles, 8, wide).astype(jnp.bfloat16)
        if count_gen * per > tiles:
            send[tiles:] = jnp.zeros((count_gen * per - tiles, 8, wide), jnp.bfloat16)
        recv[my_gen] = send[pl.ds(my_gen * per, per)]
        for copy in reduce_copies(which):
            copy.start()

    def gather_start(which):
        _, recv, full = radii[which]
        per = recv.shape[1]
        for copy in reduce_copies(which):
            copy.wait()
        total = recv[0].astype(jnp.float32)
        for slot in range(1, count_gen):
            total = total + recv[slot].astype(jnp.float32)
        full[pl.ds(my_gen * per, per)] = total.astype(jnp.bfloat16)
        for copy in gather_copies(which):
            copy.start()

    reduce_start(0)

    center(parts[0])
    late(pass_on)
    for off in range(count_ch):
        if off == 1:
            late(passed_on)
        compute(parts[1], lax.rem(my_ch + off, count_ch) * sub, sub)

    _, _, _, _, last_out, slot, _, _, made = parts[1]
    recv_b[my_gen] = rad[slot].astype(jnp.bfloat16)
    bc_copies = [
        remote(recv_b.at[my_gen], recv_b.at[my_gen], bc_send.at[off], bc_recv.at[off], place)
        for off, place in gen_peers
    ]
    for copy in bc_copies:
        copy.start()
    gather_start(0)
    late(take)
    center(parts[1])
    finish_gate()
    gate_center = stats_ref[0:1]

    def out_turn(n, _):
        for k in range(chunk):
            g = n * chunk + k
            og_ref[g] = (
                dwc_ref[...] * gates_ref[g] + gate_center * dwg_ref[g].astype(jnp.float32)
            ).astype(jnp.bfloat16)
        done_copy(n).start()
        return 0

    lax.fori_loop(0, chunks, out_turn, 0)
    oc_ref[...] = dwc_ref[...] * gate_center
    results[0].start()
    base = jnp.abs(dwc_ref[...]) * stats_ref[1:2]
    ob_ref[...] = base
    for copy in gather_copies(0):
        copy.wait()
    _, _, _, _, out, _, _, _, made = parts[0]
    whole = full_a[: made * span // 8].astype(jnp.float32).reshape(made, span, wide)
    for row in range(made):
        ob_ref[out + row] += whole[row, :, :chans] * stats_ref[2:3]
    for copy in bc_copies:
        copy.wait()
    total = recv_b[0].astype(jnp.float32)
    for slot in range(1, count_gen):
        total = total + recv_b[slot].astype(jnp.float32)
    ob_ref[last_out] += total[:, :chans] * stats_ref[2:3]
    results[1].start()

    for side, arrives, leaves in ((0, has_up, has_down), (1, has_down, has_up)):
        @pl.when(leaves)
        def _(side=side):
            center_copy(side).wait_send()
            halo_copy(side).wait_send()

        @pl.when(arrives)
        def _(side=side):
            for copy in forwards(side):
                copy.wait_send()

    for n in range(chunks):
        done_copy(n).wait()
    for copy in results:
        copy.wait()


def main_call(mesh, taps, cols, x, xc, w_expand, b_expand, w_depth, b_depth, wr, br, we, be):
    gens, pairs, span, c_in = x.shape
    chans = w_expand.shape[1]
    chunk = CHUNK
    count_gen, count_row, count_ch = mesh["gen"], mesh["row"], mesh["ch"]
    wide = -(-chans // LANES) * LANES
    chunks = gens // chunk
    assert wide == 3 * LANES and gens == 2 * PAIRS * count_ch and gens == chunks * chunk
    assert we.shape[0] <= GROUP and chunks * GROUP <= LANES
    plans, tables = [], []
    for made in (pairs - 1, 1):
        forward, inverse, tap_waves, half, step = transforms(made * span // cols, cols, taps)
        plans.append((half, step, made))
        tables += [jnp.asarray(forward), jnp.asarray(inverse), jnp.asarray(tap_waves)]
    half_a, half_b = plans[0][0], plans[1][0]
    hbm = pl.BlockSpec(memory_space=pltpu.HBM)
    dma = pltpu.SemaphoreType.DMA
    bf16, f32 = jnp.bfloat16, jnp.float32
    masks = jnp.asarray(windows(pairs * span // cols, cols, taps, plans[0][1]))
    args = [x, xc] + tables + [masks, w_expand, b_expand, w_depth, b_depth, wr, br, we, be]
    outs = [
        jax.ShapeDtypeStruct((gens, pairs, span, chans), bf16),
        jax.ShapeDtypeStruct((pairs, span, chans), f32),
        jax.ShapeDtypeStruct((pairs, span, chans), f32),
    ]
    held = [pltpu.VMEM(one.shape, one.dtype) for one in args[1:] + outs[1:]]
    held += [pltpu.VMEM(one.shape, one.dtype) for one in outs[:2]]
    held += [pltpu.VMEM((gens, 1, chans), f32), pltpu.VMEM((3, chans), f32)]
    per = -(-(plans[0][2] * span // 8) // count_gen)
    whole = pltpu.VMEM((count_gen * per, 8, wide), bf16)
    sums = [
        whole, pltpu.VMEM((count_gen, per, 8, wide), bf16), whole, pltpu.VMEM((count_gen, span, wide), bf16),
    ]
    side = count_row * count_ch
    step = plans[0][1]
    return pl.pallas_call(
        functools.partial(main_kernel, mesh, tuple(plans), chunk),
        in_specs=[hbm] * len(args),
        out_specs=[hbm] * OUTS,
        out_shape=outs,
        scratch_shapes=held
        + [
            dma((chunks,)), dma((OUTS - 1,)),
            pltpu.VMEM((pairs, gens, span, c_in), bf16), dma((HELD,)), dma((pairs,)),
            pltpu.VMEM((gens // 2, (pairs + 2) * span, 2 * LANES), bf16),
            pltpu.VMEM((2, span, c_in), bf16),
            pltpu.VMEM((pairs + 2, span, LANES), bf16),
            pltpu.VMEM((gens + 1, step, LANES), bf16),
            pltpu.VMEM((step, wide), f32),
            pltpu.VMEM((gens, pairs, span, chans), bf16),
            pltpu.VMEM((LANES, wide), f32),
            pltpu.VMEM((LANES, wide), bf16),
            pltpu.VMEM((2 * LANES, 2 * LANES), bf16),
            pltpu.VMEM((4, half_a, wide), f32),
            pltpu.VMEM((4, half_b, wide), f32),
            pltpu.VMEM((PAIRS * 4 * half_a, LANES), bf16),
            pltpu.VMEM((PAIRS, 4 * half_a, 2 * LANES), bf16),
            pltpu.VMEM((PAIRS, 2 * half_a, 2 * LANES), bf16),
            pltpu.VMEM((pairs, span, wide), f32),
            pltpu.VMEM((chunks + 1, chunk, wide), f32),
            pltpu.VMEM((LANES, wide), f32), pltpu.VMEM((wide, LANES), bf16), pltpu.VMEM((wide, LANES), bf16),
            pltpu.VMEM((LANES, wide), bf16), pltpu.VMEM((chunk, LANES), f32),
            pltpu.VMEM((gens + chunk, chans), f32),
        ]
        + sums
        + [
            pltpu.VMEM((side, 2 * chunk, LANES), f32),
            pltpu.VMEM((count_gen, 1, chans), f32),
            dma((2,)), dma((2,)), dma((2, count_ch)), dma((2, count_ch)),
            dma((2,)), dma((2,)),
            dma((1, count_gen)), dma((1, count_gen)), dma((1, count_gen)), dma((1, count_gen)),
            dma((count_gen,)), dma((count_gen,)),
            dma((side,)), dma((side,)), dma((count_gen,)), dma((count_gen,)),
        ],
        compiler_params=pltpu.CompilerParams(
            collective_id=1, has_side_effects=True, vmem_limit_bytes=ROOM
        ),
    )(*[pltpu.with_memory_space_constraint(one, pltpu.HBM) for one in args])


def final_kernel(*refs):
    half = len(refs) // 2
    sources, targets, sem = refs[:half], refs[half : 2 * half], refs[-1]
    gens, parts = sources[0].shape[0], 4
    copies = []
    for k in range(parts):
        where = pl.ds(k * (gens // parts), gens // parts)
        copies.append(pltpu.make_async_copy(sources[0].at[where], targets[0].at[where], sem.at[k]))
    for k, (source, target) in enumerate(zip(sources[1:], targets[1:])):
        copies.append(pltpu.make_async_copy(source, target, sem.at[parts + k]))
    for copy in copies:
        copy.start()
    for copy in copies:
        copy.wait()


def final_call(*arrays):
    return pl.pallas_call(
        final_kernel,
        in_specs=[pl.BlockSpec(memory_space=pltpu.VMEM)] * len(arrays),
        out_specs=[pl.BlockSpec(memory_space=pltpu.HBM)] * len(arrays),
        out_shape=[jax.ShapeDtypeStruct(one.shape, one.dtype) for one in arrays],
        scratch_shapes=[pltpu.SemaphoreType.DMA((3 + len(arrays),))],
        compiler_params=pltpu.CompilerParams(vmem_limit_bytes=1 << 20),
    )(*arrays)


def on_device(
    shape, x_center, x_gens, w_expand, b_expand, w_depth, b_depth, w_reduce, b_reduce, w_excite, b_excite
):
    gens, rows, cols, c_in = x_gens.shape
    chans = w_expand.shape[1]
    taps = w_depth.shape[0]
    margin = taps // 2
    pairs, span = rows // margin, margin * cols
    x = x_gens.reshape(gens, pairs, span, c_in)
    xc = x_center.reshape(pairs, span, c_in)
    made = main_call(
        shape, taps, cols, x, xc, w_expand, b_expand, w_depth, b_depth,
        w_reduce.T, b_reduce, w_excite, b_excite,
    )
    out_gens, out_center, out_box = final_call(*made)
    image = (rows, cols, chans)
    return out_center.reshape(image), out_gens.reshape((gens,) + image), out_box.reshape(image)


def solution(mesh):
    in_specs = (
        P(("grp", "row"), None, None),
        P(("grp", "gen"), "row", None, None),
        P(None, "ch"),
        P("ch"),
        P(None, None, "ch"),
        P("ch"),
        P(),
        P(),
        P(None, "ch"),
        P("ch"),
    )
    out_specs = (
        P(("grp", "row"), None, "ch"),
        P(("grp", "gen"), "row", None, "ch"),
        P(("grp", "row"), None, "ch"),
    )
    return jax.shard_map(
        functools.partial(on_device, dict(mesh.shape)), mesh=mesh, in_specs=in_specs, out_specs=out_specs, check_vma=False
    )
```

```python
import functools

import jax
import jax.numpy as jnp
import ml_dtypes
import numpy as np
from jax import lax
from jax.experimental import pallas as pl
from jax.experimental.pallas import tpu as pltpu
from jax.sharding import PartitionSpec as P

MESH = pl.DeviceIdType.MESH
LANES = 128
PAIRS = 8
CHUNK = 8
GROUP = 32
ROOM = 40 << 20
OUTS = 3
HELD = 16


def dot(a, b):
    return jnp.dot(a, b, preferred_element_type=jnp.float32)


def split(values):
    high = values.astype(ml_dtypes.bfloat16)
    return high, (values - high.astype(np.float64)).astype(ml_dtypes.bfloat16)


def transforms(rows, cols, taps):
    m = taps // 2
    n_r, n_c = rows + 2 * m, cols + m
    count = n_r * n_c
    r_in, c_in = np.arange(n_r)[:, None], np.arange(cols)[None, :]
    r_out = np.arange(rows)[:, None]
    tap_r, tap_c = np.arange(taps)[:, None], np.arange(taps)[None, :] - m

    def angle(freq, r, c):
        return (2 * np.pi * (freq[0] * r / n_r + freq[1] * c / n_c)).ravel()

    seen, double, single = set(), [], []
    for freq in [(u, v) for u in range(n_r) for v in range(n_c)]:
        twin = (-freq[0] % n_r, -freq[1] % n_c)
        if freq not in seen:
            (single if twin == freq else double).append(freq)
        seen |= {freq, twin}
    blocks = [[], [], [], [], [], [], [], []]
    for freq in double:
        a, t, o = angle(freq, r_in, c_in), angle(freq, tap_r, tap_c), angle(freq, r_out, c_in)
        entry = (
            np.cos(a), -np.sin(a), np.cos(t), np.sin(t), np.sin(t), np.cos(t),
            2 * np.cos(o) / count, -2 * np.sin(o) / count,
        )
        for block, part in zip(blocks, entry):
            block.append(part)
    single += [None] * (len(single) % 2)
    for one, two in zip(single[::2], single[1::2]):
        def wave(freq, r, c):
            scale = 0.0 if freq is None else 1.0
            return scale * np.cos(angle(freq or (0, 0), r, c))

        entry = (
            wave(one, r_in, c_in), wave(two, r_in, c_in),
            wave(one, tap_r, tap_c), 0 * wave(one, tap_r, tap_c),
            0 * wave(one, tap_r, tap_c), wave(two, tap_r, tap_c),
            wave(one, r_out, c_in) / count, wave(two, r_out, c_in) / count,
        )
        for block, part in zip(blocks, entry):
            block.append(part)
    half = -(-len(blocks[0]) // 8) * 8
    blocks = [np.pad(np.array(b), ((0, half - len(b)), (0, 0))) for b in blocks]
    def alternate(one, two):
        shape = (half // 8, 8, -1)
        return np.stack([one.reshape(shape), two.reshape(shape)], axis=1).reshape(2 * half, -1)

    forward = alternate(blocks[0], blocks[1])
    inverse = alternate(blocks[6], blocks[7]).T
    waves = np.concatenate(blocks[2:6], axis=0)
    high, low = split(waves)
    step = -(-taps * taps // 8) * 8
    tap_waves = np.zeros((4 * half, 4 * step), ml_dtypes.bfloat16)
    for slot, part in enumerate((high, high, low)):
        tap_waves[:, slot * step : slot * step + taps * taps] = part
    return forward.astype(ml_dtypes.bfloat16), inverse.astype(ml_dtypes.bfloat16), tap_waves, half, step


def windows(rows, cols, taps, depth):
    m = taps // 2
    tap_r, tap_c = np.divmod(np.arange(taps * taps)[:, None], taps)
    row, col = np.divmod(np.arange(rows * cols)[None, :], cols)
    inside = (col - tap_c + m >= 0) & (col - tap_c + m < cols)
    masks = np.zeros((3, depth, rows * cols), ml_dtypes.bfloat16)
    masks[0, : taps * taps] = inside
    masks[1, : taps * taps] = inside & (row - tap_r + m < 0)
    masks[2, : taps * taps] = inside & (row - tap_r + m >= rows)
    return masks


def relax_gate(ex_center, gate_radius):
    low_end = ex_center - gate_radius
    high_end = ex_center + gate_radius
    sig_low = jax.nn.sigmoid(low_end)
    sig_high = jax.nn.sigmoid(high_end)
    slope_val = jnp.minimum(sig_low * (1.0 - sig_low), sig_high * (1.0 - sig_high))
    gate_center = slope_val * ex_center + 0.5 * (
        sig_high + sig_low - slope_val * (high_end + low_end)
    )
    spread_term = 0.5 * (sig_high - sig_low - slope_val * (high_end - low_end))
    return (gate_center, slope_val, spread_term)


def main_kernel(mesh, plans, chunk, x_hbm, *refs):
    main_body(
        mesh, plans, chunk, x_hbm, refs[:HELD], refs[HELD : HELD + OUTS],
        refs[HELD + OUTS : 2 * HELD + OUTS], *refs[2 * HELD + OUTS :],
    )


def main_body(
    mesh, plans, chunk, x_hbm, sources, outs, locals_,
    oc_ref, ob_ref, dwg_ref, dwc_ref, gates_ref, stats_ref, g_sem, o_sem, xs, l_sem, x_sem,
    xall, xcs, xcp, sums, taps_f, og_ref, wf, wz, w2, spec_a, spec_b, xf_s, y1_s, y2_s,
    rad, pool, own_wr, wr_high, wr_low, we_three, br_wide, ex,
    send_a, recv_a, full_a, recv_b, squeeze, gate,
    h_send, h_recv, f_send, f_recv, c_send, c_recv,
    rs_send, rs_recv, ag_send, ag_recv, bc_send, bc_recv, sq_send, sq_recv, gt_send, gt_recv,
):
    (
        xc_ref, fwd_a, inv_a, tw_a, fwd_b, inv_b, tw_b, mask_ref,
        w_ref, b_ref, wd_ref, bd_ref, wr_ref, br_ref, we_ref, be_ref,
    ) = locals_
    count_gen, count_row, count_ch = mesh["gen"], mesh["row"], mesh["ch"]
    my_gen = lax.axis_index("gen")
    my_row = lax.axis_index("row")
    my_ch = lax.axis_index("ch")
    has_up = my_row > 0
    has_down = my_row < count_row - 1
    last = jnp.logical_and(has_up, jnp.logical_not(has_down))
    inner = jnp.logical_and(has_up, has_down)
    flip = jnp.where(last, 1, 0)
    gens, pairs, span, chans = dwg_ref.shape
    c_in = w_ref.shape[0]
    taps = wd_ref.shape[0]
    wide = wz.shape[1]
    main = wide - LANES
    chunks = gens // chunk
    all_cells = pairs * span * count_row
    sub = gens // (2 * count_ch)

    def remote(src, dst, send_sem, recv_sem, place):
        return pltpu.make_async_remote_copy(
            src_ref=src, dst_ref=dst, send_sem=send_sem, recv_sem=recv_sem,
            device_id=place, device_id_type=MESH,
        )

    gen_peers = [(off, {"gen": lax.rem(my_gen + off, count_gen)}) for off in range(1, count_gen)]
    side_peers = []
    for off_row in range(count_row):
        for off_ch in range(count_ch):
            if off_row or off_ch:
                place = {
                    "row": lax.rem(my_row + off_row, count_row),
                    "ch": lax.rem(my_ch + off_ch, count_ch),
                }
                side_peers.append((off_row * count_ch + off_ch, place))
    barrier = pltpu.get_barrier_semaphore()
    for _, place in gen_peers + side_peers:
        pl.semaphore_signal(barrier, inc=1, device_id=place, device_id_type=MESH)

    x_loads = [
        pltpu.make_async_copy(x_hbm.at[:, row], xs.at[row], x_sem.at[row]) for row in range(pairs)
    ]
    for row in (0, pairs - 1) + tuple(range(1, pairs - 1)):
        x_loads[row].start()
    loads = [
        pltpu.make_async_copy(source, target, l_sem.at[k])
        for k, (source, target) in enumerate(zip(sources, locals_))
    ]
    for load in loads:
        load.start()
    own_rows = slice(span, (1 + pairs) * span)
    for k in range(2):
        pad = slice(LANES * k + c_in, LANES * (k + 1))
        xall[:, own_rows, pad] = jnp.zeros((gens // 2, pairs * span, LANES - c_in), jnp.bfloat16)
    for place, arrives in ((0, has_up), (pairs + 1, has_down)):
        @pl.when(jnp.logical_not(arrives))
        def _(place=place):
            xall[:, place * span : (place + 1) * span] = jnp.zeros(
                (gens // 2, span, 2 * LANES), jnp.bfloat16
            )

    def fill(row):
        x_loads[row].wait()
        for g in range(gens):
            lane = slice(LANES * (g % 2), LANES * (g % 2) + c_in)
            xall[g // 2, (1 + row) * span : (2 + row) * span, lane] = xs[row, g]

    fill(0)
    fill(pairs - 1)
    pl.semaphore_wait(barrier, len(gen_peers) + len(side_peers))

    row_place = (
        {"row": lax.rem(my_row + 1, count_row)},
        {"row": lax.rem(my_row + count_row - 1, count_row)},
    )
    edge = (pairs - 1, 0)
    place_of = (0, pairs + 1)

    def edge_of(row):
        return xall.at[pl.ds(my_ch * sub, sub), pl.ds(row * span, span)]

    def halo_copy(side):
        return remote(
            edge_of(1 + edge[side]), edge_of(place_of[side]),
            h_send.at[side], h_recv.at[side], row_place[side],
        )

    def center_copy(side):
        return remote(
            sources[0].at[edge[side]], xcs.at[side], c_send.at[side], c_recv.at[side], row_place[side]
        )

    def forwards(side):
        return [
            remote(
                edge_of(place_of[side]), edge_of(place_of[side]),
                f_send.at[side, off], f_recv.at[side, off],
                {"ch": lax.rem(my_ch + off, count_ch)},
            )
            for off in range(1, count_ch)
        ]

    for side, leaves in ((0, has_down), (1, has_up)):
        @pl.when(leaves)
        def _(side=side):
            halo_copy(side).start()
            center_copy(side).start()

    for row in range(1, pairs - 1):
        fill(row)

    def pass_on(side):
        halo_copy(side).wait_recv()
        for copy in forwards(side):
            copy.start()

    def passed_on(side):
        for copy in forwards(side):
            copy.wait_recv()

    def late(action):
        @pl.when(last)
        def _():
            action(0)

        @pl.when(has_down)
        def _():
            action(1)

    mine = my_row * count_ch + my_ch
    sq_copies = [
        remote(squeeze.at[mine], squeeze.at[mine], sq_send.at[off], sq_recv.at[off], place)
        for off, place in side_peers
    ]
    gt_copies = [
        remote(gate.at[my_gen], gate.at[my_gen], gt_send.at[off], gt_recv.at[off], place)
        for off, place in gen_peers
    ]

    def send_squeeze():
        pooled = pool[...].reshape(gens + chunk, wide) * (1.0 / all_cells)
        high = pooled.astype(jnp.bfloat16)
        low = (pooled - high.astype(jnp.float32)).astype(jnp.bfloat16)
        part = dot(high, wr_high[...]) + (dot(low, wr_high[...]) + dot(high, wr_low[...]))
        packed = part[:chunk]
        for n in range(1, chunks):
            packed = packed + pltpu.roll(part[n * chunk : (n + 1) * chunk], n * GROUP, 1)
        squeeze[mine, :chunk] = packed
        squeeze[mine, chunk:] = part[gens:]
        for copy in sq_copies:
            copy.start()

    def send_gate():
        for copy in sq_copies:
            copy.wait()
        total = squeeze[0]
        for slot in range(1, count_row * count_ch):
            total = total + squeeze[slot]
        spread = [total[:chunk]]
        spread += [pltpu.roll(total[:chunk], LANES - n * GROUP, 1) for n in range(1, chunks)]
        spread.append(total[chunk:] + br_wide[...])
        total = jnp.concatenate(spread, axis=0)
        total = jnp.where(lax.broadcasted_iota(jnp.int32, total.shape, 1) < GROUP, total, 0.0)
        high = total.astype(jnp.bfloat16).astype(jnp.float32)
        three = high + pltpu.roll(total - high, GROUP, 1) + pltpu.roll(high, 2 * GROUP, 1)
        ex_all = dot(three.astype(jnp.bfloat16), we_three[...])
        ex[...] = ex_all[:, :chans]
        ex_gens = ex[:gens]
        gate[my_gen] = jnp.sum(jnp.abs(ex_gens), axis=0, keepdims=True)
        for copy in gt_copies:
            copy.start()

    def finish_gate():
        for copy in gt_copies:
            copy.wait()
        gate_radius = gate[0]
        for slot in range(1, count_gen):
            gate_radius = gate_radius + gate[slot]
        ex_center = ex[gens : gens + 1] + be_ref[...][None, :]
        gate_center, slope_val, spread_term = relax_gate(ex_center, gate_radius)
        gates_ref[...] = (slope_val * ex[:gens])[:, None, :]
        stats_ref[0:1] = gate_center
        stats_ref[1:2] = spread_term
        stats_ref[2:3] = slope_val * gate_radius + spread_term

    for load in loads:
        load.wait()
    wf[...] = jnp.zeros_like(wf)
    wf[:c_in, :chans] = w_ref[...].astype(jnp.float32)
    bias = b_ref[...][None, :]
    bias_high = bias.astype(jnp.bfloat16).astype(jnp.float32)
    wf[c_in : c_in + 1, :chans] = bias_high
    wf[c_in + 1 : c_in + 2, :chans] = bias - bias_high
    wz[...] = wf[...].astype(jnp.bfloat16)
    w2[...] = jnp.zeros_like(w2)
    w2[:LANES, :LANES] = wz[:, main:]
    w2[LANES:, LANES:] = wz[:, main:]
    wf[...] = jnp.zeros_like(wf)
    taps_f[...] = jnp.zeros_like(taps_f)
    step = plans[0][1]
    for row in range(taps):
        one = wd_ref[row]
        taps_f[row * taps : (row + 1) * taps, :chans] = one
        high = one.astype(jnp.bfloat16).astype(jnp.float32)
        for slot, part in enumerate((high, one - high, high)):
            start = slot * step + row * taps
            wf[start : start + taps, :chans] = part
    wtap = wf[...].astype(jnp.bfloat16)
    spec_a[...] = dot(tw_a[...], wtap).reshape(spec_a.shape)
    spec_b[...] = dot(tw_b[...], wtap).reshape(spec_b.shape)
    ones = jnp.where(
        lax.broadcasted_iota(jnp.int32, (span, LANES - c_in), 1) < 2, 1.0, 0.0
    ).astype(jnp.bfloat16)
    xcp[...] = jnp.zeros_like(xcp)
    xcp[1 : 1 + pairs, :, :c_in] = xc_ref[...]
    for row in range(pairs):
        xcp[1 + row, :, c_in:] = ones
    rad[...] = jnp.zeros_like(rad)
    own = wr_ref[:, :chans]
    for other in range(1, count_ch):
        own = jnp.where(my_ch == other, wr_ref[:, other * chans : (other + 1) * chans], own)
    units = own.shape[0]
    own_wr[...] = jnp.zeros_like(own_wr)
    own_wr[:units, :chans] = own
    turned = own_wr[...].T
    turned_high = turned.astype(jnp.bfloat16)
    wr_high[...] = turned_high
    wr_low[...] = (turned - turned_high.astype(jnp.float32)).astype(jnp.bfloat16)
    own_wr[...] = jnp.zeros_like(own_wr)
    we_high = we_ref[...].astype(jnp.bfloat16).astype(jnp.float32)
    own_wr[:units, :chans] = we_high
    own_wr[GROUP : GROUP + units, :chans] = we_high
    own_wr[2 * GROUP : 2 * GROUP + units, :chans] = we_ref[...] - we_high
    we_three[...] = own_wr[...].astype(jnp.bfloat16)
    br_wide[...] = jnp.zeros_like(br_wide)
    br_wide[0:1, :units] = br_ref[...][None, :]

    def take(side):
        center_copy(side).wait_recv()
        xcp[place_of[side], :, :c_in] = xcs[side]
        xcp[place_of[side], :, c_in:] = ones

    @pl.when(inner)
    def _():
        pass_on(0)
        passed_on(0)
        take(0)

    above = jnp.where(has_up, 0.0, 1.0)
    below = jnp.where(has_down, 0.0, 1.0)
    window = (
        mask_ref[0].astype(jnp.float32)
        - above * mask_ref[1].astype(jnp.float32)
        - below * mask_ref[2].astype(jnp.float32)
    ).astype(jnp.bfloat16)
    deep = window.shape[0]
    for q in range(gens // 2):
        both = dot(window, xall[q, own_rows]).astype(jnp.bfloat16)
        sums[2 * q] = both[:, :LANES]
        sums[2 * q + 1] = both[:, LANES:]
    sums[gens] = dot(window, xcp[1 : 1 + pairs].reshape(pairs * span, LANES)).astype(jnp.bfloat16)
    for n in range(chunks):
        block = dot(sums[n * chunk : (n + 1) * chunk].reshape(chunk * deep, LANES), wz[...])
        pool[n] = jnp.sum(block.reshape(chunk, deep, wide) * taps_f[...], axis=1)
    pool[chunks] = jnp.zeros((chunk, wide), jnp.float32)
    pool[chunks, 0:1] = jnp.sum(dot(sums[gens], wz[...]) * taps_f[...], axis=0, keepdims=True)
    pool[chunks, 0:1, :chans] += (pairs * span) * bd_ref[...][None, :]
    send_squeeze()

    parts = (
        (fwd_a, inv_a, spec_a, flip, flip, 0) + plans[0],
        (fwd_b, inv_b, spec_b, (pairs - 1) * (1 - flip), (pairs - 1) * (1 - flip), pairs - 1) + plans[1],
    )

    def mix(e, spec, lane, half):
        count, width = e.shape[0] // (2 * half), e.shape[1]
        e = e.reshape(count, half // 8, 2, 8, width)
        a, b, c, d = [spec[k, :, lane].reshape(1, half // 8, 8, width) for k in range(4)]
        re, im = e[:, :, 0], e[:, :, 1]
        y = jnp.stack([re * a - im * b, re * c + im * d], axis=2)
        return y.reshape(count * 2 * half, width).astype(jnp.bfloat16)

    def compute(part, start, count):
        fwd, inv, spec, first, out, slot, half, _, made = part
        depth = fwd.shape[1]
        size = 2 * half
        cells = made * span
        rows = pl.ds(pl.multiple_of(first * span, span), depth)
        where = slice(slot, slot + made)
        for u in range(count):
            xf = dot(fwd[...], xall[start + u, rows]).astype(jnp.bfloat16)
            xf_s[2 * u * size : (2 * u + 1) * size] = xf[:, :LANES]
            xf_s[(2 * u + 1) * size : (2 * u + 2) * size] = xf[:, LANES:]
        for u in range(count):
            both = xf_s[2 * u * size : (2 * u + 2) * size]
            y1_s[u, : 2 * size] = mix(dot(both, wz[:, :main]), spec, slice(0, main), half)
            e2 = dot(jnp.concatenate([both[:size], both[size:]], axis=1), w2[...])
            for k in range(2):
                lane = slice(LANES * k, LANES * (k + 1))
                y2_s[u, :size, lane] = mix(e2[:, lane], spec, slice(main, wide), half)
        total = None
        for u in range(count):
            for k in range(2):
                g = 2 * (start + u) + k
                t = dot(inv[...], y1_s[u, k * size : (k + 1) * size])
                for row in range(made):
                    dwg_ref[g, out + row, :, :main] = t[row * span : (row + 1) * span].astype(jnp.bfloat16)
                total = jnp.abs(t) if total is None else total + jnp.abs(t)
        rad[where, :, :main] += total.reshape(made, span, main)
        total = None
        for u in range(count):
            t = dot(inv[...], y2_s[u, :size])
            for k in range(2):
                g = 2 * (start + u) + k
                mine = t[:, LANES * k : LANES * (k + 1)]
                for row in range(made):
                    dwg_ref[g, out + row, :, main:] = mine[
                        row * span : (row + 1) * span, : chans - main
                    ].astype(jnp.bfloat16)
                total = jnp.abs(mine) if total is None else total + jnp.abs(mine)
        rad[where, :, main:] += total.reshape(made, span, LANES)

    def center(part):
        fwd, inv, spec, first, out, _, half, _, made = part
        depth = fwd.shape[1]
        cells = made * span
        both = xcp[pl.ds(first, depth // span)].reshape(depth, LANES)
        xf = dot(fwd[...], both).astype(jnp.bfloat16)
        y = mix(dot(xf, wz[...]), spec, slice(0, wide), half)
        t = dot(inv[...], y)
        bias = bd_ref[...][None, :]
        for row in range(made):
            dwc_ref[out + row] = t[row * span : (row + 1) * span, :chans] + bias

    def done_copy(n):
        where = pl.ds(n * chunk, chunk)
        return pltpu.make_async_copy(og_ref.at[where], outs[0].at[where], g_sem.at[n])

    results = [
        pltpu.make_async_copy(source, target, o_sem.at[k])
        for k, (source, target) in enumerate(
            zip((oc_ref, ob_ref), outs[1:])
        )
    ]

    for start in range(0, gens // 2, PAIRS):
        compute(parts[0], start, PAIRS)
    radii = ((send_a, recv_a, full_a),)

    def reduce_copies(which):
        send, recv, _ = radii[which]
        per = recv.shape[1]
        return [
            remote(
                send.at[pl.ds(place["gen"] * per, per)], recv.at[my_gen],
                rs_send.at[which, off], rs_recv.at[which, off], place,
            )
            for off, place in gen_peers
        ]

    def gather_copies(which):
        full, per = radii[which][2], radii[which][1].shape[1]
        mine = full.at[pl.ds(my_gen * per, per)]
        return [
            remote(mine, mine, ag_send.at[which, off], ag_recv.at[which, off], place)
            for off, place in gen_peers
        ]

    def reduce_start(which):
        send, recv, _ = radii[which]
        per = recv.shape[1]
        _, _, _, _, _, slot, _, _, made = parts[which]
        tiles = made * span // 8
        send[:tiles] = rad[slot : slot + made].reshape(tiles, 8, wide).astype(jnp.bfloat16)
        if count_gen * per > tiles:
            send[tiles:] = jnp.zeros((count_gen * per - tiles, 8, wide), jnp.bfloat16)
        recv[my_gen] = send[pl.ds(my_gen * per, per)]
        for copy in reduce_copies(which):
            copy.start()

    def gather_start(which):
        _, recv, full = radii[which]
        per = recv.shape[1]
        for copy in reduce_copies(which):
            copy.wait()
        total = recv[0].astype(jnp.float32)
        for slot in range(1, count_gen):
            total = total + recv[slot].astype(jnp.float32)
        full[pl.ds(my_gen * per, per)] = total.astype(jnp.bfloat16)
        for copy in gather_copies(which):
            copy.start()

    reduce_start(0)

    late(pass_on)
    for off in range(count_ch):
        if off == 1:
            send_gate()
            late(passed_on)
        compute(parts[1], lax.rem(my_ch + off, count_ch) * sub, sub)

    _, _, _, _, last_out, slot, _, _, made = parts[1]
    recv_b[my_gen] = rad[slot].astype(jnp.bfloat16)
    bc_copies = [
        remote(recv_b.at[my_gen], recv_b.at[my_gen], bc_send.at[off], bc_recv.at[off], place)
        for off, place in gen_peers
    ]
    for copy in bc_copies:
        copy.start()
    gather_start(0)
    late(take)
    center(parts[0])
    center(parts[1])
    finish_gate()
    gate_center = stats_ref[0:1]

    def out_turn(n, _):
        for k in range(chunk):
            g = n * chunk + k
            og_ref[g] = (
                dwc_ref[...] * gates_ref[g] + gate_center * dwg_ref[g].astype(jnp.float32)
            ).astype(jnp.bfloat16)
        done_copy(n).start()
        return 0

    lax.fori_loop(0, chunks, out_turn, 0)
    oc_ref[...] = dwc_ref[...] * gate_center
    results[0].start()
    base = jnp.abs(dwc_ref[...]) * stats_ref[1:2]
    ob_ref[...] = base
    for copy in gather_copies(0):
        copy.wait()
    _, _, _, _, out, _, _, _, made = parts[0]
    whole = full_a[: made * span // 8].astype(jnp.float32).reshape(made, span, wide)
    for row in range(made):
        ob_ref[out + row] += whole[row, :, :chans] * stats_ref[2:3]
    for copy in bc_copies:
        copy.wait()
    total = recv_b[0].astype(jnp.float32)
    for slot in range(1, count_gen):
        total = total + recv_b[slot].astype(jnp.float32)
    ob_ref[last_out] += total[:, :chans] * stats_ref[2:3]
    results[1].start()

    for side, arrives, leaves in ((0, has_up, has_down), (1, has_down, has_up)):
        @pl.when(leaves)
        def _(side=side):
            center_copy(side).wait_send()
            halo_copy(side).wait_send()

        @pl.when(arrives)
        def _(side=side):
            for copy in forwards(side):
                copy.wait_send()

    for n in range(chunks):
        done_copy(n).wait()
    for copy in results:
        copy.wait()


def main_call(mesh, taps, cols, x, xc, w_expand, b_expand, w_depth, b_depth, wr, br, we, be):
    gens, pairs, span, c_in = x.shape
    chans = w_expand.shape[1]
    chunk = CHUNK
    count_gen, count_row, count_ch = mesh["gen"], mesh["row"], mesh["ch"]
    wide = -(-chans // LANES) * LANES
    chunks = gens // chunk
    assert wide == 3 * LANES and gens == 2 * PAIRS * count_ch and gens == chunks * chunk
    assert we.shape[0] <= GROUP and chunks * GROUP <= LANES
    plans, tables = [], []
    for made in (pairs - 1, 1):
        forward, inverse, tap_waves, half, step = transforms(made * span // cols, cols, taps)
        plans.append((half, step, made))
        tables += [jnp.asarray(forward), jnp.asarray(inverse), jnp.asarray(tap_waves)]
    half_a, half_b = plans[0][0], plans[1][0]
    hbm = pl.BlockSpec(memory_space=pltpu.HBM)
    dma = pltpu.SemaphoreType.DMA
    bf16, f32 = jnp.bfloat16, jnp.float32
    masks = jnp.asarray(windows(pairs * span // cols, cols, taps, plans[0][1]))
    args = [x, xc] + tables + [masks, w_expand, b_expand, w_depth, b_depth, wr, br, we, be]
    outs = [
        jax.ShapeDtypeStruct((gens, pairs, span, chans), bf16),
        jax.ShapeDtypeStruct((pairs, span, chans), f32),
        jax.ShapeDtypeStruct((pairs, span, chans), f32),
    ]
    held = [pltpu.VMEM(one.shape, one.dtype) for one in args[1:] + outs[1:]]
    held += [pltpu.VMEM(one.shape, one.dtype) for one in outs[:2]]
    held += [pltpu.VMEM((gens, 1, chans), f32), pltpu.VMEM((3, chans), f32)]
    per = -(-(plans[0][2] * span // 8) // count_gen)
    whole = pltpu.VMEM((count_gen * per, 8, wide), bf16)
    sums = [
        whole, pltpu.VMEM((count_gen, per, 8, wide), bf16), whole, pltpu.VMEM((count_gen, span, wide), bf16),
    ]
    side = count_row * count_ch
    step = plans[0][1]
    return pl.pallas_call(
        functools.partial(main_kernel, mesh, tuple(plans), chunk),
        in_specs=[hbm] * len(args),
        out_specs=[hbm] * OUTS,
        out_shape=outs,
        scratch_shapes=held
        + [
            dma((chunks,)), dma((OUTS - 1,)),
            pltpu.VMEM((pairs, gens, span, c_in), bf16), dma((HELD,)), dma((pairs,)),
            pltpu.VMEM((gens // 2, (pairs + 2) * span, 2 * LANES), bf16),
            pltpu.VMEM((2, span, c_in), bf16),
            pltpu.VMEM((pairs + 2, span, LANES), bf16),
            pltpu.VMEM((gens + 1, step, LANES), bf16),
            pltpu.VMEM((step, wide), f32),
            pltpu.VMEM((gens, pairs, span, chans), bf16),
            pltpu.VMEM((LANES, wide), f32),
            pltpu.VMEM((LANES, wide), bf16),
            pltpu.VMEM((2 * LANES, 2 * LANES), bf16),
            pltpu.VMEM((4, half_a, wide), f32),
            pltpu.VMEM((4, half_b, wide), f32),
            pltpu.VMEM((PAIRS * 4 * half_a, LANES), bf16),
            pltpu.VMEM((PAIRS, 4 * half_a, 2 * LANES), bf16),
            pltpu.VMEM((PAIRS, 2 * half_a, 2 * LANES), bf16),
            pltpu.VMEM((pairs, span, wide), f32),
            pltpu.VMEM((chunks + 1, chunk, wide), f32),
            pltpu.VMEM((LANES, wide), f32), pltpu.VMEM((wide, LANES), bf16), pltpu.VMEM((wide, LANES), bf16),
            pltpu.VMEM((LANES, wide), bf16), pltpu.VMEM((chunk, LANES), f32),
            pltpu.VMEM((gens + chunk, chans), f32),
        ]
        + sums
        + [
            pltpu.VMEM((side, 2 * chunk, LANES), f32),
            pltpu.VMEM((count_gen, 1, chans), f32),
            dma((2,)), dma((2,)), dma((2, count_ch)), dma((2, count_ch)),
            dma((2,)), dma((2,)),
            dma((1, count_gen)), dma((1, count_gen)), dma((1, count_gen)), dma((1, count_gen)),
            dma((count_gen,)), dma((count_gen,)),
            dma((side,)), dma((side,)), dma((count_gen,)), dma((count_gen,)),
        ],
        compiler_params=pltpu.CompilerParams(
            collective_id=1, has_side_effects=True, vmem_limit_bytes=ROOM
        ),
    )(*[pltpu.with_memory_space_constraint(one, pltpu.HBM) for one in args])


def final_kernel(*refs):
    half = len(refs) // 2
    sources, targets, sem = refs[:half], refs[half : 2 * half], refs[-1]
    gens, parts = sources[0].shape[0], 4
    copies = []
    for k in range(parts):
        where = pl.ds(k * (gens // parts), gens // parts)
        copies.append(pltpu.make_async_copy(sources[0].at[where], targets[0].at[where], sem.at[k]))
    for k, (source, target) in enumerate(zip(sources[1:], targets[1:])):
        copies.append(pltpu.make_async_copy(source, target, sem.at[parts + k]))
    for copy in copies:
        copy.start()
    for copy in copies:
        copy.wait()


def final_call(*arrays):
    return pl.pallas_call(
        final_kernel,
        in_specs=[pl.BlockSpec(memory_space=pltpu.VMEM)] * len(arrays),
        out_specs=[pl.BlockSpec(memory_space=pltpu.HBM)] * len(arrays),
        out_shape=[jax.ShapeDtypeStruct(one.shape, one.dtype) for one in arrays],
        scratch_shapes=[pltpu.SemaphoreType.DMA((3 + len(arrays),))],
        compiler_params=pltpu.CompilerParams(vmem_limit_bytes=1 << 20),
    )(*arrays)


def on_device(
    shape, x_center, x_gens, w_expand, b_expand, w_depth, b_depth, w_reduce, b_reduce, w_excite, b_excite
):
    gens, rows, cols, c_in = x_gens.shape
    chans = w_expand.shape[1]
    taps = w_depth.shape[0]
    margin = taps // 2
    pairs, span = rows // margin, margin * cols
    x = x_gens.reshape(gens, pairs, span, c_in)
    xc = x_center.reshape(pairs, span, c_in)
    made = main_call(
        shape, taps, cols, x, xc, w_expand, b_expand, w_depth, b_depth,
        w_reduce.T, b_reduce, w_excite, b_excite,
    )
    out_gens, out_center, out_box = final_call(*made)
    image = (rows, cols, chans)
    return out_center.reshape(image), out_gens.reshape((gens,) + image), out_box.reshape(image)


def solution(mesh):
    in_specs = (
        P(("grp", "row"), None, None),
        P(("grp", "gen"), "row", None, None),
        P(None, "ch"),
        P("ch"),
        P(None, None, "ch"),
        P("ch"),
        P(),
        P(),
        P(None, "ch"),
        P("ch"),
    )
    out_specs = (
        P(("grp", "row"), None, "ch"),
        P(("grp", "gen"), "row", None, "ch"),
        P(("grp", "row"), None, "ch"),
    )
    return jax.shard_map(
        functools.partial(on_device, dict(mesh.shape)), mesh=mesh, in_specs=in_specs, out_specs=out_specs, check_vma=False
    )
```

```python
import functools

import jax
import jax.numpy as jnp
import ml_dtypes
import numpy as np
from jax import lax
from jax.experimental import pallas as pl
from jax.experimental.pallas import tpu as pltpu
from jax.sharding import PartitionSpec as P

MESH = pl.DeviceIdType.MESH
LANES = 128
PAIRS = 8
CHUNK = 8
GROUP = 32
ROOM = 40 << 20
OUTS = 3
HELD = 16


def dot(a, b):
    return jnp.dot(a, b, preferred_element_type=jnp.float32)


def split(values):
    high = values.astype(ml_dtypes.bfloat16)
    return high, (values - high.astype(np.float64)).astype(ml_dtypes.bfloat16)


def transforms(rows, cols, taps):
    m = taps // 2
    n_r, n_c = rows + 2 * m, cols + m
    count = n_r * n_c
    r_in, c_in = np.arange(n_r)[:, None], np.arange(cols)[None, :]
    r_out = np.arange(rows)[:, None]
    tap_r, tap_c = np.arange(taps)[:, None], np.arange(taps)[None, :] - m

    def angle(freq, r, c):
        return (2 * np.pi * (freq[0] * r / n_r + freq[1] * c / n_c)).ravel()

    seen, double, single = set(), [], []
    for freq in [(u, v) for u in range(n_r) for v in range(n_c)]:
        twin = (-freq[0] % n_r, -freq[1] % n_c)
        if freq not in seen:
            (single if twin == freq else double).append(freq)
        seen |= {freq, twin}
    blocks = [[], [], [], [], [], [], [], []]
    for freq in double:
        a, t, o = angle(freq, r_in, c_in), angle(freq, tap_r, tap_c), angle(freq, r_out, c_in)
        entry = (
            np.cos(a), -np.sin(a), np.cos(t), np.sin(t), np.sin(t), np.cos(t),
            2 * np.cos(o) / count, -2 * np.sin(o) / count,
        )
        for block, part in zip(blocks, entry):
            block.append(part)
    single += [None] * (len(single) % 2)
    for one, two in zip(single[::2], single[1::2]):
        def wave(freq, r, c):
            scale = 0.0 if freq is None else 1.0
            return scale * np.cos(angle(freq or (0, 0), r, c))

        entry = (
            wave(one, r_in, c_in), wave(two, r_in, c_in),
            wave(one, tap_r, tap_c), 0 * wave(one, tap_r, tap_c),
            0 * wave(one, tap_r, tap_c), wave(two, tap_r, tap_c),
            wave(one, r_out, c_in) / count, wave(two, r_out, c_in) / count,
        )
        for block, part in zip(blocks, entry):
            block.append(part)
    half = -(-len(blocks[0]) // 8) * 8
    blocks = [np.pad(np.array(b), ((0, half - len(b)), (0, 0))) for b in blocks]
    def alternate(one, two):
        shape = (half // 8, 8, -1)
        return np.stack([one.reshape(shape), two.reshape(shape)], axis=1).reshape(2 * half, -1)

    forward = alternate(blocks[0], blocks[1])
    inverse = alternate(blocks[6], blocks[7]).T
    waves = np.concatenate(blocks[2:6], axis=0)
    high, low = split(waves)
    step = -(-taps * taps // 8) * 8
    tap_waves = np.zeros((4 * half, 4 * step), ml_dtypes.bfloat16)
    for slot, part in enumerate((high, high, low)):
        tap_waves[:, slot * step : slot * step + taps * taps] = part
    return forward.astype(ml_dtypes.bfloat16), inverse.astype(ml_dtypes.bfloat16), tap_waves, half, step


def windows(rows, cols, taps, depth):
    m = taps // 2
    tap_r, tap_c = np.divmod(np.arange(taps * taps)[:, None], taps)
    row, col = np.divmod(np.arange(rows * cols)[None, :], cols)
    inside = (col - tap_c + m >= 0) & (col - tap_c + m < cols)
    masks = np.zeros((3, depth, rows * cols), ml_dtypes.bfloat16)
    masks[0, : taps * taps] = inside
    masks[1, : taps * taps] = inside & (row - tap_r + m < 0)
    masks[2, : taps * taps] = inside & (row - tap_r + m >= rows)
    return masks


def relax_gate(ex_center, gate_radius):
    low_end = ex_center - gate_radius
    high_end = ex_center + gate_radius
    sig_low = jax.nn.sigmoid(low_end)
    sig_high = jax.nn.sigmoid(high_end)
    slope_val = jnp.minimum(sig_low * (1.0 - sig_low), sig_high * (1.0 - sig_high))
    gate_center = slope_val * ex_center + 0.5 * (
        sig_high + sig_low - slope_val * (high_end + low_end)
    )
    spread_term = 0.5 * (sig_high - sig_low - slope_val * (high_end - low_end))
    return (gate_center, slope_val, spread_term)


def main_kernel(mesh, plans, chunk, x_hbm, *refs):
    main_body(
        mesh, plans, chunk, x_hbm, refs[:HELD], refs[HELD : HELD + OUTS],
        refs[HELD + OUTS : 2 * HELD + OUTS], *refs[2 * HELD + OUTS :],
    )


def main_body(
    mesh, plans, chunk, x_hbm, sources, outs, locals_,
    oc_ref, ob_ref, dwg_ref, dwc_ref, gates_ref, stats_ref, g_sem, o_sem, xs, l_sem, x_sem,
    xall, xcs, xcp, sums, taps_f, og_ref, wf, wz, w2, spec_a, spec_b, xf_s, y1_s, y2_s,
    rad, pool, own_wr, wr_high, wr_low, we_three, br_wide, ex,
    send_a, recv_a, full_a, recv_b, squeeze, gate,
    h_send, h_recv, f_send, f_recv, c_send, c_recv,
    rs_send, rs_recv, ag_send, ag_recv, bc_send, bc_recv, sq_send, sq_recv, gt_send, gt_recv,
):
    (
        xc_ref, fwd_a, inv_a, tw_a, fwd_b, inv_b, tw_b, mask_ref,
        w_ref, b_ref, wd_ref, bd_ref, wr_ref, br_ref, we_ref, be_ref,
    ) = locals_
    count_gen, count_row, count_ch = mesh["gen"], mesh["row"], mesh["ch"]
    my_gen = lax.axis_index("gen")
    my_row = lax.axis_index("row")
    my_ch = lax.axis_index("ch")
    has_up = my_row > 0
    has_down = my_row < count_row - 1
    last = jnp.logical_and(has_up, jnp.logical_not(has_down))
    inner = jnp.logical_and(has_up, has_down)
    flip = jnp.where(last, 1, 0)
    gens, pairs, span, chans = dwg_ref.shape
    c_in = w_ref.shape[0]
    taps = wd_ref.shape[0]
    wide = wz.shape[1]
    main = wide - LANES
    chunks = gens // chunk
    all_cells = pairs * span * count_row
    sub = gens // (2 * count_ch)

    def remote(src, dst, send_sem, recv_sem, place):
        return pltpu.make_async_remote_copy(
            src_ref=src, dst_ref=dst, send_sem=send_sem, recv_sem=recv_sem,
            device_id=place, device_id_type=MESH,
        )

    gen_peers = [(off, {"gen": lax.rem(my_gen + off, count_gen)}) for off in range(1, count_gen)]
    side_peers = []
    for off_row in range(count_row):
        for off_ch in range(count_ch):
            if off_row or off_ch:
                place = {
                    "row": lax.rem(my_row + off_row, count_row),
                    "ch": lax.rem(my_ch + off_ch, count_ch),
                }
                side_peers.append((off_row * count_ch + off_ch, place))
    barrier = pltpu.get_barrier_semaphore()
    for _, place in gen_peers + side_peers:
        pl.semaphore_signal(barrier, inc=1, device_id=place, device_id_type=MESH)

    x_loads = [
        pltpu.make_async_copy(x_hbm.at[:, row], xs.at[row], x_sem.at[row]) for row in range(pairs)
    ]
    for row in (0, pairs - 1) + tuple(range(1, pairs - 1)):
        x_loads[row].start()
    loads = [
        pltpu.make_async_copy(source, target, l_sem.at[k])
        for k, (source, target) in enumerate(zip(sources, locals_))
    ]
    for load in loads:
        load.start()
    own_rows = slice(span, (1 + pairs) * span)
    for k in range(2):
        pad = slice(LANES * k + c_in, LANES * (k + 1))
        xall[:, own_rows, pad] = jnp.zeros((gens // 2, pairs * span, LANES - c_in), jnp.bfloat16)
    for place, arrives in ((0, has_up), (pairs + 1, has_down)):
        @pl.when(jnp.logical_not(arrives))
        def _(place=place):
            xall[:, place * span : (place + 1) * span] = jnp.zeros(
                (gens // 2, span, 2 * LANES), jnp.bfloat16
            )

    def fill(row):
        x_loads[row].wait()
        for g in range(gens):
            lane = slice(LANES * (g % 2), LANES * (g % 2) + c_in)
            xall[g // 2, (1 + row) * span : (2 + row) * span, lane] = xs[row, g]

    fill(0)
    fill(pairs - 1)
    pl.semaphore_wait(barrier, len(gen_peers) + len(side_peers))

    row_place = (
        {"row": lax.rem(my_row + 1, count_row)},
        {"row": lax.rem(my_row + count_row - 1, count_row)},
    )
    edge = (pairs - 1, 0)
    place_of = (0, pairs + 1)

    def edge_of(row):
        return xall.at[pl.ds(my_ch * sub, sub), pl.ds(row * span, span)]

    def halo_copy(side):
        return remote(
            edge_of(1 + edge[side]), edge_of(place_of[side]),
            h_send.at[side], h_recv.at[side], row_place[side],
        )

    def center_copy(side):
        return remote(
            sources[0].at[edge[side]], xcs.at[side], c_send.at[side], c_recv.at[side], row_place[side]
        )

    def forwards(side):
        return [
            remote(
                edge_of(place_of[side]), edge_of(place_of[side]),
                f_send.at[side, off], f_recv.at[side, off],
                {"ch": lax.rem(my_ch + off, count_ch)},
            )
            for off in range(1, count_ch)
        ]

    for side, leaves in ((0, has_down), (1, has_up)):
        @pl.when(leaves)
        def _(side=side):
            halo_copy(side).start()
            center_copy(side).start()

    for row in range(1, pairs - 1):
        fill(row)

    def pass_on(side):
        halo_copy(side).wait_recv()
        for copy in forwards(side):
            copy.start()

    def passed_on(side):
        for copy in forwards(side):
            copy.wait_recv()

    def late(action):
        @pl.when(last)
        def _():
            action(0)

        @pl.when(has_down)
        def _():
            action(1)

    mine = my_row * count_ch + my_ch
    sq_copies = [
        remote(squeeze.at[mine], squeeze.at[mine], sq_send.at[off], sq_recv.at[off], place)
        for off, place in side_peers
    ]
    gt_copies = [
        remote(gate.at[my_gen], gate.at[my_gen], gt_send.at[off], gt_recv.at[off], place)
        for off, place in gen_peers
    ]

    def send_squeeze():
        pooled = pool[...].reshape(gens + chunk, wide) * (1.0 / all_cells)
        high = pooled.astype(jnp.bfloat16)
        low = (pooled - high.astype(jnp.float32)).astype(jnp.bfloat16)
        part = dot(high, wr_high[...]) + (dot(low, wr_high[...]) + dot(high, wr_low[...]))
        packed = part[:chunk]
        for n in range(1, chunks):
            packed = packed + pltpu.roll(part[n * chunk : (n + 1) * chunk], n * GROUP, 1)
        squeeze[mine, :chunk] = packed
        squeeze[mine, chunk:] = part[gens:]
        for copy in sq_copies:
            copy.start()

    def send_gate():
        for copy in sq_copies:
            copy.wait()
        total = squeeze[0]
        for slot in range(1, count_row * count_ch):
            total = total + squeeze[slot]
        spread = [total[:chunk]]
        spread += [pltpu.roll(total[:chunk], LANES - n * GROUP, 1) for n in range(1, chunks)]
        spread.append(total[chunk:] + br_wide[...])
        total = jnp.concatenate(spread, axis=0)
        total = jnp.where(lax.broadcasted_iota(jnp.int32, total.shape, 1) < GROUP, total, 0.0)
        high = total.astype(jnp.bfloat16).astype(jnp.float32)
        three = high + pltpu.roll(total - high, GROUP, 1) + pltpu.roll(high, 2 * GROUP, 1)
        ex_all = dot(three.astype(jnp.bfloat16), we_three[...])
        ex[...] = ex_all[:, :chans]
        ex_gens = ex[:gens]
        gate[my_gen] = jnp.sum(jnp.abs(ex_gens), axis=0, keepdims=True)
        for copy in gt_copies:
            copy.start()

    def finish_gate():
        for copy in gt_copies:
            copy.wait()
        gate_radius = gate[0]
        for slot in range(1, count_gen):
            gate_radius = gate_radius + gate[slot]
        ex_center = ex[gens : gens + 1] + be_ref[...][None, :]
        gate_center, slope_val, spread_term = relax_gate(ex_center, gate_radius)
        gates_ref[...] = (slope_val * ex[:gens])[:, None, :]
        stats_ref[0:1] = gate_center
        stats_ref[1:2] = spread_term
        stats_ref[2:3] = slope_val * gate_radius + spread_term

    for load in loads:
        load.wait()
    wf[...] = jnp.zeros_like(wf)
    wf[:c_in, :chans] = w_ref[...].astype(jnp.float32)
    bias = b_ref[...][None, :]
    bias_high = bias.astype(jnp.bfloat16).astype(jnp.float32)
    wf[c_in : c_in + 1, :chans] = bias_high
    wf[c_in + 1 : c_in + 2, :chans] = bias - bias_high
    wz[...] = wf[...].astype(jnp.bfloat16)
    w2[...] = jnp.zeros_like(w2)
    w2[:LANES, :LANES] = wz[:, main:]
    w2[LANES:, LANES:] = wz[:, main:]
    wf[...] = jnp.zeros_like(wf)
    taps_f[...] = jnp.zeros_like(taps_f)
    step = plans[0][1]
    for row in range(taps):
        one = wd_ref[row]
        taps_f[row * taps : (row + 1) * taps, :chans] = one
        high = one.astype(jnp.bfloat16).astype(jnp.float32)
        for slot, part in enumerate((high, one - high, high)):
            start = slot * step + row * taps
            wf[start : start + taps, :chans] = part
    wtap = wf[...].astype(jnp.bfloat16)
    spec_a[...] = dot(tw_a[...], wtap).reshape(spec_a.shape)
    spec_b[...] = dot(tw_b[...], wtap).reshape(spec_b.shape)
    ones = jnp.where(
        lax.broadcasted_iota(jnp.int32, (span, LANES - c_in), 1) < 2, 1.0, 0.0
    ).astype(jnp.bfloat16)
    xcp[...] = jnp.zeros_like(xcp)
    xcp[1 : 1 + pairs, :, :c_in] = xc_ref[...]
    for row in range(pairs):
        xcp[1 + row, :, c_in:] = ones
    rad[...] = jnp.zeros_like(rad)
    own = wr_ref[:, :chans]
    for other in range(1, count_ch):
        own = jnp.where(my_ch == other, wr_ref[:, other * chans : (other + 1) * chans], own)
    units = own.shape[0]
    own_wr[...] = jnp.zeros_like(own_wr)
    own_wr[:units, :chans] = own
    turned = own_wr[...].T
    turned_high = turned.astype(jnp.bfloat16)
    wr_high[...] = turned_high
    wr_low[...] = (turned - turned_high.astype(jnp.float32)).astype(jnp.bfloat16)
    own_wr[...] = jnp.zeros_like(own_wr)
    we_high = we_ref[...].astype(jnp.bfloat16).astype(jnp.float32)
    own_wr[:units, :chans] = we_high
    own_wr[GROUP : GROUP + units, :chans] = we_high
    own_wr[2 * GROUP : 2 * GROUP + units, :chans] = we_ref[...] - we_high
    we_three[...] = own_wr[...].astype(jnp.bfloat16)
    br_wide[...] = jnp.zeros_like(br_wide)
    br_wide[0:1, :units] = br_ref[...][None, :]

    def take(side):
        center_copy(side).wait_recv()
        xcp[place_of[side], :, :c_in] = xcs[side]
        xcp[place_of[side], :, c_in:] = ones

    @pl.when(inner)
    def _():
        pass_on(0)
        passed_on(0)
        take(0)

    above = jnp.where(has_up, 0.0, 1.0)
    below = jnp.where(has_down, 0.0, 1.0)
    window = (
        mask_ref[0].astype(jnp.float32)
        - above * mask_ref[1].astype(jnp.float32)
        - below * mask_ref[2].astype(jnp.float32)
    ).astype(jnp.bfloat16)
    deep = window.shape[0]
    for q in range(gens // 2):
        both = dot(window, xall[q, own_rows]).astype(jnp.bfloat16)
        sums[2 * q] = both[:, :LANES]
        sums[2 * q + 1] = both[:, LANES:]
    sums[gens] = dot(window, xcp[1 : 1 + pairs].reshape(pairs * span, LANES)).astype(jnp.bfloat16)
    for n in range(chunks):
        block = dot(sums[n * chunk : (n + 1) * chunk].reshape(chunk * deep, LANES), wz[...])
        pool[n] = jnp.sum(block.reshape(chunk, deep, wide) * taps_f[...], axis=1)
    pool[chunks] = jnp.zeros((chunk, wide), jnp.float32)
    pool[chunks, 0:1] = jnp.sum(dot(sums[gens], wz[...]) * taps_f[...], axis=0, keepdims=True)
    pool[chunks, 0:1, :chans] += (pairs * span) * bd_ref[...][None, :]
    send_squeeze()

    parts = (
        (fwd_a, inv_a, spec_a, flip, flip, 0) + plans[0],
        (fwd_b, inv_b, spec_b, (pairs - 1) * (1 - flip), (pairs - 1) * (1 - flip), pairs - 1) + plans[1],
    )

    def mix(e, spec, lane, half):
        count, width = e.shape[0] // (2 * half), e.shape[1]
        e = e.reshape(count, half // 8, 2, 8, width)
        a, b, c, d = [spec[k, :, lane].reshape(1, half // 8, 8, width) for k in range(4)]
        re, im = e[:, :, 0], e[:, :, 1]
        y = jnp.stack([re * a - im * b, re * c + im * d], axis=2)
        return y.reshape(count * 2 * half, width).astype(jnp.bfloat16)

    def compute(part, start, count):
        fwd, inv, spec, first, out, slot, half, _, made = part
        depth = fwd.shape[1]
        size = 2 * half
        cells = made * span
        rows = pl.ds(pl.multiple_of(first * span, span), depth)
        where = slice(slot, slot + made)
        for u in range(count):
            xf = dot(fwd[...], xall[start + u, rows]).astype(jnp.bfloat16)
            xf_s[2 * u * size : (2 * u + 1) * size] = xf[:, :LANES]
            xf_s[(2 * u + 1) * size : (2 * u + 2) * size] = xf[:, LANES:]
        for u in range(count):
            both = xf_s[2 * u * size : (2 * u + 2) * size]
            y1_s[u, : 2 * size] = mix(dot(both, wz[:, :main]), spec, slice(0, main), half)
            e2 = dot(jnp.concatenate([both[:size], both[size:]], axis=1), w2[...])
            for k in range(2):
                lane = slice(LANES * k, LANES * (k + 1))
                y2_s[u, :size, lane] = mix(e2[:, lane], spec, slice(main, wide), half)
        total = None
        for u in range(count):
            for k in range(2):
                g = 2 * (start + u) + k
                t = dot(inv[...], y1_s[u, k * size : (k + 1) * size])
                for row in range(made):
                    dwg_ref[g, out + row, :, :main] = t[row * span : (row + 1) * span].astype(jnp.bfloat16)
                total = jnp.abs(t) if total is None else total + jnp.abs(t)
        rad[where, :, :main] += total.reshape(made, span, main)
        total = None
        for u in range(count):
            t = dot(inv[...], y2_s[u, :size])
            for k in range(2):
                g = 2 * (start + u) + k
                mine = t[:, LANES * k : LANES * (k + 1)]
                for row in range(made):
                    dwg_ref[g, out + row, :, main:] = mine[
                        row * span : (row + 1) * span, : chans - main
                    ].astype(jnp.bfloat16)
                total = jnp.abs(mine) if total is None else total + jnp.abs(mine)
        rad[where, :, main:] += total.reshape(made, span, LANES)

    def center(part):
        fwd, inv, spec, first, out, _, half, _, made = part
        depth = fwd.shape[1]
        cells = made * span
        both = xcp[pl.ds(first, depth // span)].reshape(depth, LANES)
        xf = dot(fwd[...], both).astype(jnp.bfloat16)
        y = mix(dot(xf, wz[...]), spec, slice(0, wide), half)
        t = dot(inv[...], y)
        bias = bd_ref[...][None, :]
        for row in range(made):
            dwc_ref[out + row] = t[row * span : (row + 1) * span, :chans] + bias

    def done_copy(n):
        where = pl.ds(n * chunk, chunk)
        return pltpu.make_async_copy(og_ref.at[where], outs[0].at[where], g_sem.at[n])

    results = [
        pltpu.make_async_copy(source, target, o_sem.at[k])
        for k, (source, target) in enumerate(
            zip((oc_ref, ob_ref), outs[1:])
        )
    ]

    compute(parts[0], 0, gens // 2)
    radii = ((send_a, recv_a, full_a),)

    def reduce_copies(which):
        send, recv, _ = radii[which]
        per = recv.shape[1]
        return [
            remote(
                send.at[pl.ds(place["gen"] * per, per)], recv.at[my_gen],
                rs_send.at[which, off], rs_recv.at[which, off], place,
            )
            for off, place in gen_peers
        ]

    def gather_copies(which):
        full, per = radii[which][2], radii[which][1].shape[1]
        mine = full.at[pl.ds(my_gen * per, per)]
        return [
            remote(mine, mine, ag_send.at[which, off], ag_recv.at[which, off], place)
            for off, place in gen_peers
        ]

    def reduce_start(which):
        send, recv, _ = radii[which]
        per = recv.shape[1]
        _, _, _, _, _, slot, _, _, made = parts[which]
        tiles = made * span // 8
        send[:tiles] = rad[slot : slot + made].reshape(tiles, 8, wide).astype(jnp.bfloat16)
        if count_gen * per > tiles:
            send[tiles:] = jnp.zeros((count_gen * per - tiles, 8, wide), jnp.bfloat16)
        recv[my_gen] = send[pl.ds(my_gen * per, per)]
        for copy in reduce_copies(which):
            copy.start()

    def gather_start(which):
        _, recv, full = radii[which]
        per = recv.shape[1]
        for copy in reduce_copies(which):
            copy.wait()
        total = recv[0].astype(jnp.float32)
        for slot in range(1, count_gen):
            total = total + recv[slot].astype(jnp.float32)
        full[pl.ds(my_gen * per, per)] = total.astype(jnp.bfloat16)
        for copy in gather_copies(which):
            copy.start()

    reduce_start(0)

    late(pass_on)
    for off in range(count_ch):
        if off == 1:
            send_gate()
            late(passed_on)
        compute(parts[1], lax.rem(my_ch + off, count_ch) * sub, sub)

    _, _, _, _, last_out, slot, _, _, made = parts[1]
    recv_b[my_gen] = rad[slot].astype(jnp.bfloat16)
    bc_copies = [
        remote(recv_b.at[my_gen], recv_b.at[my_gen], bc_send.at[off], bc_recv.at[off], place)
        for off, place in gen_peers
    ]
    for copy in bc_copies:
        copy.start()
    gather_start(0)
    late(take)
    center(parts[0])
    center(parts[1])
    finish_gate()
    gate_center = stats_ref[0:1]

    def out_turn(n, _):
        for k in range(chunk):
            g = n * chunk + k
            og_ref[g] = (
                dwc_ref[...] * gates_ref[g] + gate_center * dwg_ref[g].astype(jnp.float32)
            ).astype(jnp.bfloat16)
        done_copy(n).start()
        return 0

    lax.fori_loop(0, chunks, out_turn, 0)
    oc_ref[...] = dwc_ref[...] * gate_center
    results[0].start()
    base = jnp.abs(dwc_ref[...]) * stats_ref[1:2]
    ob_ref[...] = base
    for copy in gather_copies(0):
        copy.wait()
    _, _, _, _, out, _, _, _, made = parts[0]
    whole = full_a[: made * span // 8].astype(jnp.float32).reshape(made, span, wide)
    for row in range(made):
        ob_ref[out + row] += whole[row, :, :chans] * stats_ref[2:3]
    for copy in bc_copies:
        copy.wait()
    total = recv_b[0].astype(jnp.float32)
    for slot in range(1, count_gen):
        total = total + recv_b[slot].astype(jnp.float32)
    ob_ref[last_out] += total[:, :chans] * stats_ref[2:3]
    results[1].start()

    for side, arrives, leaves in ((0, has_up, has_down), (1, has_down, has_up)):
        @pl.when(leaves)
        def _(side=side):
            center_copy(side).wait_send()
            halo_copy(side).wait_send()

        @pl.when(arrives)
        def _(side=side):
            for copy in forwards(side):
                copy.wait_send()

    for n in range(chunks):
        done_copy(n).wait()
    for copy in results:
        copy.wait()


def main_call(mesh, taps, cols, x, xc, w_expand, b_expand, w_depth, b_depth, wr, br, we, be):
    gens, pairs, span, c_in = x.shape
    chans = w_expand.shape[1]
    chunk = CHUNK
    count_gen, count_row, count_ch = mesh["gen"], mesh["row"], mesh["ch"]
    wide = -(-chans // LANES) * LANES
    chunks = gens // chunk
    assert wide == 3 * LANES and gens == 2 * PAIRS * count_ch and gens == chunks * chunk
    assert we.shape[0] <= GROUP and chunks * GROUP <= LANES
    plans, tables = [], []
    for made in (pairs - 1, 1):
        forward, inverse, tap_waves, half, step = transforms(made * span // cols, cols, taps)
        plans.append((half, step, made))
        tables += [jnp.asarray(forward), jnp.asarray(inverse), jnp.asarray(tap_waves)]
    half_a, half_b = plans[0][0], plans[1][0]
    hbm = pl.BlockSpec(memory_space=pltpu.HBM)
    dma = pltpu.SemaphoreType.DMA
    bf16, f32 = jnp.bfloat16, jnp.float32
    masks = jnp.asarray(windows(pairs * span // cols, cols, taps, plans[0][1]))
    args = [x, xc] + tables + [masks, w_expand, b_expand, w_depth, b_depth, wr, br, we, be]
    outs = [
        jax.ShapeDtypeStruct((gens, pairs, span, chans), bf16),
        jax.ShapeDtypeStruct((pairs, span, chans), f32),
        jax.ShapeDtypeStruct((pairs, span, chans), f32),
    ]
    held = [pltpu.VMEM(one.shape, one.dtype) for one in args[1:] + outs[1:]]
    held += [pltpu.VMEM(one.shape, one.dtype) for one in outs[:2]]
    held += [pltpu.VMEM((gens, 1, chans), f32), pltpu.VMEM((3, chans), f32)]
    per = -(-(plans[0][2] * span // 8) // count_gen)
    whole = pltpu.VMEM((count_gen * per, 8, wide), bf16)
    sums = [
        whole, pltpu.VMEM((count_gen, per, 8, wide), bf16), whole, pltpu.VMEM((count_gen, span, wide), bf16),
    ]
    side = count_row * count_ch
    step = plans[0][1]
    return pl.pallas_call(
        functools.partial(main_kernel, mesh, tuple(plans), chunk),
        in_specs=[hbm] * len(args),
        out_specs=[hbm] * OUTS,
        out_shape=outs,
        scratch_shapes=held
        + [
            dma((chunks,)), dma((OUTS - 1,)),
            pltpu.VMEM((pairs, gens, span, c_in), bf16), dma((HELD,)), dma((pairs,)),
            pltpu.VMEM((gens // 2, (pairs + 2) * span, 2 * LANES), bf16),
            pltpu.VMEM((2, span, c_in), bf16),
            pltpu.VMEM((pairs + 2, span, LANES), bf16),
            pltpu.VMEM((gens + 1, step, LANES), bf16),
            pltpu.VMEM((step, wide), f32),
            pltpu.VMEM((gens, pairs, span, chans), bf16),
            pltpu.VMEM((LANES, wide), f32),
            pltpu.VMEM((LANES, wide), bf16),
            pltpu.VMEM((2 * LANES, 2 * LANES), bf16),
            pltpu.VMEM((4, half_a, wide), f32),
            pltpu.VMEM((4, half_b, wide), f32),
            pltpu.VMEM((gens * 2 * half_a, LANES), bf16),
            pltpu.VMEM((gens // 2, 4 * half_a, 2 * LANES), bf16),
            pltpu.VMEM((gens // 2, 2 * half_a, 2 * LANES), bf16),
            pltpu.VMEM((pairs, span, wide), f32),
            pltpu.VMEM((chunks + 1, chunk, wide), f32),
            pltpu.VMEM((LANES, wide), f32), pltpu.VMEM((wide, LANES), bf16), pltpu.VMEM((wide, LANES), bf16),
            pltpu.VMEM((LANES, wide), bf16), pltpu.VMEM((chunk, LANES), f32),
            pltpu.VMEM((gens + chunk, chans), f32),
        ]
        + sums
        + [
            pltpu.VMEM((side, 2 * chunk, LANES), f32),
            pltpu.VMEM((count_gen, 1, chans), f32),
            dma((2,)), dma((2,)), dma((2, count_ch)), dma((2, count_ch)),
            dma((2,)), dma((2,)),
            dma((1, count_gen)), dma((1, count_gen)), dma((1, count_gen)), dma((1, count_gen)),
            dma((count_gen,)), dma((count_gen,)),
            dma((side,)), dma((side,)), dma((count_gen,)), dma((count_gen,)),
        ],
        compiler_params=pltpu.CompilerParams(
            collective_id=1, has_side_effects=True, vmem_limit_bytes=ROOM
        ),
    )(*[pltpu.with_memory_space_constraint(one, pltpu.HBM) for one in args])


def final_kernel(*refs):
    half = len(refs) // 2
    sources, targets, sem = refs[:half], refs[half : 2 * half], refs[-1]
    gens, parts = sources[0].shape[0], 4
    copies = []
    for k in range(parts):
        where = pl.ds(k * (gens // parts), gens // parts)
        copies.append(pltpu.make_async_copy(sources[0].at[where], targets[0].at[where], sem.at[k]))
    for k, (source, target) in enumerate(zip(sources[1:], targets[1:])):
        copies.append(pltpu.make_async_copy(source, target, sem.at[parts + k]))
    for copy in copies:
        copy.start()
    for copy in copies:
        copy.wait()


def final_call(*arrays):
    return pl.pallas_call(
        final_kernel,
        in_specs=[pl.BlockSpec(memory_space=pltpu.VMEM)] * len(arrays),
        out_specs=[pl.BlockSpec(memory_space=pltpu.HBM)] * len(arrays),
        out_shape=[jax.ShapeDtypeStruct(one.shape, one.dtype) for one in arrays],
        scratch_shapes=[pltpu.SemaphoreType.DMA((3 + len(arrays),))],
        compiler_params=pltpu.CompilerParams(vmem_limit_bytes=1 << 20),
    )(*arrays)


def on_device(
    shape, x_center, x_gens, w_expand, b_expand, w_depth, b_depth, w_reduce, b_reduce, w_excite, b_excite
):
    gens, rows, cols, c_in = x_gens.shape
    chans = w_expand.shape[1]
    taps = w_depth.shape[0]
    margin = taps // 2
    pairs, span = rows // margin, margin * cols
    x = x_gens.reshape(gens, pairs, span, c_in)
    xc = x_center.reshape(pairs, span, c_in)
    made = main_call(
        shape, taps, cols, x, xc, w_expand, b_expand, w_depth, b_depth,
        w_reduce.T, b_reduce, w_excite, b_excite,
    )
    out_gens, out_center, out_box = final_call(*made)
    image = (rows, cols, chans)
    return out_center.reshape(image), out_gens.reshape((gens,) + image), out_box.reshape(image)


def solution(mesh):
    in_specs = (
        P(("grp", "row"), None, None),
        P(("grp", "gen"), "row", None, None),
        P(None, "ch"),
        P("ch"),
        P(None, None, "ch"),
        P("ch"),
        P(),
        P(),
        P(None, "ch"),
        P("ch"),
    )
    out_specs = (
        P(("grp", "row"), None, "ch"),
        P(("grp", "gen"), "row", None, "ch"),
        P(("grp", "row"), None, "ch"),
    )
    return jax.shard_map(
        functools.partial(on_device, dict(mesh.shape)), mesh=mesh, in_specs=in_specs, out_specs=out_specs, check_vma=False
    )
```
